256 devices in a mesh: pipe: 4 (over x), expert: 64 (over y, z, core).
Axes of the slice: x: 4, y: 4, z: 8, core: 2. Of those that a mesh axis runs over, the one named last changes fastest.
Arguments:
- hidden_in: bfloat16 [4, 8192, 4096], P('pipe', 'expert'), may hold values from -90 to 90
- out_grad: bfloat16 [4, 8192, 4096], P('pipe', 'expert'), may hold values from -6 to 6
- expert_ids: int32 [4, 8192, 8], P('pipe', 'expert'), may hold values from 0 to 127, as said below
- route_weight: bfloat16 [4, 8192, 8], P('pipe', 'expert'), may hold values from 0.25 to 1
- norm_gain: float32 [4, 4096], P('pipe'), may hold values from 0.25 to 1.75
- w_gate_up: bfloat16 [4, 64, 2, 192, 4096], P('pipe', 'expert'), may hold values from -0.09375 to 0.09375
- w_down: bfloat16 [4, 64, 192, 4096], P('pipe', 'expert'), may hold values from -0.15625 to 0.15625
Outputs:
- handed_grad: bfloat16 [4, 8192, 4096], P('pipe', 'expert')
- grad_gate_up: bfloat16 [4, 64, 2, 192, 4096], P('pipe', 'expert')
- grad_down: bfloat16 [4, 64, 192, 4096], P('pipe', 'expert')
- grad_combine: float32 [4, 8192, 8], P('pipe', 'expert')
The draws below stay inside these ranges and needn't reach their ends.
Inputs may be any that keep to these rules, and one draw needn't show every extreme that they name: `expert_ids`: each token names 8 different experts. In each layer, at most 8 tokens of one aligned block of 128 tokens name any one of the experts 0 to 7, and one of these experts is named by exactly 8 tokens of every block.
All inputs are finite; a program needn't handle non-finite values.
Results may differ from the reference program's by a relative error of at most 0.008.
Values may be sent and summed in bfloat16 or wider, within the bound.
A program may use at most 128 MiB of HBM per device.

```python
import math
import jax
import jax.numpy as jnp
from jax import lax

D = 4096
FF = 1536
EXPERTS = 128
TOPK = 8
TOK_DEV = 128
F_DEV = 192
EXP_FLY = 8
SLABS = 64
SPECIALIST_CAP = 8
TOKENS = 8192
LAYERS = 4


def draw_hidden_in(key, part):
    key_rows, key_cols, key_base = jax.random.split(key, 3)
    row_scale = jnp.exp(jax.random.uniform(key_rows, (LAYERS, TOKENS, 1), jnp.float32, math.log(0.5), math.log(5.0)))
    col_scale = jnp.exp(jax.random.uniform(key_cols, (LAYERS, 1, D), jnp.float32, math.log(0.3), math.log(3.0)))
    values = jnp.clip(jax.random.normal(key_base, (LAYERS, TOKENS, D), jnp.float32), -6.0, 6.0)
    return (values * row_scale * col_scale).astype(jnp.bfloat16)


def draw_expert_ids(key, part):
    seed_sequence = jax.random.split(key, 6)
    specialist_span = EXP_FLY
    tile_shape_sizes = (LAYERS, SLABS, specialist_span)
    tally_starts = jax.random.randint(seed_sequence[0], tile_shape_sizes, SPECIALIST_CAP // 4, SPECIALIST_CAP // 2 + 1)
    arrival_surges = jax.random.randint(seed_sequence[1], tile_shape_sizes, 0, 8) == 0
    heaviest_specialist = jax.random.randint(seed_sequence[2], (LAYERS, 1, 1), 0, specialist_span)
    specialist_tallies = jnp.where(arrival_surges | (jnp.arange(specialist_span)[None, None, :] == heaviest_specialist), SPECIALIST_CAP, tally_starts)
    scores = jax.random.randint(seed_sequence[3], (LAYERS, SLABS, specialist_span, TOK_DEV), 0, 1 << 20)
    scores = scores * TOK_DEV + jnp.arange(TOK_DEV)
    ranks = jnp.argsort(jnp.argsort(scores, axis=-1), axis=-1)
    member = jnp.swapaxes(ranks < specialist_tallies[..., None], 2, 3)
    marked = jnp.sort(jnp.where(member, jnp.arange(specialist_span), EXPERTS), axis=-1)
    padding = jnp.full((LAYERS, SLABS, TOK_DEV, TOPK - specialist_span), EXPERTS, jnp.int32)
    marked = jnp.concatenate([marked.astype(jnp.int32), padding], axis=-1)
    taken = jnp.sum(member.astype(jnp.int32), axis=-1)[..., None]
    outside_count = EXPERTS - specialist_span
    scores_out = jax.random.randint(seed_sequence[4], (LAYERS, SLABS, TOK_DEV, outside_count), 0, 1 << 20)
    scores_out = scores_out * outside_count + jnp.arange(outside_count)
    outside = jnp.argsort(scores_out, axis=-1)[..., :TOPK] + specialist_span
    slot_range = jnp.arange(TOPK)
    filler = jnp.take_along_axis(outside, jnp.clip(slot_range - taken, 0, TOPK - 1), axis=-1)
    chosen = jnp.where(slot_range < taken, marked, filler)
    scores_slot = jax.random.randint(seed_sequence[5], (LAYERS, SLABS, TOK_DEV, TOPK), 0, 1 << 20) * TOPK + slot_range
    ordering = jnp.argsort(scores_slot, axis=-1)
    chosen = jnp.take_along_axis(chosen, ordering, axis=-1)
    return chosen.reshape(LAYERS, TOKENS, TOPK).astype(jnp.int32)


def level_of(rng, dims, cuts, smallest, largest):
    loudness, own = 1.0, jax.random.fold_in(rng, 6)
    for axis_at, blocks in cuts:
        heights = jnp.exp(jax.random.uniform(jax.random.fold_in(own, axis_at), (blocks,), jnp.float32, smallest / len(cuts), largest / len(cuts)))
        loudness = loudness * jnp.repeat(heights, dims[axis_at] // blocks).reshape([-1 if axis == axis_at else 1 for axis in range(len(dims))])
    return loudness


def bell_draw(own_key, dims, deviation, limit, cuts=(), kind=jnp.bfloat16):
    array = jax.random.normal(own_key, dims, jnp.float32) * deviation
    if len(cuts) > 0:
        array = level_of(own_key, dims, cuts, -0.22, 0.18) * array
    return jnp.clip(array, min=-limit, max=limit).astype(kind)


def setup_inputs(seed: int = 0) -> dict:
    seeds = jax.random.split(jax.random.key(seed), 8)
    return {
        "hidden_in": draw_hidden_in(jax.random.fold_in(seeds[7], 71), 0),
        "out_grad": bell_draw(seeds[1], (LAYERS, TOKENS, D), 1.0, 6.0, ((0, 4), (1, 64))),
        "expert_ids": draw_expert_ids(jax.random.fold_in(seeds[7], 71), 0),
        "route_weight": jnp.clip(0.25 + 0.75 * jax.random.uniform(seeds[3], (LAYERS, TOKENS, TOPK), jnp.float32) ** level_of(seeds[3], (LAYERS, TOKENS, TOPK), ((0, 4), (1, 64)), -0.2, 0.2), 0.25, 1.0).astype(jnp.bfloat16),
        "norm_gain": jnp.clip(1.0 + 0.15 * jax.random.normal(seeds[4], (LAYERS, D), jnp.float32), 0.25, 1.75),
        "w_gate_up": bell_draw(seeds[5], (LAYERS, SLABS, 2, F_DEV, D), D ** -0.5, 0.09375, ((0, 4), (1, 64))),
        "w_down": bell_draw(seeds[6], (LAYERS, SLABS, F_DEV, D), FF ** -0.5, 0.15625, ((0, 4), (1, 64))),
    }


def reference(hidden_in, out_grad, expert_ids, route_weight, norm_gain, w_gate_up, w_down):
    specialist_span = EXP_FLY
    group = SLABS // EXP_FLY
    total_rows = SLABS * SPECIALIST_CAP
    handed_list = []
    gate_up_list = []
    down_list = []
    combine_list = []
    for layer_idx in range(LAYERS):
        tokens_f = hidden_in[layer_idx].astype(jnp.float32)
        rms_value = jnp.sqrt(lax.optimization_barrier(jnp.mean(tokens_f * tokens_f, axis=-1, keepdims=True)) + 1e-06)
        normed = tokens_f / rms_value
        gain_row = norm_gain[layer_idx].astype(jnp.float32)
        normed_in = (normed * gain_row).astype(jnp.bfloat16)
        grad_out = out_grad[layer_idx]
        chosen = expert_ids[layer_idx]
        picked = chosen[:, :, None] == jnp.arange(specialist_span, dtype=jnp.int32)[None, None, :]
        member = jnp.any(picked, axis=1).astype(jnp.int32)
        weight_te = lax.optimization_barrier(jnp.sum(jnp.where(picked, route_weight[layer_idx].astype(jnp.float32)[:, :, None], jnp.float32(0.0)), axis=1))
        blocked = member.reshape(SLABS, TOK_DEV, specialist_span)
        position = (jnp.cumsum(blocked, axis=1) - blocked).reshape(TOKENS, specialist_span).astype(jnp.int32)
        source = (jnp.arange(TOKENS, dtype=jnp.int32) // TOK_DEV).astype(jnp.int32)
        grad_normed = jnp.zeros((TOKENS, D), jnp.float32)
        grad_combine = jnp.zeros((TOKENS, TOPK), jnp.float32)
        gate_up_parts = []
        down_parts = []
        for expert_idx in range(specialist_span):
            target = jnp.where(member[:, expert_idx] == 1, source * SPECIALIST_CAP + position[:, expert_idx], total_rows).astype(jnp.int32)
            rows_in = jnp.zeros((total_rows + 1, D), jnp.float32).at[target].add(normed_in.astype(jnp.float32))[:total_rows].astype(jnp.bfloat16)
            rows_grad = jnp.zeros((total_rows + 1, D), jnp.float32).at[target].add(grad_out.astype(jnp.float32))[:total_rows].astype(jnp.bfloat16)
            rows_weight = jnp.zeros((total_rows + 1,), jnp.float32).at[target].add(weight_te[:, expert_idx])[:total_rows]
            first_slab = expert_idx * group
            gate_up_w = w_gate_up[layer_idx, first_slab:first_slab + group].astype(jnp.float32)
            down_w = w_down[layer_idx, first_slab:first_slab + group].astype(jnp.float32)
            rows_in_f = rows_in.astype(jnp.float32)
            rows_grad_f = rows_grad.astype(jnp.float32)
            weight_col = rows_weight[:, None, None]
            gate_pre = jnp.einsum('rd,sfd->rsf', rows_in_f, gate_up_w[:, 0])
            up_pre = jnp.einsum('rd,sfd->rsf', rows_in_f, gate_up_w[:, 1])
            sigmoid_gate = jax.nn.sigmoid(gate_pre)
            active = gate_pre * sigmoid_gate
            hidden_act = active * up_pre
            back_proj = jnp.einsum('rd,sfd->rsf', rows_grad_f, down_w)
            grad_hidden = weight_col * back_proj
            grad_gate = (grad_hidden * up_pre * sigmoid_gate * (1.0 + gate_pre * (1.0 - sigmoid_gate))).astype(jnp.bfloat16).astype(jnp.float32)
            grad_up = (grad_hidden * active).astype(jnp.bfloat16).astype(jnp.float32)
            scaled_hidden = (weight_col * hidden_act).astype(jnp.bfloat16).astype(jnp.float32)
            gate_grad = jnp.einsum('rsf,rd->sfd', grad_gate, rows_in_f)
            up_grad = jnp.einsum('rsf,rd->sfd', grad_up, rows_in_f)
            gate_up_parts.append(jnp.stack([gate_grad, up_grad], axis=1).astype(jnp.bfloat16))
            down_parts.append(jnp.einsum('rsf,rd->sfd', scaled_hidden, rows_grad_f).astype(jnp.bfloat16))
            input_part = jnp.einsum('rsf,sfd->rsd', grad_gate, gate_up_w[:, 0]) + jnp.einsum('rsf,sfd->rsd', grad_up, gate_up_w[:, 1])
            input_sum = lax.optimization_barrier(jnp.sum(input_part.astype(jnp.bfloat16).astype(jnp.float32), axis=1))
            combine_sum = lax.optimization_barrier(jnp.sum(lax.optimization_barrier(jnp.sum(hidden_act * back_proj, axis=-1)).astype(jnp.bfloat16).astype(jnp.float32), axis=1))
            extended = jnp.concatenate([input_sum, jnp.zeros((1, D), jnp.float32)], axis=0)
            grad_normed = grad_normed + extended[target]
            comb_ext = jnp.concatenate([combine_sum, jnp.zeros((1,), jnp.float32)], axis=0)
            grad_combine = grad_combine + jnp.where(picked[:, :, expert_idx], comb_ext[target][:, None], jnp.float32(0.0))
        scaled = grad_normed * gain_row
        inner_mean = lax.optimization_barrier(jnp.mean(scaled * normed, axis=-1, keepdims=True))
        grad_tokens = (grad_out.astype(jnp.float32) + (scaled - normed * inner_mean) / rms_value).astype(jnp.bfloat16)
        handed_list.append(grad_tokens)
        gate_up_list.append(jnp.concatenate(gate_up_parts, axis=0))
        down_list.append(jnp.concatenate(down_parts, axis=0))
        combine_list.append(grad_combine)
    handed_grad = jnp.roll(jnp.stack(handed_list, axis=0), -1, axis=0)
    return (handed_grad, jnp.stack(gate_up_list, axis=0), jnp.stack(down_list, axis=0), jnp.stack(combine_list, axis=0))
```

```python
import jax
import jax.numpy as jnp
from jax import lax
from jax.experimental import pallas as pl
from jax.experimental.pallas import tpu as pltpu
from jax.sharding import PartitionSpec as P

SPLIT = 8
CAP = 8
NY = 4
NZ = 8
LINE = 4
MESH = pl.DeviceIdType.MESH
F32 = jnp.float32
BF16 = jnp.bfloat16


def nt(left, right):
    return lax.dot_general(left, right, (((1,), (1,)), ((), ())), preferred_element_type=F32)


def nn(left, right):
    return lax.dot_general(left, right, (((1,), (0,)), ((), ())), preferred_element_type=F32)


def tn(left, right):
    return lax.dot_general(left, right, (((0,), (0,)), ((), ())), preferred_element_type=F32)


def expert_kernel(
    mine_ref,
    wgu_hbm,
    wd_hbm,
    back_ref,
    ggu_hbm,
    gd_hbm,
    rows,
    wgu,
    wd,
    part,
    swap,
    summed,
    landed,
    da,
    db,
    hd,
    ggu,
    gd,
    row_sem,
    pair_sem,
    right_sem,
    left_sem,
    share_sem,
    entry_sem,
    swap_send,
    swap_recv,
    back_send,
    back_recv,
    w_sem,
    out_sem,
):
    me = lax.axis_index("expert")
    core = lax.rem(me, 2)
    z = lax.rem(me // 2, NZ)
    y = me // (2 * NZ)
    half = z // LINE
    pos = lax.rem(z, LINE)
    width = mine_ref.shape[2]
    hidden = wd.shape[0]
    halfw = width // 2
    outw = halfw + 128
    partner = me + 1 - 2 * core

    def at(yy, zz, cc):
        return (yy * NZ + zz) * 2 + cc

    barrier = pltpu.get_barrier_semaphore()

    @pl.loop(1, NY * NZ)
    def _(step):
        other = lax.rem(me // 2 + step, NY * NZ) * 2 + core
        pl.semaphore_signal(barrier, inc=1, device_id={"expert": other}, device_id_type=MESH)

    pl.semaphore_signal(barrier, inc=1, device_id={"expert": partner}, device_id_type=MESH)

    w_copies = [
        pltpu.make_async_copy(wgu_hbm, wgu, w_sem.at[0]),
        pltpu.make_async_copy(wd_hbm, wd, w_sem.at[1]),
    ]
    for copy in w_copies:
        copy.start()
    pl.semaphore_wait(barrier, NY * NZ)

    def remote(src, dst, send, recv, other):
        return pltpu.make_async_remote_copy(
            src_ref=src,
            dst_ref=dst,
            send_sem=send,
            recv_sem=recv,
            device_id={"expert": other},
            device_id_type=MESH,
        )

    def piece(kind, src_z, src_y):
        return rows.at[kind, src_z * NY + src_y]

    entry_z = jnp.where(pos >= 2, lax.rem(LINE * (half + 1), NZ), lax.rem(LINE * half + NZ - 1, NZ))
    slot = z * NY + y

    def entry(src_idx, sem_idx, other):
        return remote(
            mine_ref.at[src_idx], rows.at[core, slot], entry_sem.at[sem_idx], row_sem.at[slot], other
        )

    own_copy = pltpu.make_async_copy(mine_ref.at[y * 2 + half], rows.at[core, slot], row_sem.at[slot])
    own_copy.start()
    for step in range(NY):
        yy = lax.rem(y + step, NY)
        if step > 0:
            entry(yy * 2 + half, step, at(yy, z, core)).start()
        entry(yy * 2 + 1 - half, NY + step, at(yy, entry_z, core)).start()

    def forward(src_z, src_y, sems, sem_idx, other):
        return remote(
            piece(core, src_z, src_y),
            piece(core, src_z, src_y),
            sems.at[sem_idx],
            row_sem.at[src_z * NY + src_y],
            other,
        )

    def share(src_z, src_y):
        idx = src_z * NY + src_y
        return remote(
            piece(core, src_z, src_y),
            piece(core, src_z, src_y),
            share_sem.at[idx],
            pair_sem.at[idx],
            partner,
        )

    def arrived(src_z, src_y):
        idx = src_z * NY + src_y
        pltpu.make_async_copy(mine_ref.at[0], piece(core, src_z, src_y), row_sem.at[idx]).wait()

    right = at(y, lax.rem(z + 1, NZ), core)
    left = at(y, lax.rem(z + NZ - 1, NZ), core)

    @pl.loop(0, 6 * NY)
    def _(step):
        hop = step // NY
        src_y = lax.rem(y + lax.rem(step, NY), NY)
        from_left = lax.rem(z - hop + NZ, NZ)
        from_right = lax.rem(z + hop, NZ)

        @pl.when(hop <= pos + 2)
        def _():
            arrived(from_left, src_y)

            @pl.when(pos < LINE - 1)
            def _():
                forward(from_left, src_y, right_sem, step, right).start()

            @pl.when((hop == 0) & (pos > 0))
            def _():
                forward(from_left, src_y, left_sem, step, left).start()

            share(from_left, src_y).start()

        @pl.when((hop >= 1) & (hop <= 5 - pos))
        def _():
            arrived(from_right, src_y)

            @pl.when(pos > 0)
            def _():
                forward(from_right, src_y, left_sem, step, left).start()

            share(from_right, src_y).start()

    for copy in w_copies:
        copy.wait()

    pieces = 8
    chunk = pieces * 16
    my_half = pl.multiple_of(core * outw, 128)
    their_half = pl.multiple_of((1 - core) * outw, 128)

    def swap_copy(q):
        first = q * pieces
        return remote(
            part.at[pl.ds(first, pieces), :, pl.ds(their_half, outw)],
            swap.at[pl.ds(first, pieces)],
            swap_send.at[q],
            swap_recv.at[q],
            partner,
        )

    line_slot = (y * 2 + half) * LINE + pos

    def back_copy(idx):
        src_z = idx // NY
        src_y = lax.rem(idx, NY)
        return remote(
            summed.at[idx],
            landed.at[line_slot],
            back_send.at[idx],
            back_recv.at[line_slot],
            at(src_y, src_z, core),
        )

    def back_local(idx):
        return pltpu.make_async_copy(summed.at[idx], landed.at[line_slot], back_recv.at[line_slot])

    my_idx = z * NY + y

    def give_back(q):
        swap_copy(q).wait_recv()

        @pl.loop(0, pieces)
        def _(i):
            idx = q * pieces + i
            summed[idx] = (
                part[idx, :, pl.ds(my_half, outw)].astype(F32) + swap[idx].astype(F32)
            ).astype(BF16)

            @pl.when(idx == my_idx)
            def _():
                back_local(idx).start()

            @pl.when(idx != my_idx)
            def _():
                back_copy(idx).start()

    @pl.loop(0, 4)
    def _(order):
        q = lax.rem(z // 2 + 2 + order, 4)

        @pl.loop(0, pieces)
        def _(i):
            idx = q * pieces + i
            pltpu.make_async_copy(
                mine_ref.at[0], rows.at[1 - core, idx], pair_sem.at[idx]
            ).wait()

        u = rows[0, pl.ds(q * pieces, pieces)].reshape(chunk, width)
        dy = rows[1, pl.ds(q * pieces, pieces)].reshape(chunk, width)
        a = nt(u, wgu[0])
        b = nt(u, wgu[1])
        g = nt(dy, wd[...])
        sig = jax.nn.sigmoid(a)
        act = a * sig
        hdn = act * b
        dga = (g * b * sig * (1.0 + a * (1.0 - sig))).astype(BF16)
        dgb = (g * act).astype(BF16)
        where = pl.ds(pl.multiple_of(q * chunk, chunk), chunk)
        da[where] = dga
        db[where] = dgb
        hd[where] = hdn.astype(BF16)
        dc = jnp.sum(hdn * g, axis=1, keepdims=True)
        dc = jnp.broadcast_to(dc.astype(BF16), (chunk, 128)).reshape(pieces, 16, 128)
        for h in range(2):
            tile = 512
            for n in range(halfw // tile):
                col = h * halfw + n * tile
                du = nn(dga, wgu[0, :, col : col + tile]) + nn(dgb, wgu[1, :, col : col + tile])
                part[pl.ds(q * pieces, pieces), :, h * outw + n * tile : h * outw + (n + 1) * tile] = (
                    du.astype(BF16).reshape(pieces, 16, tile)
                )
            part[pl.ds(q * pieces, pieces), :, h * outw + halfw : (h + 1) * outw] = dc
        swap_copy(q).start()

        @pl.when(order > 0)
        def _():
            give_back(lax.rem(z // 2 + 1 + order, 4))

    give_back(lax.rem(z // 2 + 1, 4))

    tile = 512
    for n in range(width // tile):
        cols = slice(n * tile, (n + 1) * tile)
        u = rows[0, :, :, cols].reshape(-1, tile)
        dy = rows[1, :, :, cols].reshape(-1, tile)
        ggu[0, :, cols] = tn(da[...], u).astype(BF16)
        ggu[1, :, cols] = tn(db[...], u).astype(BF16)
        gd[:, cols] = tn(hd[...], dy).astype(BF16)
    out_copies = [
        pltpu.make_async_copy(ggu, ggu_hbm, out_sem.at[0]),
        pltpu.make_async_copy(gd, gd_hbm, out_sem.at[1]),
    ]
    for copy in out_copies:
        copy.start()

    for step in range(NY):
        if step > 0:
            entry(y * 2 + half, step, partner).wait_send()
        entry(y * 2 + 1 - half, NY + step, partner).wait_send()

    @pl.loop(0, 6 * NY)
    def _(step):
        hop = step // NY
        src_y = lax.rem(y + lax.rem(step, NY), NY)
        from_left = lax.rem(z - hop + NZ, NZ)
        from_right = lax.rem(z + hop, NZ)

        @pl.when((hop <= pos + 2) & (pos < LINE - 1))
        def _():
            forward(from_left, src_y, right_sem, step, right).wait_send()

        @pl.when((hop <= 5 - pos) & (pos > 0))
        def _():
            forward(from_right, src_y, left_sem, step, left).wait_send()

    @pl.loop(0, NY * NZ)
    def _(idx):
        share(idx // NY, lax.rem(idx, NY)).wait_send()

    @pl.loop(0, 4)
    def _(q):
        swap_copy(q).wait_send()

    @pl.loop(0, NY * 2)
    def _(e):
        total = jnp.zeros((16, outw), F32)
        for i in range(LINE):
            idx = e * LINE + i
            pltpu.make_async_copy(summed.at[0], landed.at[idx], back_recv.at[idx]).wait()
            total = total + landed[idx].astype(F32)
        back_ref[e] = total

    @pl.loop(0, NY * NZ)
    def _(idx):
        @pl.when(idx != my_idx)
        def _():
            back_copy(idx).wait_send()

    for copy in out_copies:
        copy.wait()


def experts(mine, wgu, wd):
    width = mine.shape[2]
    hidden = wd.shape[0]
    outw = width // 2 + 128
    slots = NY * NZ
    dma = pltpu.SemaphoreType.DMA
    return pl.pallas_call(
        expert_kernel,
        out_shape=(
            jax.ShapeDtypeStruct((NY * 2, 16, outw), F32),
            jax.ShapeDtypeStruct(wgu.shape, BF16),
            jax.ShapeDtypeStruct(wd.shape, BF16),
        ),
        in_specs=[
            pl.BlockSpec(memory_space=pltpu.VMEM),
            pl.BlockSpec(memory_space=pl.ANY),
            pl.BlockSpec(memory_space=pl.ANY),
        ],
        out_specs=(
            pl.BlockSpec(memory_space=pltpu.VMEM),
            pl.BlockSpec(memory_space=pl.ANY),
            pl.BlockSpec(memory_space=pl.ANY),
        ),
        scratch_shapes=[
            pltpu.VMEM((2, slots, 16, width), BF16),
            pltpu.VMEM(wgu.shape, BF16),
            pltpu.VMEM(wd.shape, BF16),
            pltpu.VMEM((slots, 16, 2 * outw), BF16),
            pltpu.VMEM((slots, 16, outw), BF16),
            pltpu.VMEM((slots, 16, outw), BF16),
            pltpu.VMEM((slots, 16, outw), BF16),
            pltpu.VMEM((slots * 16, hidden), BF16),
            pltpu.VMEM((slots * 16, hidden), BF16),
            pltpu.VMEM((slots * 16, hidden), BF16),
            pltpu.VMEM(wgu.shape, BF16),
            pltpu.VMEM(wd.shape, BF16),
            dma((slots,)),
            dma((slots,)),
            dma((6 * NY,)),
            dma((6 * NY,)),
            dma((slots,)),
            dma((2 * NY,)),
            dma((4,)),
            dma((4,)),
            dma((slots,)),
            dma((slots,)),
            dma((2,)),
            dma((2,)),
        ],
        compiler_params=pltpu.CompilerParams(
            collective_id=0, has_side_effects=True, vmem_limit_bytes=60 * 1024 * 1024
        ),
    )(mine, wgu, wd)


def on_device(hidden_in, out_grad, expert_ids, route_weight, norm_gain, w_gate_up, w_down):
    tokens_in = hidden_in[0]
    grad_out = out_grad[0]
    chosen = expert_ids[0]
    weights_in = route_weight[0]
    gain_row = norm_gain[0]
    devices = lax.axis_size("expert")
    span = devices // SPLIT
    width = tokens_in.shape[1]
    core = lax.rem(lax.axis_index("expert"), 2)
    pairs = [(i, i ^ 1) for i in range(devices)]

    tokens_f = tokens_in.astype(F32)
    rms_value = jnp.sqrt(jnp.mean(tokens_f * tokens_f, axis=-1, keepdims=True) + 1e-06)
    normed = tokens_f / rms_value
    normed_in = (normed * gain_row).astype(BF16)
    expert_range = jnp.arange(span, dtype=jnp.int32)
    picked = chosen[:, :, None] == expert_range[None, None, :]
    member = jnp.any(picked, axis=1).astype(jnp.int32)
    weight_te = jnp.sum(jnp.where(picked, weights_in.astype(F32)[:, :, None], 0.0), axis=1)
    position = jnp.cumsum(member, axis=0) - member
    slot_range = jnp.arange(CAP, dtype=jnp.int32)
    placing = (position.T[:, None, :] == slot_range[None, :, None]) & (member.T[:, None, :] == 1)
    place_f = placing.astype(F32)
    place_bf = placing.astype(BF16)
    place_w = (place_f * weight_te.T[:, None, :]).astype(BF16)
    sent_in = jnp.einsum("wst,td->wsd", place_bf, normed_in, preferred_element_type=F32).astype(BF16)
    sent_grad = jnp.einsum("wst,td->wsd", place_w, grad_out, preferred_element_type=F32).astype(BF16)
    keep = jnp.where(core == 0, sent_in, sent_grad)
    give = jnp.where(core == 0, sent_grad, sent_in)
    got = lax.ppermute(give, "expert", pairs)
    first = jnp.where(core == 0, keep, got)
    second = jnp.where(core == 0, got, keep)
    mine = jnp.concatenate([first, second], axis=1)

    back, grad_gate_up, grad_down = experts(mine, w_gate_up[0, 0], w_down[0, 0])

    rows_first, rows_second = back[:, :CAP], back[:, CAP:]
    keep = jnp.where(core == 0, rows_first, rows_second)
    give = jnp.where(core == 0, rows_second, rows_first)
    got = lax.ppermute(give.astype(BF16), "expert", pairs).astype(F32)
    halfw = width // 2
    low = jnp.where(core == 0, keep, got)
    high = jnp.where(core == 0, got, keep)
    summed_in = jnp.concatenate([low[:, :, :halfw], high[:, :, :halfw]], axis=-1)
    summed_comb = 0.5 * (low[:, :, halfw] + high[:, :, halfw])

    grad_normed = jnp.einsum("wst,wsd->td", place_f, summed_in, precision=lax.Precision.HIGHEST)
    comb_te = jnp.sum(place_f * summed_comb[:, :, None], axis=1)
    comb_te = comb_te / jnp.where(member.T == 1, weight_te.T, 1.0)
    grad_combine = jnp.sum(jnp.where(picked, comb_te.T[:, None, :], 0.0), axis=-1)
    scaled = grad_normed * gain_row
    inner_mean = jnp.mean(scaled * normed, axis=-1, keepdims=True)
    grad_tokens = (
        grad_out.astype(F32) + (scaled - normed * inner_mean) / rms_value
    ).astype(BF16)
    stages = lax.axis_size("pipe")
    handed = lax.ppermute(grad_tokens, "pipe", [((i + 1) % stages, i) for i in range(stages)])
    return (
        handed[None],
        grad_gate_up[None, None],
        grad_down[None, None],
        grad_combine[None],
    )


def solution(mesh):
    return jax.shard_map(
        on_device,
        mesh=mesh,
        in_specs=(
            P("pipe", "expert", None),
            P("pipe", "expert", None),
            P("pipe", "expert", None),
            P("pipe", "expert", None),
            P("pipe", None),
            P("pipe", "expert", None, None, None),
            P("pipe", "expert", None, None),
        ),
        out_specs=(
            P("pipe", "expert", None),
            P("pipe", "expert", None, None, None),
            P("pipe", "expert", None, None),
            P("pipe", "expert", None),
        ),
        check_vma=False,
    )
```

```python
import jax
import jax.numpy as jnp
from jax import lax
from jax.experimental import pallas as pl
from jax.experimental.pallas import tpu as pltpu
from jax.sharding import PartitionSpec as P

SPLIT = 8
CAP = 8
NY = 4
NZ = 8
LINE = 4
MESH = pl.DeviceIdType.MESH
F32 = jnp.float32
BF16 = jnp.bfloat16


def nt(left, right):
    return lax.dot_general(left, right, (((1,), (1,)), ((), ())), preferred_element_type=F32)


def nn(left, right):
    return lax.dot_general(left, right, (((1,), (0,)), ((), ())), preferred_element_type=F32)


def tn(left, right):
    return lax.dot_general(left, right, (((0,), (0,)), ((), ())), preferred_element_type=F32)


def expert_kernel(
    mine_ref,
    wgu_hbm,
    wd_hbm,
    hidden_ref,
    grad_ref,
    gain_ref,
    place_ref,
    back_ref,
    ggu_hbm,
    gd_hbm,
    hidden_next,
    grad_next,
    gain_next,
    place_next,
    rows,
    wgu,
    wd,
    part,
    swap,
    chain,
    summed,
    final,
    acc,
    da,
    db,
    hd,
    ggu,
    gd,
    row_sem,
    pair_sem,
    right_sem,
    left_sem,
    share_sem,
    entry_sem,
    swap_send,
    swap_recv,
    chain_send,
    chain_recv,
    final_send,
    back_recv,
    w_sem,
    out_sem,
    early_send,
    early_recv,
):
    me = lax.axis_index("expert")
    stage = lax.axis_index("pipe")
    stages = lax.axis_size("pipe")
    before = lax.rem(stage + stages - 1, stages)
    after = lax.rem(stage + 1, stages)
    core = lax.rem(me, 2)
    z = lax.rem(me // 2, NZ)
    y = me // (2 * NZ)
    half = z // LINE
    pos = lax.rem(z, LINE)
    expert = y * 2 + half
    width = mine_ref.shape[2]
    halfw = width // 2
    outw = halfw + 128
    slots = NY * NZ
    last = LINE - 1
    at_end = (pos == 0) | (pos == last)

    def at(yy, zz, cc):
        return (yy * NZ + zz) * 2 + cc

    partner = at(y, z, 1 - core)
    right = at(y, lax.rem(z + 1, NZ), core)
    left = at(y, lax.rem(z + NZ - 1, NZ), core)
    entry_z = jnp.where(pos >= 2, lax.rem(LINE * (half + 1), NZ), lax.rem(LINE * half + NZ - 1, NZ))

    barrier = pltpu.get_barrier_semaphore()

    def greet(pipe, other):
        pl.semaphore_signal(
            barrier, inc=1, device_id={"pipe": pipe, "expert": other}, device_id_type=MESH
        )

    greet(stage, partner)
    for step in range(1, NY):
        greet(stage, at(lax.rem(y + step, NY), z, core))

    @pl.when(pos > 0)
    def _():
        greet(stage, left)

    @pl.when(pos < last)
    def _():
        greet(stage, right)

    @pl.when(at_end)
    def _():
        way = jnp.where(pos == 0, NZ - 1, 1)
        for hop in (1, 2):
            for yy in range(NY):
                greet(stage, at(yy, lax.rem(z + hop * way, NZ), core))

    for cc in range(2):
        for yy in range(NY):
            greet(after, at(yy, z, cc))
            greet(after, at(yy, entry_z, cc))

    w_copies = [
        pltpu.make_async_copy(wgu_hbm, wgu, w_sem.at[0]),
        pltpu.make_async_copy(wd_hbm, wd, w_sem.at[1]),
    ]
    for copy in w_copies:
        copy.start()
    common = 1 + (NY - 1) + NY + 2 * NY
    pl.semaphore_wait(barrier, jnp.where(at_end, common + 1 + 4 * NY, common + 2))

    def remote(src, dst, send, recv, other, pipe=None):
        return pltpu.make_async_remote_copy(
            src_ref=src,
            dst_ref=dst,
            send_sem=send,
            recv_sem=recv,
            device_id={"pipe": stage if pipe is None else pipe, "expert": other},
            device_id_type=MESH,
        )

    slot = z * NY + y

    def entry(src_idx, sem_idx, other):
        return remote(
            mine_ref.at[src_idx], rows.at[core, slot], entry_sem.at[sem_idx], row_sem.at[slot], other
        )

    own_copy = pltpu.make_async_copy(mine_ref.at[expert], rows.at[core, slot], row_sem.at[slot])
    own_copy.start()
    for step in range(NY):
        yy = lax.rem(y + step, NY)
        if step > 0:
            entry(yy * 2 + half, step, at(yy, z, core)).start()
        entry(yy * 2 + 1 - half, NY + step, at(yy, entry_z, core)).start()

    early = [
        remote(src, dst, early_send.at[i], early_recv.at[i], me, before)
        for i, (src, dst) in enumerate(
            (
                (hidden_ref, hidden_next),
                (grad_ref, grad_next),
                (gain_ref, gain_next),
                (place_ref, place_next),
            )
        )
    ]
    for copy in early:
        copy.start()

    def piece(idx):
        return rows.at[core, idx]

    def forward(idx, sems, sem_idx, other):
        return remote(piece(idx), piece(idx), sems.at[sem_idx], row_sem.at[idx], other)

    def share(idx):
        return remote(piece(idx), piece(idx), share_sem.at[idx], pair_sem.at[idx], partner)

    def arrived(idx):
        pltpu.make_async_copy(mine_ref.at[0], piece(idx), row_sem.at[idx]).wait()

    def z_of(offset):
        return lax.rem(z + offset + NZ, NZ)

    my_half = pl.multiple_of(core * outw, 128)
    their_half = pl.multiple_of((1 - core) * outw, 128)
    block = NY * 16

    def swap_copy(src_z):
        span = pl.ds(src_z * NY, NY)
        return remote(
            part.at[span, :, pl.ds(their_half, outw)],
            swap.at[span],
            swap_send.at[src_z],
            swap_recv.at[src_z],
            partner,
        )

    def compute(src_z):
        @pl.loop(0, NY)
        def _(j):
            idx = src_z * NY + j
            pltpu.make_async_copy(
                mine_ref.at[0], rows.at[1 - core, idx], pair_sem.at[idx]
            ).wait()

        span = pl.ds(src_z * NY, NY)
        u = rows[0, span].reshape(block, width)
        dy = rows[1, span].reshape(block, width)
        a = nt(u, wgu[0])
        b = nt(u, wgu[1])
        g = nt(dy, wd[...])
        sig = jax.nn.sigmoid(a)
        act = a * sig
        hdn = act * b
        dga = (g * b * sig * (1.0 + a * (1.0 - sig))).astype(BF16)
        dgb = (g * act).astype(BF16)
        where = pl.ds(pl.multiple_of(src_z * block, block), block)
        da[where] = dga
        db[where] = dgb
        hd[where] = hdn.astype(BF16)
        dc = jnp.sum(hdn * g, axis=1, keepdims=True)
        dc = jnp.broadcast_to(dc.astype(BF16), (block, 128)).reshape(NY, 16, 128)
        part[span, :, :128] = dc
        part[span, :, width + 128 :] = dc
        tile = 512
        for n in range(width // tile):
            du = nn(dga, wgu[0, :, n * tile : (n + 1) * tile]) + nn(
                dgb, wgu[1, :, n * tile : (n + 1) * tile]
            )
            part[span, :, 128 + n * tile : 128 + (n + 1) * tile] = du.astype(BF16).reshape(
                NY, 16, tile
            )
        swap_copy(src_z).start()

    def chain_in(idx):
        pltpu.make_async_copy(summed.at[0], chain.at[idx], chain_recv.at[idx]).wait()
        acc[...] += chain[idx].astype(F32)

    def chain_out(idx, dst, other):
        return remote(summed.at[idx], chain.at[dst], chain_send.at[idx], chain_recv.at[dst], other)

    def final_out(number, cc, src_y, src_z):
        return remote(
            final.at[number, pl.ds(cc * CAP, CAP)],
            back_ref.at[expert, :, pl.ds(my_half, outw)],
            final_send.at[2 * number + cc],
            back_recv.at[2 * expert + core],
            at(src_y, src_z, cc),
            before,
        )

    def finish(number, src_y, src_z):
        final[number] = acc[...]
        for cc in range(2):
            final_out(number, cc, src_y, src_z).start()

    def combine(src_z, hop, kind):
        swap_copy(src_z).wait_recv()

        @pl.loop(0, NY)
        def _(j):
            idx = src_z * NY + j
            acc[...] = part[idx, :, pl.ds(my_half, outw)].astype(F32) + swap[idx].astype(F32)
            if kind == 0:

                @pl.when(pos < last)
                def _():
                    chain_in(idx)

                @pl.when(pos > 0)
                def _():
                    chain_in(slots + j)

                finish(j, j, src_z)
            elif kind < 0:

                @pl.when(pos < last)
                def _():
                    chain_in(idx)

                @pl.when(pos > 0)
                def _():
                    summed[idx] = acc[...].astype(BF16)
                    chain_out(idx, idx, left).start()

                @pl.when(pos == 0)
                def _():
                    finish(hop * NY + j, j, src_z)
            else:

                @pl.when(pos > 0)
                def _():
                    chain_in(idx)

                @pl.when(pos < last)
                def _():
                    summed[idx] = acc[...].astype(BF16)
                    chain_out(idx, jnp.where(hop == 1, slots + j, idx), right).start()

                @pl.when(pos == last)
                def _():
                    finish(hop * NY + j, j, src_z)

    wait_own = 2 + 2 * jnp.where(pos >= 2, pos, last - pos)

    @pl.loop(0, 11)
    def _(it):
        @pl.when(it <= 5)
        def _():
            @pl.loop(0, NY)
            def _(j):
                src_y = lax.rem(y + j, NY)
                number = it * NY + j
                from_left = z_of(-it) * NY + src_y
                from_right = z_of(it) * NY + src_y

                @pl.when(it <= pos + 2)
                def _():
                    arrived(from_left)

                    @pl.when(pos < last)
                    def _():
                        forward(from_left, right_sem, number, right).start()

                    @pl.when((it == 0) & (pos > 0))
                    def _():
                        forward(from_left, left_sem, number, left).start()

                    share(from_left).start()

                @pl.when((it >= 1) & (it <= 5 - pos))
                def _():
                    arrived(from_right)

                    @pl.when(pos > 0)
                    def _():
                        forward(from_right, left_sem, number, left).start()

                    share(from_right).start()

        @pl.when(it == 1)
        def _():
            for copy in w_copies:
                copy.wait()

        hop = it - 1

        @pl.loop(0, 2)
        def _(way):
            @pl.when(
                (hop <= 5)
                & (hop >= way)
                & (hop <= jnp.where(way == 0, pos + 2, 5 - pos))
            )
            def _():
                compute(z_of(jnp.where(way == 0, -hop, hop)))

        hop_l = it - 2 - 2 * (last - pos)

        @pl.when((hop_l >= 1) & (hop_l <= pos + 2))
        def _():
            combine(z_of(-hop_l), hop_l, -1)

        hop_r = it - 2 - 2 * pos

        @pl.when((hop_r >= 1) & (hop_r <= 5 - pos))
        def _():
            combine(z_of(hop_r), hop_r, 1)

        @pl.when(it == wait_own)
        def _():
            combine(z, 0, 0)

        @pl.loop(0, 2)
        def _(s):
            n = 2 * (it - 6) - 1 + s
            tile = 512

            @pl.when((n >= 0) & (n < width // tile))
            def _():
                cols = pl.ds(pl.multiple_of(n * tile, tile), tile)
                u = rows[0, :, :, cols].reshape(-1, tile)
                dy = rows[1, :, :, cols].reshape(-1, tile)
                ggu[0, :, cols] = tn(da[...], u).astype(BF16)
                ggu[1, :, cols] = tn(db[...], u).astype(BF16)
                gd[:, cols] = tn(hd[...], dy).astype(BF16)

    out_copies = [
        pltpu.make_async_copy(ggu, ggu_hbm, out_sem.at[0]),
        pltpu.make_async_copy(gd, gd_hbm, out_sem.at[1]),
    ]
    for copy in out_copies:
        copy.start()

    for step in range(NY):
        if step > 0:
            entry(expert, step, partner).wait_send()
        entry(expert, NY + step, partner).wait_send()
    for copy in early:
        copy.wait()

    @pl.loop(0, 6)
    def _(hop):
        from_left = z_of(-hop)
        from_right = z_of(hop)

        @pl.loop(0, NY)
        def _(j):
            src_y = lax.rem(y + j, NY)

            @pl.when((hop <= pos + 2) & (pos < last))
            def _():
                forward(from_left * NY + src_y, right_sem, hop * NY + j, right).wait_send()

            @pl.when((hop <= 5 - pos) & (pos > 0))
            def _():
                forward(from_right * NY + src_y, left_sem, hop * NY + j, left).wait_send()

            @pl.when((hop >= 1) & (hop <= pos + 2) & (pos > 0))
            def _():
                idx = from_left * NY + j
                chain_out(idx, idx, left).wait_send()

            @pl.when((hop >= 1) & (hop <= 5 - pos) & (pos < last))
            def _():
                idx = from_right * NY + j
                chain_out(idx, idx, right).wait_send()

            @pl.when((hop == 0) | ((hop <= 2) & at_end))
            def _():
                for cc in range(2):
                    final_out(hop * NY + j, cc, j, z).wait_send()

    @pl.loop(0, slots)
    def _(idx):
        share(idx).wait_send()

    @pl.loop(0, NZ)
    def _(src_z):
        swap_copy(src_z).wait_send()

    for e in range(NY * 2):
        for cc in range(2):
            pltpu.make_async_copy(
                final.at[0, pl.ds(0, CAP)],
                back_ref.at[e, :, pl.ds(cc * outw, outw)],
                back_recv.at[2 * e + cc],
            ).wait()
    for copy in out_copies:
        copy.wait()


def experts(mine, wgu, wd, hidden, grad, gain, place):
    width = mine.shape[2]
    units = wd.shape[0]
    outw = width // 2 + 128
    slots = NY * NZ
    dma = pltpu.SemaphoreType.DMA
    hbm = pl.BlockSpec(memory_space=pl.ANY)
    vmem = pl.BlockSpec(memory_space=pltpu.VMEM)
    like = lambda array: jax.ShapeDtypeStruct(array.shape, array.dtype)
    return pl.pallas_call(
        expert_kernel,
        out_shape=(
            jax.ShapeDtypeStruct((NY * 2, CAP, 2 * outw), F32),
            like(wgu),
            like(wd),
            like(hidden),
            like(grad),
            like(gain),
            like(place),
        ),
        in_specs=[vmem] + [hbm] * 6,
        out_specs=[vmem] + [hbm] * 6,
        scratch_shapes=[
            pltpu.VMEM((2, slots, 16, width), BF16),
            pltpu.VMEM(wgu.shape, BF16),
            pltpu.VMEM(wd.shape, BF16),
            pltpu.VMEM((slots, 16, 2 * outw), BF16),
            pltpu.VMEM((slots, 16, outw), BF16),
            pltpu.VMEM((slots + NY, 16, outw), BF16),
            pltpu.VMEM((slots, 16, outw), BF16),
            pltpu.VMEM((3 * NY, 16, outw), F32),
            pltpu.VMEM((16, outw), F32),
            pltpu.VMEM((slots * 16, units), BF16),
            pltpu.VMEM((slots * 16, units), BF16),
            pltpu.VMEM((slots * 16, units), BF16),
            pltpu.VMEM(wgu.shape, BF16),
            pltpu.VMEM(wd.shape, BF16),
            dma((slots,)),
            dma((slots,)),
            dma((6 * NY,)),
            dma((6 * NY,)),
            dma((slots,)),
            dma((2 * NY,)),
            dma((NZ,)),
            dma((NZ,)),
            dma((slots,)),
            dma((slots + NY,)),
            dma((6 * NY,)),
            dma((4 * NY,)),
            dma((2,)),
            dma((2,)),
            dma((4,)),
            dma((4,)),
        ],
        compiler_params=pltpu.CompilerParams(
            collective_id=0, has_side_effects=True, vmem_limit_bytes=60 * 1024 * 1024
        ),
    )(mine, wgu, wd, hidden, grad, gain, place)


def on_device(hidden_in, out_grad, expert_ids, route_weight, norm_gain, w_gate_up, w_down):
    tokens_in = hidden_in[0]
    grad_out = out_grad[0]
    chosen = expert_ids[0]
    weights_in = route_weight[0]
    gain_row = norm_gain[0]
    devices = lax.axis_size("expert")
    span = devices // SPLIT
    width = tokens_in.shape[1]
    core = lax.rem(lax.axis_index("expert"), 2)
    pairs = [(i, i ^ 1) for i in range(devices)]

    tokens_f = tokens_in.astype(F32)
    rms_value = jnp.sqrt(jnp.mean(tokens_f * tokens_f, axis=-1, keepdims=True) + 1e-06)
    normed = tokens_f / rms_value
    normed_in = (normed * gain_row).astype(BF16)
    expert_range = jnp.arange(span, dtype=jnp.int32)
    picked = chosen[:, :, None] == expert_range[None, None, :]
    member = jnp.any(picked, axis=1).astype(jnp.int32)
    weight_te = jnp.sum(jnp.where(picked, weights_in.astype(F32)[:, :, None], 0.0), axis=1)
    position = jnp.cumsum(member, axis=0) - member
    slot_range = jnp.arange(CAP, dtype=jnp.int32)
    placing = (position.T[:, None, :] == slot_range[None, :, None]) & (member.T[:, None, :] == 1)
    place_f = placing.astype(F32)
    place_bf = placing.astype(BF16)
    place_w = (place_f * weight_te.T[:, None, :]).astype(BF16)
    sent_in = jnp.einsum("wst,td->wsd", place_bf, normed_in, preferred_element_type=F32).astype(BF16)
    sent_grad = jnp.einsum("wst,td->wsd", place_w, grad_out, preferred_element_type=F32).astype(BF16)
    keep = jnp.where(core == 0, sent_in, sent_grad)
    give = jnp.where(core == 0, sent_grad, sent_in)
    got = lax.ppermute(give, "expert", pairs)
    first = jnp.where(core == 0, keep, got)
    second = jnp.where(core == 0, got, keep)
    mine = jnp.concatenate([first, second], axis=1)

    back, grad_gate_up, grad_down, hidden_next, grad_next, gain_next, place_next = experts(
        mine,
        w_gate_up[0, 0],
        w_down[0, 0],
        tokens_in,
        grad_out,
        gain_row.reshape(-1, 128),
        place_bf.reshape(span * CAP, -1),
    )

    stages = lax.axis_size("pipe")
    comb_rows = lax.ppermute(
        back[:, :, 0], "pipe", [(i, (i + 1) % stages) for i in range(stages)]
    )
    summed_in = back[:, :, 128 : width + 128].reshape(span * CAP, width)
    grad_normed = lax.dot_general(
        place_next.astype(F32),
        summed_in,
        (((0,), (0,)), ((), ())),
        precision=lax.Precision.HIGHEST,
        preferred_element_type=F32,
    )
    next_f = hidden_next.astype(F32)
    next_rms = jnp.sqrt(jnp.mean(next_f * next_f, axis=-1, keepdims=True) + 1e-06)
    next_normed = next_f / next_rms
    scaled = grad_normed * gain_next.reshape(width)
    inner_mean = jnp.mean(scaled * next_normed, axis=-1, keepdims=True)
    handed = (
        grad_next.astype(F32) + (scaled - next_normed * inner_mean) / next_rms
    ).astype(BF16)

    comb_te = jnp.sum(place_f * comb_rows[:, :, None], axis=1)
    comb_te = comb_te / jnp.where(member.T == 1, weight_te.T, 1.0)
    grad_combine = jnp.sum(jnp.where(picked, comb_te.T[:, None, :], 0.0), axis=-1)
    return (
        handed[None],
        grad_gate_up[None, None],
        grad_down[None, None],
        grad_combine[None],
    )


def solution(mesh):
    return jax.shard_map(
        on_device,
        mesh=mesh,
        in_specs=(
            P("pipe", "expert", None),
            P("pipe", "expert", None),
            P("pipe", "expert", None),
            P("pipe", "expert", None),
            P("pipe", None),
            P("pipe", "expert", None, None, None),
            P("pipe", "expert", None, None),
        ),
        out_specs=(
            P("pipe", "expert", None),
            P("pipe", "expert", None, None, None),
            P("pipe", "expert", None, None),
            P("pipe", "expert", None),
        ),
        check_vma=False,
    )
```

```python
import jax
import jax.numpy as jnp
from jax import lax
from jax.experimental import pallas as pl
from jax.experimental.pallas import tpu as pltpu
from jax.sharding import PartitionSpec as P

SPLIT = 8
CAP = 8
NY = 4
NZ = 8
LINE = 4
MESH = pl.DeviceIdType.MESH
F32 = jnp.float32
BF16 = jnp.bfloat16


def nt(left, right):
    return lax.dot_general(left, right, (((1,), (1,)), ((), ())), preferred_element_type=F32)


def nn(left, right):
    return lax.dot_general(left, right, (((1,), (0,)), ((), ())), preferred_element_type=F32)


def tn(left, right):
    return lax.dot_general(left, right, (((0,), (0,)), ((), ())), preferred_element_type=F32)


def expert_kernel(
    mine_ref,
    wgu_hbm,
    wd_hbm,
    hidden_ref,
    grad_ref,
    gain_ref,
    place_ref,
    back_ref,
    ggu_hbm,
    gd_hbm,
    hidden_next,
    grad_next,
    gain_next,
    place_next,
    rows,
    wgu,
    wd,
    part,
    swap,
    chain,
    summed,
    final,
    acc,
    da,
    db,
    hd,
    ggu,
    gd,
    row_sem,
    pair_sem,
    right_sem,
    left_sem,
    share_sem,
    entry_sem,
    swap_send,
    swap_recv,
    chain_send,
    chain_recv,
    final_send,
    back_recv,
    w_sem,
    out_sem,
    early_send,
    early_recv,
):
    me = lax.axis_index("expert")
    stage = lax.axis_index("pipe")
    stages = lax.axis_size("pipe")
    before = lax.rem(stage + stages - 1, stages)
    after = lax.rem(stage + 1, stages)
    core = lax.rem(me, 2)
    z = lax.rem(me // 2, NZ)
    y = me // (2 * NZ)
    half = z // LINE
    pos = lax.rem(z, LINE)
    expert = y * 2 + half
    width = mine_ref.shape[2]
    halfw = width // 2
    outw = halfw + 128
    slots = NY * NZ
    last = LINE - 1
    at_end = (pos == 0) | (pos == last)

    def at(yy, zz, cc):
        return (yy * NZ + zz) * 2 + cc

    partner = at(y, z, 1 - core)
    right = at(y, lax.rem(z + 1, NZ), core)
    left = at(y, lax.rem(z + NZ - 1, NZ), core)
    entry_z = jnp.where(pos >= 2, lax.rem(LINE * (half + 1), NZ), lax.rem(LINE * half + NZ - 1, NZ))

    barrier = pltpu.get_barrier_semaphore()

    def greet(pipe, other):
        pl.semaphore_signal(
            barrier, inc=1, device_id={"pipe": pipe, "expert": other}, device_id_type=MESH
        )

    greet(stage, partner)
    for step in range(1, NY):
        greet(stage, at(lax.rem(y + step, NY), z, core))

    @pl.when(pos > 0)
    def _():
        greet(stage, left)

    @pl.when(pos < last)
    def _():
        greet(stage, right)

    @pl.when(at_end)
    def _():
        way = jnp.where(pos == 0, NZ - 1, 1)
        for hop in (1, 2):
            for yy in range(NY):
                greet(stage, at(yy, lax.rem(z + hop * way, NZ), core))

    for cc in range(2):
        for yy in range(NY):
            greet(after, at(yy, z, cc))
            greet(after, at(yy, entry_z, cc))

    w_copies = [
        pltpu.make_async_copy(wgu_hbm, wgu, w_sem.at[0]),
        pltpu.make_async_copy(wd_hbm, wd, w_sem.at[1]),
    ]
    for copy in w_copies:
        copy.start()
    common = 1 + (NY - 1) + NY + 2 * NY
    pl.semaphore_wait(barrier, jnp.where(at_end, common + 1 + 4 * NY, common + 2))

    def remote(src, dst, send, recv, other, pipe=None):
        return pltpu.make_async_remote_copy(
            src_ref=src,
            dst_ref=dst,
            send_sem=send,
            recv_sem=recv,
            device_id={"pipe": stage if pipe is None else pipe, "expert": other},
            device_id_type=MESH,
        )

    slot = z * NY + y

    def entry(src_idx, sem_idx, other):
        return remote(
            mine_ref.at[src_idx], rows.at[core, slot], entry_sem.at[sem_idx], row_sem.at[slot], other
        )

    own_copy = pltpu.make_async_copy(mine_ref.at[expert], rows.at[core, slot], row_sem.at[slot])
    own_copy.start()
    for step in range(NY):
        yy = lax.rem(y + step, NY)
        if step > 0:
            entry(yy * 2 + half, step, at(yy, z, core)).start()
        entry(yy * 2 + 1 - half, NY + step, at(yy, entry_z, core)).start()

    early = [
        remote(src, dst, early_send.at[i], early_recv.at[i], me, before)
        for i, (src, dst) in enumerate(
            (
                (hidden_ref, hidden_next),
                (grad_ref, grad_next),
                (gain_ref, gain_next),
                (place_ref, place_next),
            )
        )
    ]
    for copy in early:
        copy.start()

    def piece(idx):
        return rows.at[core, idx]

    def forward(idx, sems, other):
        return remote(piece(idx), piece(idx), sems.at[idx], row_sem.at[idx], other)

    def share(idx):
        return remote(piece(idx), piece(idx), share_sem.at[idx], pair_sem.at[idx], partner)

    def arrived(idx):
        pltpu.make_async_copy(mine_ref.at[0], piece(idx), row_sem.at[idx]).wait()

    def z_of(offset):
        return lax.rem(z + offset + NZ, NZ)

    my_half = pl.multiple_of(core * outw, 128)
    their_half = pl.multiple_of((1 - core) * outw, 128)
    block = NY * 16

    def swap_copy(src_z):
        span = pl.ds(src_z * NY, NY)
        return remote(
            part.at[span, :, pl.ds(their_half, outw)],
            swap.at[span],
            swap_send.at[src_z],
            swap_recv.at[src_z],
            partner,
        )

    def compute(src_z):
        @pl.loop(0, NY)
        def _(j):
            idx = src_z * NY + j
            pltpu.make_async_copy(
                mine_ref.at[0], rows.at[1 - core, idx], pair_sem.at[idx]
            ).wait()

        span = pl.ds(src_z * NY, NY)
        u = rows[0, span].reshape(block, width)
        dy = rows[1, span].reshape(block, width)
        a = nt(u, wgu[0])
        b = nt(u, wgu[1])
        g = nt(dy, wd[...])
        sig = jax.nn.sigmoid(a)
        act = a * sig
        hdn = act * b
        dga = (g * b * sig * (1.0 + a * (1.0 - sig))).astype(BF16)
        dgb = (g * act).astype(BF16)
        where = pl.ds(pl.multiple_of(src_z * block, block), block)
        da[where] = dga
        db[where] = dgb
        hd[where] = hdn.astype(BF16)
        dc = jnp.sum(hdn * g, axis=1, keepdims=True)
        dc = jnp.broadcast_to(dc.astype(BF16), (block, 128)).reshape(NY, 16, 128)
        part[span, :, :128] = dc
        part[span, :, width + 128 :] = dc
        tile = 512
        for n in range(width // tile):
            du = nn(dga, wgu[0, :, n * tile : (n + 1) * tile]) + nn(
                dgb, wgu[1, :, n * tile : (n + 1) * tile]
            )
            part[span, :, 128 + n * tile : 128 + (n + 1) * tile] = du.astype(BF16).reshape(
                NY, 16, tile
            )
        swap_copy(src_z).start()

    def chain_in(idx):
        pltpu.make_async_copy(summed.at[0], chain.at[idx], chain_recv.at[idx]).wait()
        acc[...] += chain[idx].astype(F32)

    def chain_out(idx, dst, other):
        return remote(summed.at[idx], chain.at[dst], chain_send.at[idx], chain_recv.at[dst], other)

    def final_out(number, cc, src_y, src_z):
        return remote(
            final.at[number, pl.ds(cc * CAP, CAP)],
            back_ref.at[expert, :, pl.ds(my_half, outw)],
            final_send.at[2 * number + cc],
            back_recv.at[2 * expert + core],
            at(src_y, src_z, cc),
            before,
        )

    def finish(number, src_y, src_z):
        final[number] = acc[...].astype(BF16)
        for cc in range(2):
            final_out(number, cc, src_y, src_z).start()

    def combine(src_z, hop, kind):
        swap_copy(src_z).wait_recv()

        @pl.loop(0, NY)
        def _(j):
            idx = src_z * NY + j
            acc[...] = part[idx, :, pl.ds(my_half, outw)].astype(F32) + swap[idx].astype(F32)
            if kind == 0:

                @pl.when(pos < last)
                def _():
                    chain_in(idx)

                @pl.when(pos > 0)
                def _():
                    chain_in(slots + j)

                finish(j, j, src_z)
            elif kind < 0:

                @pl.when(pos < last)
                def _():
                    chain_in(idx)

                @pl.when(pos > 0)
                def _():
                    summed[idx] = acc[...].astype(BF16)
                    chain_out(idx, idx, left).start()

                @pl.when(pos == 0)
                def _():
                    finish(hop * NY + j, j, src_z)
            else:

                @pl.when(pos > 0)
                def _():
                    chain_in(idx)

                @pl.when(pos < last)
                def _():
                    summed[idx] = acc[...].astype(BF16)
                    chain_out(idx, jnp.where(hop == 1, slots + j, idx), right).start()

                @pl.when(pos == last)
                def _():
                    finish(hop * NY + j, j, src_z)

    def list_at(place, slot):
        near = jnp.where(slot == 1, place - 1, jnp.where(slot == 5, 1, place + 4 - slot))
        return jnp.where(place < 2, place + 3 - slot, near)

    def origin(slot):
        return jnp.where(slot == 1, 1, jnp.where(slot == 5, 2, slot - 4))

    flip = last - pos

    def own_idx(j):
        return z * NY + lax.rem(y + NY - j, NY)

    @pl.loop(0, 16)
    def _(it):
        slot_now = it // 2
        part_now = lax.rem(it, 2)

        for jj in range(2):
            j = 2 * part_now + jj
            src_y = lax.rem(y + NY - j, NY)

            @pl.when(slot_now == 0)
            def _():
                idx = own_idx(j)
                arrived(idx)

                @pl.when(pos == 1)
                def _():
                    forward(idx, right_sem, right).start()

                @pl.when(pos == 2)
                def _():
                    forward(idx, left_sem, left).start()

                share(idx).start()

            @pl.when((slot_now >= 1) & (slot_now <= pos + 2))
            def _():
                idx = z_of(-list_at(pos, slot_now)) * NY + src_y
                arrived(idx)

                @pl.when(pos < last)
                def _():
                    forward(idx, right_sem, right).start()

                share(idx).start()

            @pl.when((slot_now >= 1) & (slot_now <= flip + 2))
            def _():
                idx = z_of(list_at(flip, slot_now)) * NY + src_y
                arrived(idx)

                @pl.when(pos > 0)
                def _():
                    forward(idx, left_sem, left).start()

                share(idx).start()

        @pl.when(((it == 5) & (pos == 0)) | ((it == 9) & (pos == 2)))
        def _():
            for j in range(NY):
                forward(own_idx(j), right_sem, right).start()

        @pl.when(((it == 5) & (flip == 0)) | ((it == 9) & (flip == 2)))
        def _():
            for j in range(NY):
                forward(own_idx(j), left_sem, left).start()

        @pl.when(it == 2)
        def _():
            for copy in w_copies:
                copy.wait()

        slot_done = slot_now - 1
        limit = jnp.where(part_now == 0, pos + 2, flip + 2)

        @pl.when((slot_done >= part_now) & (slot_done <= limit) & (slot_done <= 5))
        def _():
            place = jnp.where(part_now == 0, pos, flip)
            away = jnp.where(slot_done == 0, 0, list_at(place, slot_done))
            compute(z_of(jnp.where(part_now == 0, -away, away)))

        since_l = it - 3 - flip
        slot_l = since_l // 2
        away_l = pos - origin(slot_l)

        @pl.when((since_l >= 2) & (lax.rem(since_l + 2, 2) == 0) & (slot_l <= 5) & (away_l >= 1))
        def _():
            combine(z_of(-away_l), away_l, -1)

        since_r = it - 4 - pos
        slot_r = since_r // 2
        away_r = flip - origin(slot_r)

        @pl.when((since_r >= 2) & (lax.rem(since_r + 2, 2) == 0) & (slot_r <= 5) & (away_r >= 1))
        def _():
            combine(z_of(away_r), away_r, 1)

        @pl.when(it == 14 + lax.rem(pos, 2))
        def _():
            combine(z, 0, 0)

        @pl.loop(0, 3)
        def _(s):
            n = 3 * (it - 13) - 1 + s
            tile = 512

            @pl.when((n >= 0) & (n < width // tile))
            def _():
                cols = pl.ds(pl.multiple_of(n * tile, tile), tile)
                u = rows[0, :, :, cols].reshape(-1, tile)
                dy = rows[1, :, :, cols].reshape(-1, tile)
                ggu[0, :, cols] = tn(da[...], u).astype(BF16)
                ggu[1, :, cols] = tn(db[...], u).astype(BF16)
                gd[:, cols] = tn(hd[...], dy).astype(BF16)

    out_copies = [
        pltpu.make_async_copy(ggu, ggu_hbm, out_sem.at[0]),
        pltpu.make_async_copy(gd, gd_hbm, out_sem.at[1]),
    ]
    for copy in out_copies:
        copy.start()

    for step in range(NY):
        if step > 0:
            entry(expert, step, partner).wait_send()
        entry(expert, NY + step, partner).wait_send()
    for copy in early:
        copy.wait()

    @pl.loop(0, 6)
    def _(hop):
        from_left = z_of(-hop)
        from_right = z_of(hop)

        @pl.loop(0, NY)
        def _(j):
            @pl.when((hop <= pos + 2) & (pos < last))
            def _():
                forward(from_left * NY + j, right_sem, right).wait_send()

            @pl.when((hop <= 5 - pos) & (pos > 0))
            def _():
                forward(from_right * NY + j, left_sem, left).wait_send()

            @pl.when((hop >= 1) & (hop <= pos + 2) & (pos > 0))
            def _():
                idx = from_left * NY + j
                chain_out(idx, idx, left).wait_send()

            @pl.when((hop >= 1) & (hop <= 5 - pos) & (pos < last))
            def _():
                idx = from_right * NY + j
                chain_out(idx, idx, right).wait_send()

            @pl.when((hop == 0) | ((hop <= 2) & at_end))
            def _():
                for cc in range(2):
                    final_out(hop * NY + j, cc, j, z).wait_send()

    @pl.loop(0, slots)
    def _(idx):
        share(idx).wait_send()

    @pl.loop(0, NZ)
    def _(src_z):
        swap_copy(src_z).wait_send()

    for e in range(NY * 2):
        for cc in range(2):
            pltpu.make_async_copy(
                final.at[0, pl.ds(0, CAP)],
                back_ref.at[e, :, pl.ds(cc * outw, outw)],
                back_recv.at[2 * e + cc],
            ).wait()
    for copy in out_copies:
        copy.wait()


def experts(mine, wgu, wd, hidden, grad, gain, place):
    width = mine.shape[2]
    units = wd.shape[0]
    outw = width // 2 + 128
    slots = NY * NZ
    dma = pltpu.SemaphoreType.DMA
    hbm = pl.BlockSpec(memory_space=pl.ANY)
    vmem = pl.BlockSpec(memory_space=pltpu.VMEM)
    like = lambda array: jax.ShapeDtypeStruct(array.shape, array.dtype)
    return pl.pallas_call(
        expert_kernel,
        out_shape=(
            jax.ShapeDtypeStruct((NY * 2, CAP, 2 * outw), BF16),
            like(wgu),
            like(wd),
            like(hidden),
            like(grad),
            like(gain),
            like(place),
        ),
        in_specs=[vmem] + [hbm] * 6,
        out_specs=[vmem] + [hbm] * 6,
        scratch_shapes=[
            pltpu.VMEM((2, slots, 16, width), BF16),
            pltpu.VMEM(wgu.shape, BF16),
            pltpu.VMEM(wd.shape, BF16),
            pltpu.VMEM((slots, 16, 2 * outw), BF16),
            pltpu.VMEM((slots, 16, outw), BF16),
            pltpu.VMEM((slots + NY, 16, outw), BF16),
            pltpu.VMEM((slots, 16, outw), BF16),
            pltpu.VMEM((3 * NY, 16, outw), BF16),
            pltpu.VMEM((16, outw), F32),
            pltpu.VMEM((slots * 16, units), BF16),
            pltpu.VMEM((slots * 16, units), BF16),
            pltpu.VMEM((slots * 16, units), BF16),
            pltpu.VMEM(wgu.shape, BF16),
            pltpu.VMEM(wd.shape, BF16),
            dma((slots,)),
            dma((slots,)),
            dma((slots,)),
            dma((slots,)),
            dma((slots,)),
            dma((2 * NY,)),
            dma((NZ,)),
            dma((NZ,)),
            dma((slots,)),
            dma((slots + NY,)),
            dma((6 * NY,)),
            dma((4 * NY,)),
            dma((2,)),
            dma((2,)),
            dma((4,)),
            dma((4,)),
        ],
        compiler_params=pltpu.CompilerParams(
            collective_id=0, has_side_effects=True, vmem_limit_bytes=60 * 1024 * 1024
        ),
    )(mine, wgu, wd, hidden, grad, gain, place)


def on_device(hidden_in, out_grad, expert_ids, route_weight, norm_gain, w_gate_up, w_down):
    tokens_in = hidden_in[0]
    grad_out = out_grad[0]
    chosen = expert_ids[0]
    weights_in = route_weight[0]
    gain_row = norm_gain[0]
    devices = lax.axis_size("expert")
    span = devices // SPLIT
    width = tokens_in.shape[1]
    core = lax.rem(lax.axis_index("expert"), 2)
    pairs = [(i, i ^ 1) for i in range(devices)]

    tokens_f = tokens_in.astype(F32)
    rms_value = jnp.sqrt(jnp.mean(tokens_f * tokens_f, axis=-1, keepdims=True) + 1e-06)
    normed = tokens_f / rms_value
    normed_in = (normed * gain_row).astype(BF16)
    expert_range = jnp.arange(span, dtype=jnp.int32)
    picked = chosen[:, :, None] == expert_range[None, None, :]
    member = jnp.any(picked, axis=1).astype(jnp.int32)
    weight_te = jnp.sum(jnp.where(picked, weights_in.astype(F32)[:, :, None], 0.0), axis=1)
    position = jnp.cumsum(member, axis=0) - member
    slot_range = jnp.arange(CAP, dtype=jnp.int32)
    placing = (position.T[:, None, :] == slot_range[None, :, None]) & (member.T[:, None, :] == 1)
    place_f = placing.astype(F32)
    place_bf = placing.astype(BF16)
    place_w = (place_f * weight_te.T[:, None, :]).astype(BF16)
    sent_in = jnp.einsum("wst,td->wsd", place_bf, normed_in, preferred_element_type=F32).astype(BF16)
    sent_grad = jnp.einsum("wst,td->wsd", place_w, grad_out, preferred_element_type=F32).astype(BF16)
    keep = jnp.where(core == 0, sent_in, sent_grad)
    give = jnp.where(core == 0, sent_grad, sent_in)
    got = lax.ppermute(give, "expert", pairs)
    first = jnp.where(core == 0, keep, got)
    second = jnp.where(core == 0, got, keep)
    mine = jnp.concatenate([first, second], axis=1)

    back, grad_gate_up, grad_down, hidden_next, grad_next, gain_next, place_next = experts(
        mine,
        w_gate_up[0, 0],
        w_down[0, 0],
        tokens_in,
        grad_out,
        gain_row.reshape(-1, 128),
        place_bf.reshape(span * CAP, -1),
    )

    stages = lax.axis_size("pipe")
    comb_rows = lax.ppermute(
        back[:, :, 0].astype(F32), "pipe", [(i, (i + 1) % stages) for i in range(stages)]
    )
    summed_in = back[:, :, 128 : width + 128].reshape(span * CAP, width)
    grad_normed = lax.dot_general(
        place_next, summed_in, (((0,), (0,)), ((), ())), preferred_element_type=F32
    )
    next_f = hidden_next.astype(F32)
    next_rms = jnp.sqrt(jnp.mean(next_f * next_f, axis=-1, keepdims=True) + 1e-06)
    next_normed = next_f / next_rms
    scaled = grad_normed * gain_next.reshape(width)
    inner_mean = jnp.mean(scaled * next_normed, axis=-1, keepdims=True)
    handed = (
        grad_next.astype(F32) + (scaled - next_normed * inner_mean) / next_rms
    ).astype(BF16)

    comb_te = jnp.sum(place_f * comb_rows[:, :, None], axis=1)
    comb_te = comb_te / jnp.where(member.T == 1, weight_te.T, 1.0)
    grad_combine = jnp.sum(jnp.where(picked, comb_te.T[:, None, :], 0.0), axis=-1)
    return (
        handed[None],
        grad_gate_up[None, None],
        grad_down[None, None],
        grad_combine[None],
    )


def solution(mesh):
    return jax.shard_map(
        on_device,
        mesh=mesh,
        in_specs=(
            P("pipe", "expert", None),
            P("pipe", "expert", None),
            P("pipe", "expert", None),
            P("pipe", "expert", None),
            P("pipe", None),
            P("pipe", "expert", None, None, None),
            P("pipe", "expert", None, None),
        ),
        out_specs=(
            P("pipe", "expert", None),
            P("pipe", "expert", None, None, None),
            P("pipe", "expert", None, None),
            P("pipe", "expert", None),
        ),
        check_vma=False,
    )
```

```python
import jax
import jax.numpy as jnp
from jax import lax
from jax.experimental import pallas as pl
from jax.experimental.pallas import tpu as pltpu
from jax.sharding import PartitionSpec as P

SPLIT = 8
CAP = 8
NY = 4
NZ = 8
LINE = 4
MESH = pl.DeviceIdType.MESH
F32 = jnp.float32
BF16 = jnp.bfloat16


def nt(left, right):
    return lax.dot_general(left, right, (((1,), (1,)), ((), ())), preferred_element_type=F32)


def nn(left, right):
    return lax.dot_general(left, right, (((1,), (0,)), ((), ())), preferred_element_type=F32)


def tn(left, right):
    return lax.dot_general(left, right, (((0,), (0,)), ((), ())), preferred_element_type=F32)


def expert_kernel(
    mine_ref,
    wgu_hbm,
    wd_hbm,
    hidden_ref,
    grad_ref,
    gain_ref,
    place_ref,
    back_ref,
    ggu_hbm,
    gd_hbm,
    hidden_next,
    grad_next,
    gain_next,
    place_next,
    rows,
    wgu,
    wd,
    part,
    swap,
    chain,
    summed,
    final,
    acc,
    da,
    db,
    hd,
    ggu,
    gd,
    row_sem,
    pair_sem,
    right_sem,
    left_sem,
    share_sem,
    entry_sem,
    swap_send,
    swap_recv,
    chain_send,
    chain_recv,
    final_send,
    back_recv,
    w_sem,
    out_sem,
    early_send,
    early_recv,
):
    me = lax.axis_index("expert")
    stage = lax.axis_index("pipe")
    stages = lax.axis_size("pipe")
    before = lax.rem(stage + stages - 1, stages)
    after = lax.rem(stage + 1, stages)
    core = lax.rem(me, 2)
    z = lax.rem(me // 2, NZ)
    y = me // (2 * NZ)
    half = z // LINE
    pos = lax.rem(z, LINE)
    expert = y * 2 + half
    width = mine_ref.shape[2]
    halfw = width // 2
    outw = halfw + 128
    slots = NY * NZ
    last = LINE - 1
    at_end = (pos == 0) | (pos == last)

    def at(yy, zz, cc):
        return (yy * NZ + zz) * 2 + cc

    partner = at(y, z, 1 - core)
    right = at(y, lax.rem(z + 1, NZ), core)
    left = at(y, lax.rem(z + NZ - 1, NZ), core)
    entry_z = jnp.where(pos >= 2, lax.rem(LINE * (half + 1), NZ), lax.rem(LINE * half + NZ - 1, NZ))

    barrier = pltpu.get_barrier_semaphore()

    def greet(pipe, other):
        pl.semaphore_signal(
            barrier, inc=1, device_id={"pipe": pipe, "expert": other}, device_id_type=MESH
        )

    greet(stage, partner)
    for step in range(1, NY):
        greet(stage, at(lax.rem(y + step, NY), z, core))

    @pl.when(pos > 0)
    def _():
        greet(stage, left)

    @pl.when(pos < last)
    def _():
        greet(stage, right)

    @pl.when(at_end)
    def _():
        way = jnp.where(pos == 0, NZ - 1, 1)
        for hop in (1, 2):
            for yy in range(NY):
                greet(stage, at(yy, lax.rem(z + hop * way, NZ), core))

    for cc in range(2):
        for yy in range(NY):
            greet(after, at(yy, z, cc))
            greet(after, at(yy, entry_z, cc))

    w_copies = [
        pltpu.make_async_copy(wgu_hbm, wgu, w_sem.at[0]),
        pltpu.make_async_copy(wd_hbm, wd, w_sem.at[1]),
    ]
    for copy in w_copies:
        copy.start()
    common = 1 + (NY - 1) + NY + 2 * NY
    pl.semaphore_wait(barrier, jnp.where(at_end, common + 1 + 4 * NY, common + 2))

    def remote(src, dst, send, recv, other, pipe=None):
        return pltpu.make_async_remote_copy(
            src_ref=src,
            dst_ref=dst,
            send_sem=send,
            recv_sem=recv,
            device_id={"pipe": stage if pipe is None else pipe, "expert": other},
            device_id_type=MESH,
        )

    slot = z * NY + y

    def entry(src_idx, sem_idx, other):
        return remote(
            mine_ref.at[src_idx], rows.at[core, slot], entry_sem.at[sem_idx], row_sem.at[slot], other
        )

    own_copy = pltpu.make_async_copy(mine_ref.at[expert], rows.at[core, slot], row_sem.at[slot])
    own_copy.start()
    for step in range(NY):
        yy = lax.rem(y + step, NY)
        if step > 0:
            entry(yy * 2 + half, step, at(yy, z, core)).start()

    def entry_far(step):
        yy = lax.rem(y + step, NY)
        return entry(yy * 2 + 1 - half, NY + step, at(yy, entry_z, core))

    @pl.when(jnp.logical_not(at_end))
    def _():
        for step in range(NY):
            entry_far(step).start()

    early = [
        remote(src, dst, early_send.at[i], early_recv.at[i], me, before)
        for i, (src, dst) in enumerate(
            (
                (hidden_ref, hidden_next),
                (grad_ref, grad_next),
                (gain_ref, gain_next),
                (place_ref, place_next),
            )
        )
    ]
    for copy in early:
        copy.start()

    def piece(idx):
        return rows.at[core, idx]

    def forward(idx, sems, other):
        return remote(piece(idx), piece(idx), sems.at[idx], row_sem.at[idx], other)

    def share(idx):
        return remote(piece(idx), piece(idx), share_sem.at[idx], pair_sem.at[idx], partner)

    def arrived(idx):
        pltpu.make_async_copy(mine_ref.at[0], piece(idx), row_sem.at[idx]).wait()

    def z_of(offset):
        return lax.rem(z + offset + NZ, NZ)

    my_half = pl.multiple_of(core * outw, 128)
    their_half = pl.multiple_of((1 - core) * outw, 128)
    block = NY * 16

    def swap_copy(src_z):
        span = pl.ds(src_z * NY, NY)
        return remote(
            part.at[span, :, pl.ds(their_half, outw)],
            swap.at[span],
            swap_send.at[src_z],
            swap_recv.at[src_z],
            partner,
        )

    def compute(src_z):
        @pl.loop(0, NY)
        def _(j):
            idx = src_z * NY + j
            pltpu.make_async_copy(
                mine_ref.at[0], rows.at[1 - core, idx], pair_sem.at[idx]
            ).wait()

        span = pl.ds(src_z * NY, NY)
        u = rows[0, span].reshape(block, width)
        dy = rows[1, span].reshape(block, width)
        a = nt(u, wgu[0])
        b = nt(u, wgu[1])
        g = nt(dy, wd[...])
        sig = jax.nn.sigmoid(a)
        act = a * sig
        hdn = act * b
        dga = (g * b * sig * (1.0 + a * (1.0 - sig))).astype(BF16)
        dgb = (g * act).astype(BF16)
        where = pl.ds(pl.multiple_of(src_z * block, block), block)
        da[where] = dga
        db[where] = dgb
        hd[where] = hdn.astype(BF16)
        dc = jnp.sum(hdn * g, axis=1, keepdims=True)
        dc = jnp.broadcast_to(dc.astype(BF16), (block, 128)).reshape(NY, 16, 128)
        part[span, :, :128] = dc
        part[span, :, width + 128 :] = dc
        tile = 512
        for n in range(width // tile):
            du = nn(dga, wgu[0, :, n * tile : (n + 1) * tile]) + nn(
                dgb, wgu[1, :, n * tile : (n + 1) * tile]
            )
            part[span, :, 128 + n * tile : 128 + (n + 1) * tile] = du.astype(BF16).reshape(
                NY, 16, tile
            )
        swap_copy(src_z).start()

    def chain_in(idx):
        pltpu.make_async_copy(summed.at[0], chain.at[idx], chain_recv.at[idx]).wait()
        acc[...] += chain[idx].astype(F32)

    def chain_out(idx, dst, other):
        return remote(summed.at[idx], chain.at[dst], chain_send.at[idx], chain_recv.at[dst], other)

    def final_out(number, cc, src_y, src_z):
        return remote(
            final.at[number, pl.ds(cc * CAP, CAP)],
            back_ref.at[expert, :, pl.ds(my_half, outw)],
            final_send.at[2 * number + cc],
            back_recv.at[2 * expert + core],
            at(src_y, src_z, cc),
            before,
        )

    def finish(number, src_y, src_z):
        final[number] = acc[...].astype(BF16)
        for cc in range(2):
            final_out(number, cc, src_y, src_z).start()

    def combine(src_z, hop, kind):
        swap_copy(src_z).wait_recv()

        @pl.loop(0, NY)
        def _(j):
            idx = src_z * NY + j
            acc[...] = part[idx, :, pl.ds(my_half, outw)].astype(F32) + swap[idx].astype(F32)
            if kind == 0:

                @pl.when(pos < last)
                def _():
                    chain_in(idx)

                @pl.when(pos > 0)
                def _():
                    chain_in(slots + j)

                finish(j, j, src_z)
            elif kind < 0:

                @pl.when(pos < last)
                def _():
                    chain_in(idx)

                @pl.when(pos > 0)
                def _():
                    summed[idx] = acc[...].astype(BF16)
                    chain_out(idx, idx, left).start()

                @pl.when(pos == 0)
                def _():
                    finish(hop * NY + j, j, src_z)
            else:

                @pl.when(pos > 0)
                def _():
                    chain_in(idx)

                @pl.when(pos < last)
                def _():
                    summed[idx] = acc[...].astype(BF16)
                    chain_out(idx, jnp.where(hop == 1, slots + j, idx), right).start()

                @pl.when(pos == last)
                def _():
                    finish(hop * NY + j, j, src_z)

    def pick(values, index, default=0):
        out = default
        for i, value in enumerate(values):
            out = jnp.where(index == i, value, out)
        return out

    def list_at(place, slot):
        code = pick((0o12, 0o231, 0o3421, 0o145320), place)
        return lax.rem(code // pick((1, 8, 64, 512, 4096, 32768), slot, 8**6), 8)

    def origin(slot):
        return pick((9, 1, 0, -2, -1, 2), slot)

    flip = last - pos

    def own_idx(j):
        return z * NY + lax.rem(y + NY - j, NY)

    @pl.loop(0, 16)
    def _(it):
        slot_now = it // 2
        part_now = lax.rem(it, 2)
        from_l = list_at(pos, slot_now)
        from_r = list_at(flip, slot_now)

        for jj in range(2):
            j = 2 * part_now + jj
            src_y = lax.rem(y + NY - j, NY)

            @pl.when(slot_now == 0)
            def _():
                idx = own_idx(j)
                arrived(idx)

                @pl.when(pos <= 1)
                def _():
                    forward(idx, right_sem, right).start()

                @pl.when(pos >= 2)
                def _():
                    forward(idx, left_sem, left).start()

                share(idx).start()

            @pl.when(from_l > 0)
            def _():
                idx = z_of(-from_l) * NY + src_y
                arrived(idx)

                @pl.when(pos < last)
                def _():
                    forward(idx, right_sem, right).start()

                share(idx).start()

            @pl.when(from_r > 0)
            def _():
                idx = z_of(from_r) * NY + src_y
                arrived(idx)

                @pl.when(pos > 0)
                def _():
                    forward(idx, left_sem, left).start()

                share(idx).start()

        @pl.when((it == 1) & at_end)
        def _():
            for step in range(NY):
                entry_far(step).start()

        @pl.when((it == 7) & (pos == 2))
        def _():
            for j in range(NY):
                forward(own_idx(j), right_sem, right).start()

        @pl.when((it == 7) & (pos == 1))
        def _():
            for j in range(NY):
                forward(own_idx(j), left_sem, left).start()

        @pl.when(it == 1)
        def _():
            for copy in w_copies:
                copy.wait()

        away = jnp.where(part_now == 0, -list_at(pos, slot_now - 1), list_at(flip, slot_now - 1))

        @pl.when((it == 1) | ((it >= 2) & (away != 0)))
        def _():
            compute(z_of(jnp.where(it == 1, 0, away)))

        since_l = it - 3 - flip
        slot_l = since_l // 2
        away_l = pos - origin(slot_l)

        @pl.when((since_l >= 2) & (lax.rem(since_l + 2, 2) == 0) & (slot_l <= 5) & (away_l >= 1))
        def _():
            combine(z_of(-away_l), away_l, -1)

        since_r = it - 4 - pos
        slot_r = since_r // 2
        away_r = flip - origin(slot_r)

        @pl.when((since_r >= 2) & (lax.rem(since_r + 2, 2) == 0) & (slot_r <= 5) & (away_r >= 1))
        def _():
            combine(z_of(away_r), away_r, 1)

        @pl.when(it == pick((10, 15, 14, 11), pos))
        def _():
            combine(z, 0, 0)

        @pl.loop(0, 3)
        def _(s):
            n = 3 * (it - 13) - 1 + s
            tile = 512

            @pl.when((n >= 0) & (n < width // tile))
            def _():
                cols = pl.ds(pl.multiple_of(n * tile, tile), tile)
                u = rows[0, :, :, cols].reshape(-1, tile)
                dy = rows[1, :, :, cols].reshape(-1, tile)
                ggu[0, :, cols] = tn(da[...], u).astype(BF16)
                ggu[1, :, cols] = tn(db[...], u).astype(BF16)
                gd[:, cols] = tn(hd[...], dy).astype(BF16)

    out_copies = [
        pltpu.make_async_copy(ggu, ggu_hbm, out_sem.at[0]),
        pltpu.make_async_copy(gd, gd_hbm, out_sem.at[1]),
    ]
    for copy in out_copies:
        copy.start()

    for step in range(NY):
        if step > 0:
            entry(expert, step, partner).wait_send()
        entry(expert, NY + step, partner).wait_send()
    for copy in early:
        copy.wait()

    @pl.loop(0, 6)
    def _(hop):
        from_left = z_of(-hop)
        from_right = z_of(hop)

        @pl.loop(0, NY)
        def _(j):
            @pl.when((hop <= pos + 2) & (pos < last))
            def _():
                forward(from_left * NY + j, right_sem, right).wait_send()

            @pl.when((hop <= 5 - pos) & (pos > 0))
            def _():
                forward(from_right * NY + j, left_sem, left).wait_send()

            @pl.when((hop >= 1) & (hop <= pos + 2) & (pos > 0))
            def _():
                idx = from_left * NY + j
                chain_out(idx, idx, left).wait_send()

            @pl.when((hop >= 1) & (hop <= 5 - pos) & (pos < last))
            def _():
                idx = from_right * NY + j
                chain_out(idx, idx, right).wait_send()

            @pl.when((hop == 0) | ((hop <= 2) & at_end))
            def _():
                for cc in range(2):
                    final_out(hop * NY + j, cc, j, z).wait_send()

    @pl.loop(0, slots)
    def _(idx):
        share(idx).wait_send()

    @pl.loop(0, NZ)
    def _(src_z):
        swap_copy(src_z).wait_send()

    for e in range(NY * 2):
        for cc in range(2):
            pltpu.make_async_copy(
                final.at[0, pl.ds(0, CAP)],
                back_ref.at[e, :, pl.ds(cc * outw, outw)],
                back_recv.at[2 * e + cc],
            ).wait()
    for copy in out_copies:
        copy.wait()


def experts(mine, wgu, wd, hidden, grad, gain, place):
    width = mine.shape[2]
    units = wd.shape[0]
    outw = width // 2 + 128
    slots = NY * NZ
    dma = pltpu.SemaphoreType.DMA
    hbm = pl.BlockSpec(memory_space=pl.ANY)
    vmem = pl.BlockSpec(memory_space=pltpu.VMEM)
    like = lambda array: jax.ShapeDtypeStruct(array.shape, array.dtype)
    return pl.pallas_call(
        expert_kernel,
        out_shape=(
            jax.ShapeDtypeStruct((NY * 2, CAP, 2 * outw), BF16),
            like(wgu),
            like(wd),
            like(hidden),
            like(grad),
            like(gain),
            like(place),
        ),
        in_specs=[vmem] + [hbm] * 6,
        out_specs=[vmem] + [hbm] * 6,
        scratch_shapes=[
            pltpu.VMEM((2, slots, 16, width), BF16),
            pltpu.VMEM(wgu.shape, BF16),
            pltpu.VMEM(wd.shape, BF16),
            pltpu.VMEM((slots, 16, 2 * outw), BF16),
            pltpu.VMEM((slots, 16, outw), BF16),
            pltpu.VMEM((slots + NY, 16, outw), BF16),
            pltpu.VMEM((slots, 16, outw), BF16),
            pltpu.VMEM((3 * NY, 16, outw), BF16),
            pltpu.VMEM((16, outw), F32),
            pltpu.VMEM((slots * 16, units), BF16),
            pltpu.VMEM((slots * 16, units), BF16),
            pltpu.VMEM((slots * 16, units), BF16),
            pltpu.VMEM(wgu.shape, BF16),
            pltpu.VMEM(wd.shape, BF16),
            dma((slots,)),
            dma((slots,)),
            dma((slots,)),
            dma((slots,)),
            dma((slots,)),
            dma((2 * NY,)),
            dma((NZ,)),
            dma((NZ,)),
            dma((slots,)),
            dma((slots + NY,)),
            dma((6 * NY,)),
            dma((4 * NY,)),
            dma((2,)),
            dma((2,)),
            dma((4,)),
            dma((4,)),
        ],
        compiler_params=pltpu.CompilerParams(
            collective_id=0, has_side_effects=True, vmem_limit_bytes=60 * 1024 * 1024
        ),
    )(mine, wgu, wd, hidden, grad, gain, place)


def on_device(hidden_in, out_grad, expert_ids, route_weight, norm_gain, w_gate_up, w_down):
    tokens_in = hidden_in[0]
    grad_out = out_grad[0]
    chosen = expert_ids[0]
    weights_in = route_weight[0]
    gain_row = norm_gain[0]
    devices = lax.axis_size("expert")
    span = devices // SPLIT
    width = tokens_in.shape[1]
    core = lax.rem(lax.axis_index("expert"), 2)
    pairs = [(i, i ^ 1) for i in range(devices)]

    tokens_f = tokens_in.astype(F32)
    rms_value = jnp.sqrt(jnp.mean(tokens_f * tokens_f, axis=-1, keepdims=True) + 1e-06)
    normed = tokens_f / rms_value
    normed_in = (normed * gain_row).astype(BF16)
    expert_range = jnp.arange(span, dtype=jnp.int32)
    picked = chosen[:, :, None] == expert_range[None, None, :]
    member = jnp.any(picked, axis=1).astype(jnp.int32)
    weight_te = jnp.sum(jnp.where(picked, weights_in.astype(F32)[:, :, None], 0.0), axis=1)
    position = jnp.cumsum(member, axis=0) - member
    slot_range = jnp.arange(CAP, dtype=jnp.int32)
    placing = (position.T[:, None, :] == slot_range[None, :, None]) & (member.T[:, None, :] == 1)
    place_f = placing.astype(F32)
    place_bf = placing.astype(BF16)
    place_w = (place_f * weight_te.T[:, None, :]).astype(BF16)
    sent_in = jnp.einsum("wst,td->wsd", place_bf, normed_in, preferred_element_type=F32).astype(BF16)
    sent_grad = jnp.einsum("wst,td->wsd", place_w, grad_out, preferred_element_type=F32).astype(BF16)
    keep = jnp.where(core == 0, sent_in, sent_grad)
    give = jnp.where(core == 0, sent_grad, sent_in)
    got = lax.ppermute(give, "expert", pairs)
    first = jnp.where(core == 0, keep, got)
    second = jnp.where(core == 0, got, keep)
    mine = jnp.concatenate([first, second], axis=1)

    back, grad_gate_up, grad_down, hidden_next, grad_next, gain_next, place_next = experts(
        mine,
        w_gate_up[0, 0],
        w_down[0, 0],
        tokens_in,
        grad_out,
        gain_row.reshape(-1, 128),
        place_bf.reshape(span * CAP, -1),
    )

    stages = lax.axis_size("pipe")
    comb_rows = lax.ppermute(
        back[:, :, 0].astype(F32), "pipe", [(i, (i + 1) % stages) for i in range(stages)]
    )
    summed_in = back[:, :, 128 : width + 128].reshape(span * CAP, width)
    grad_normed = lax.dot_general(
        place_next, summed_in, (((0,), (0,)), ((), ())), preferred_element_type=F32
    )
    next_f = hidden_next.astype(F32)
    next_rms = jnp.sqrt(jnp.mean(next_f * next_f, axis=-1, keepdims=True) + 1e-06)
    next_normed = next_f / next_rms
    scaled = grad_normed * gain_next.reshape(width)
    inner_mean = jnp.mean(scaled * next_normed, axis=-1, keepdims=True)
    handed = (
        grad_next.astype(F32) + (scaled - next_normed * inner_mean) / next_rms
    ).astype(BF16)

    comb_te = jnp.sum(place_f * comb_rows[:, :, None], axis=1)
    comb_te = comb_te / jnp.where(member.T == 1, weight_te.T, 1.0)
    grad_combine = jnp.sum(jnp.where(picked, comb_te.T[:, None, :], 0.0), axis=-1)
    return (
        handed[None],
        grad_gate_up[None, None],
        grad_down[None, None],
        grad_combine[None],
    )


def solution(mesh):
    return jax.shard_map(
        on_device,
        mesh=mesh,
        in_specs=(
            P("pipe", "expert", None),
            P("pipe", "expert", None),
            P("pipe", "expert", None),
            P("pipe", "expert", None),
            P("pipe", None),
            P("pipe", "expert", None, None, None),
            P("pipe", "expert", None, None),
        ),
        out_specs=(
            P("pipe", "expert", None),
            P("pipe", "expert", None, None, None),
            P("pipe", "expert", None, None),
            P("pipe", "expert", None),
        ),
        check_vma=False,
    )
```

```python
import jax
import jax.numpy as jnp
from jax import lax
from jax.experimental import pallas as pl
from jax.experimental.pallas import tpu as pltpu
from jax.sharding import PartitionSpec as P

SPLIT = 8
CAP = 8
NY = 4
NZ = 8
LINE = 4
MESH = pl.DeviceIdType.MESH
F32 = jnp.float32
BF16 = jnp.bfloat16


def nt(left, right):
    return lax.dot_general(left, right, (((1,), (1,)), ((), ())), preferred_element_type=F32)


def nn(left, right):
    return lax.dot_general(left, right, (((1,), (0,)), ((), ())), preferred_element_type=F32)


def tn(left, right):
    return lax.dot_general(left, right, (((0,), (0,)), ((), ())), preferred_element_type=F32)


def expert_kernel(
    mine_ref,
    wgu_hbm,
    wd_hbm,
    hidden_ref,
    grad_ref,
    gain_ref,
    place_ref,
    back_ref,
    dc_ref,
    ggu_hbm,
    gd_hbm,
    hidden_next,
    grad_next,
    gain_next,
    place_next,
    rows,
    wgu,
    wd,
    part,
    swap,
    chain,
    summed,
    final,
    acc,
    da,
    db,
    hd,
    ggu,
    gd,
    row_sem,
    pair_sem,
    right_sem,
    left_sem,
    share_sem,
    entry_sem,
    swap_send,
    swap_recv,
    chain_send,
    chain_recv,
    final_send,
    back_recv,
    dc_send,
    dc_recv,
    w_sem,
    out_sem,
    early_send,
    early_recv,
):
    me = lax.axis_index("expert")
    stage = lax.axis_index("pipe")
    stages = lax.axis_size("pipe")
    before = lax.rem(stage + stages - 1, stages)
    after = lax.rem(stage + 1, stages)
    core = lax.rem(me, 2)
    z = lax.rem(me // 2, NZ)
    y = me // (2 * NZ)
    half = z // LINE
    pos = lax.rem(z, LINE)
    expert = y * 2 + half
    width = mine_ref.shape[2]
    halfw = width // 2
    outw = halfw + 128
    slots = NY * NZ
    last = LINE - 1
    at_end = (pos == 0) | (pos == last)

    def at(yy, zz, cc):
        return (yy * NZ + zz) * 2 + cc

    partner = at(y, z, 1 - core)
    right = at(y, lax.rem(z + 1, NZ), core)
    left = at(y, lax.rem(z + NZ - 1, NZ), core)
    entry_z = jnp.where(pos >= 2, lax.rem(LINE * (half + 1), NZ), lax.rem(LINE * half + NZ - 1, NZ))

    barrier = pltpu.get_barrier_semaphore()

    def greet(pipe, other):
        pl.semaphore_signal(
            barrier, inc=1, device_id={"pipe": pipe, "expert": other}, device_id_type=MESH
        )

    greet(stage, partner)
    for step in range(1, NY):
        greet(stage, at(lax.rem(y + step, NY), z, core))

    @pl.when(pos > 0)
    def _():
        greet(stage, left)

    @pl.when(pos < last)
    def _():
        greet(stage, right)

    @pl.when(at_end)
    def _():
        way = jnp.where(pos == 0, NZ - 1, 1)
        for hop in (1, 2):
            for yy in range(NY):
                greet(stage, at(yy, lax.rem(z + hop * way, NZ), core))

    for cc in range(2):
        for yy in range(NY):
            greet(after, at(yy, z, cc))
            greet(after, at(yy, entry_z, cc))
    for yy in range(NY):
        greet(stage, at(yy, entry_z, 0))

        @pl.when((yy != y) | (core != 0))
        def _():
            greet(stage, at(yy, z, 0))

    w_copies = [
        pltpu.make_async_copy(wgu_hbm, wgu, w_sem.at[0]),
        pltpu.make_async_copy(wd_hbm, wd, w_sem.at[1]),
    ]
    for copy in w_copies:
        copy.start()
    common = 1 + (NY - 1) + NY + 2 * NY + jnp.where(core == 0, 2 * NY - 1, 0)
    ends = 1 + 4 * NY + jnp.where(core == 0, 4 * NY, 0)
    pl.semaphore_wait(barrier, common + jnp.where(at_end, ends, 2))

    def remote(src, dst, send, recv, other, pipe=None):
        return pltpu.make_async_remote_copy(
            src_ref=src,
            dst_ref=dst,
            send_sem=send,
            recv_sem=recv,
            device_id={"pipe": stage if pipe is None else pipe, "expert": other},
            device_id_type=MESH,
        )

    slot = z * NY + y

    def entry(src_idx, sem_idx, other):
        return remote(
            mine_ref.at[src_idx], rows.at[core, slot], entry_sem.at[sem_idx], row_sem.at[slot], other
        )

    own_copy = pltpu.make_async_copy(mine_ref.at[expert], rows.at[core, slot], row_sem.at[slot])
    own_copy.start()
    for step in range(NY):
        yy = lax.rem(y + step, NY)
        if step > 0:
            entry(yy * 2 + half, step, at(yy, z, core)).start()

    def entry_far(step):
        yy = lax.rem(y + step, NY)
        return entry(yy * 2 + 1 - half, NY + step, at(yy, entry_z, core))

    @pl.when(jnp.logical_not(at_end))
    def _():
        for step in range(NY):
            entry_far(step).start()

    early = [
        remote(src, dst, early_send.at[i], early_recv.at[i], me, before)
        for i, (src, dst) in enumerate(
            (
                (hidden_ref, hidden_next),
                (grad_ref, grad_next),
                (gain_ref, gain_next),
                (place_ref, place_next),
            )
        )
    ]
    for copy in early:
        copy.start()

    def piece(idx):
        return rows.at[core, idx]

    def forward(idx, sems, other):
        return remote(piece(idx), piece(idx), sems.at[idx], row_sem.at[idx], other)

    def share(idx):
        return remote(piece(idx), piece(idx), share_sem.at[idx], pair_sem.at[idx], partner)

    def arrived(idx):
        pltpu.make_async_copy(mine_ref.at[0], piece(idx), row_sem.at[idx]).wait()

    def z_of(offset):
        return lax.rem(z + offset + NZ, NZ)

    my_half = pl.multiple_of(core * outw, 128)
    their_half = pl.multiple_of((1 - core) * outw, 128)
    block = NY * 16

    def swap_copy(src_z):
        span = pl.ds(src_z * NY, NY)
        return remote(
            part.at[span, :, pl.ds(their_half, outw)],
            swap.at[span],
            swap_send.at[src_z],
            swap_recv.at[src_z],
            partner,
        )

    def compute(src_z):
        @pl.loop(0, NY)
        def _(j):
            idx = src_z * NY + j
            pltpu.make_async_copy(
                mine_ref.at[0], rows.at[1 - core, idx], pair_sem.at[idx]
            ).wait()

        span = pl.ds(src_z * NY, NY)
        u = rows[0, span].reshape(block, width)
        dy = rows[1, span].reshape(block, width)
        a = nt(u, wgu[0])
        b = nt(u, wgu[1])
        g = nt(dy, wd[...])
        sig = jax.nn.sigmoid(a)
        act = a * sig
        hdn = act * b
        dga = (g * b * sig * (1.0 + a * (1.0 - sig))).astype(BF16)
        dgb = (g * act).astype(BF16)
        where = pl.ds(pl.multiple_of(src_z * block, block), block)
        da[where] = dga
        db[where] = dgb
        hd[where] = hdn.astype(BF16)
        dc = jnp.sum(hdn * g, axis=1, keepdims=True)
        dc = jnp.broadcast_to(dc.astype(BF16), (block, 128)).reshape(NY, 16, 128)
        part[span, :, :128] = dc
        part[span, :, width + 128 :] = dc
        tile = 512
        for turn in range(2):
            low = (1 - core if turn == 0 else core) * halfw
            for n in range(halfw // tile):
                cols = pl.ds(pl.multiple_of(low + n * tile, tile), tile)
                du = nn(dga, wgu[0, :, cols]) + nn(dgb, wgu[1, :, cols])
                part[span, :, pl.ds(pl.multiple_of(128 + low + n * tile, 128), tile)] = (
                    du.astype(BF16).reshape(NY, 16, tile)
                )
            if turn == 0:
                swap_copy(src_z).start()

    def chain_in(idx):
        pltpu.make_async_copy(summed.at[0], chain.at[idx], chain_recv.at[idx]).wait()
        acc[...] += chain[idx].astype(F32)

    def chain_out(idx, dst, other):
        return remote(summed.at[idx], chain.at[dst], chain_send.at[idx], chain_recv.at[dst], other)

    def final_out(number, cc, src_y, src_z):
        return remote(
            final.at[number, pl.ds(cc * CAP, CAP)],
            back_ref.at[expert, :, pl.ds(my_half, outw)],
            final_send.at[2 * number + cc],
            back_recv.at[2 * expert + core],
            at(src_y, src_z, cc),
            before,
        )

    def dc_out(number, cc, src_y, src_z):
        return remote(
            final.at[number, pl.ds(cc * CAP, CAP), pl.ds(0, 128)],
            dc_ref.at[expert],
            dc_send.at[2 * number + cc],
            dc_recv.at[expert],
            at(src_y, src_z, cc),
        )

    def dc_own(number):
        return pltpu.make_async_copy(
            final.at[number, pl.ds(0, CAP), pl.ds(0, 128)], dc_ref.at[expert], dc_recv.at[expert]
        )

    def finish(number, src_y, src_z):
        final[number] = acc[...].astype(BF16)
        for cc in range(2):
            final_out(number, cc, src_y, src_z).start()

        @pl.when(core == 0)
        def _():
            dc_out(number, 1, src_y, src_z).start()

            @pl.when((src_y == y) & (src_z == z))
            def _():
                dc_own(number).start()

            @pl.when((src_y != y) | (src_z != z))
            def _():
                dc_out(number, 0, src_y, src_z).start()

    def combine(src_z, hop, kind):
        swap_copy(src_z).wait_recv()

        @pl.loop(0, NY)
        def _(j):
            idx = src_z * NY + j
            acc[...] = part[idx, :, pl.ds(my_half, outw)].astype(F32) + swap[idx].astype(F32)
            if kind == 0:

                @pl.when(pos < last)
                def _():
                    chain_in(idx)

                @pl.when(pos > 0)
                def _():
                    chain_in(slots + j)

                finish(j, j, src_z)
            elif kind < 0:

                @pl.when(pos < last)
                def _():
                    chain_in(idx)

                @pl.when(pos > 0)
                def _():
                    summed[idx] = acc[...].astype(BF16)
                    chain_out(idx, idx, left).start()

                @pl.when(pos == 0)
                def _():
                    finish(hop * NY + j, j, src_z)
            else:

                @pl.when(pos > 0)
                def _():
                    chain_in(idx)

                @pl.when(pos < last)
                def _():
                    summed[idx] = acc[...].astype(BF16)
                    chain_out(idx, jnp.where(hop == 1, slots + j, idx), right).start()

                @pl.when(pos == last)
                def _():
                    finish(hop * NY + j, j, src_z)

    def pick(values, index, default=0):
        out = default
        for i, value in enumerate(values):
            out = jnp.where(index == i, value, out)
        return out

    def list_at(place, slot):
        code = pick((0o12, 0o231, 0o3421, 0o145320), place)
        return lax.rem(code // pick((1, 8, 64, 512, 4096, 32768), slot, 8**6), 8)

    def origin(slot):
        return pick((9, 1, 0, -2, -1, 2), slot)

    flip = last - pos

    def own_idx(j):
        return z * NY + lax.rem(y + NY - j, NY)

    @pl.loop(0, 15)
    def _(it):
        slot_now = it // 2
        part_now = lax.rem(it, 2)
        from_l = list_at(pos, slot_now)
        from_r = list_at(flip, slot_now)

        for jj in range(2):
            j = 2 * part_now + jj
            src_y = lax.rem(y + NY - j, NY)

            @pl.when(slot_now == 0)
            def _():
                idx = own_idx(j)
                arrived(idx)

                @pl.when(pos <= 1)
                def _():
                    forward(idx, right_sem, right).start()

                @pl.when(pos >= 2)
                def _():
                    forward(idx, left_sem, left).start()

                share(idx).start()

            @pl.when(from_l > 0)
            def _():
                idx = z_of(-from_l) * NY + src_y
                arrived(idx)

                @pl.when(pos < last)
                def _():
                    forward(idx, right_sem, right).start()

                share(idx).start()

            @pl.when(from_r > 0)
            def _():
                idx = z_of(from_r) * NY + src_y
                arrived(idx)

                @pl.when(pos > 0)
                def _():
                    forward(idx, left_sem, left).start()

                share(idx).start()

        @pl.when((it == 1) & at_end)
        def _():
            for step in range(NY):
                entry_far(step).start()

        @pl.when((it == 7) & (pos == 2))
        def _():
            for j in range(NY):
                forward(own_idx(j), right_sem, right).start()

        @pl.when((it == 7) & (pos == 1))
        def _():
            for j in range(NY):
                forward(own_idx(j), left_sem, left).start()

        @pl.when(it == 1)
        def _():
            for copy in w_copies:
                copy.wait()

        gone_l = list_at(pos, slot_now - 1)
        gone_r = list_at(flip, slot_now - 1)
        late = slot_now >= 4
        away = jnp.where(
            part_now == 0,
            jnp.where(late & (gone_r > 0), gone_r, -gone_l),
            jnp.where(late, 0, gone_r),
        )

        @pl.when((it == 1) | ((it >= 2) & (away != 0)))
        def _():
            compute(z_of(jnp.where(it == 1, 0, away)))

        since_l = it - 3 - flip
        slot_l = since_l // 2
        away_l = pos - origin(slot_l)

        @pl.when((since_l >= 2) & (lax.rem(since_l + 2, 2) == 0) & (slot_l <= 5) & (away_l >= 1))
        def _():
            combine(z_of(-away_l), away_l, -1)

        since_r = it - 3 - pos
        slot_r = (since_r + 16) // 2 - 8
        away_r = flip - origin(slot_r)
        odd_r = lax.rem(since_r + 16, 2)

        @pl.when(
            (slot_r >= jnp.where(odd_r == 1, 1, 3))
            & (slot_r <= jnp.where(odd_r == 1, 2, 5))
            & (away_r >= 1)
        )
        def _():
            combine(z_of(away_r), away_r, 1)

        @pl.when(it == pick((10, 14, 14, 11), pos))
        def _():
            combine(z, 0, 0)

        @pl.loop(0, 4)
        def _(s):
            n = 4 * (it - 13) + s
            tile = 512

            @pl.when((n >= 0) & (n < width // tile))
            def _():
                cols = pl.ds(pl.multiple_of(n * tile, tile), tile)
                u = rows[0, :, :, cols].reshape(-1, tile)
                dy = rows[1, :, :, cols].reshape(-1, tile)
                ggu[0, :, cols] = tn(da[...], u).astype(BF16)
                ggu[1, :, cols] = tn(db[...], u).astype(BF16)
                gd[:, cols] = tn(hd[...], dy).astype(BF16)

    out_copies = [
        pltpu.make_async_copy(ggu, ggu_hbm, out_sem.at[0]),
        pltpu.make_async_copy(gd, gd_hbm, out_sem.at[1]),
    ]
    for copy in out_copies:
        copy.start()

    for step in range(NY):
        if step > 0:
            entry(expert, step, partner).wait_send()
        entry(expert, NY + step, partner).wait_send()
    for copy in early:
        copy.wait()

    @pl.loop(0, 6)
    def _(hop):
        from_left = z_of(-hop)
        from_right = z_of(hop)

        @pl.loop(0, NY)
        def _(j):
            @pl.when((hop <= pos + 2) & (pos < last))
            def _():
                forward(from_left * NY + j, right_sem, right).wait_send()

            @pl.when((hop <= 5 - pos) & (pos > 0))
            def _():
                forward(from_right * NY + j, left_sem, left).wait_send()

            @pl.when((hop >= 1) & (hop <= pos + 2) & (pos > 0))
            def _():
                idx = from_left * NY + j
                chain_out(idx, idx, left).wait_send()

            @pl.when((hop >= 1) & (hop <= 5 - pos) & (pos < last))
            def _():
                idx = from_right * NY + j
                chain_out(idx, idx, right).wait_send()

            @pl.when((hop == 0) | ((hop <= 2) & at_end))
            def _():
                for cc in range(2):
                    final_out(hop * NY + j, cc, j, z).wait_send()

                @pl.when(core == 0)
                def _():
                    dc_out(hop * NY + j, 1, j, z).wait_send()

                    @pl.when((hop > 0) | (j != y))
                    def _():
                        dc_out(hop * NY + j, 0, j, z).wait_send()

    @pl.loop(0, slots)
    def _(idx):
        share(idx).wait_send()

    @pl.loop(0, NZ)
    def _(src_z):
        swap_copy(src_z).wait_send()

    for e in range(NY * 2):
        for cc in range(2):
            pltpu.make_async_copy(
                final.at[0, pl.ds(0, CAP)],
                back_ref.at[e, :, pl.ds(cc * outw, outw)],
                back_recv.at[2 * e + cc],
            ).wait()
        pltpu.make_async_copy(
            final.at[0, pl.ds(0, CAP), pl.ds(0, 128)], dc_ref.at[e], dc_recv.at[e]
        ).wait()
    for copy in out_copies:
        copy.wait()


def experts(mine, wgu, wd, hidden, grad, gain, place):
    width = mine.shape[2]
    units = wd.shape[0]
    outw = width // 2 + 128
    slots = NY * NZ
    dma = pltpu.SemaphoreType.DMA
    hbm = pl.BlockSpec(memory_space=pl.ANY)
    vmem = pl.BlockSpec(memory_space=pltpu.VMEM)
    like = lambda array: jax.ShapeDtypeStruct(array.shape, array.dtype)
    return pl.pallas_call(
        expert_kernel,
        out_shape=(
            jax.ShapeDtypeStruct((NY * 2, CAP, 2 * outw), BF16),
            jax.ShapeDtypeStruct((NY * 2, CAP, 128), BF16),
            like(wgu),
            like(wd),
            like(hidden),
            like(grad),
            like(gain),
            like(place),
        ),
        in_specs=[vmem] + [hbm] * 6,
        out_specs=[vmem, vmem] + [hbm] * 6,
        scratch_shapes=[
            pltpu.VMEM((2, slots, 16, width), BF16),
            pltpu.VMEM(wgu.shape, BF16),
            pltpu.VMEM(wd.shape, BF16),
            pltpu.VMEM((slots, 16, 2 * outw), BF16),
            pltpu.VMEM((slots, 16, outw), BF16),
            pltpu.VMEM((slots + NY, 16, outw), BF16),
            pltpu.VMEM((slots, 16, outw), BF16),
            pltpu.VMEM((3 * NY, 16, outw), BF16),
            pltpu.VMEM((16, outw), F32),
            pltpu.VMEM((slots * 16, units), BF16),
            pltpu.VMEM((slots * 16, units), BF16),
            pltpu.VMEM((slots * 16, units), BF16),
            pltpu.VMEM(wgu.shape, BF16),
            pltpu.VMEM(wd.shape, BF16),
            dma((slots,)),
            dma((slots,)),
            dma((slots,)),
            dma((slots,)),
            dma((slots,)),
            dma((2 * NY,)),
            dma((NZ,)),
            dma((NZ,)),
            dma((slots,)),
            dma((slots + NY,)),
            dma((6 * NY,)),
            dma((4 * NY,)),
            dma((6 * NY,)),
            dma((2 * NY,)),
            dma((2,)),
            dma((2,)),
            dma((4,)),
            dma((4,)),
        ],
        compiler_params=pltpu.CompilerParams(
            collective_id=0, has_side_effects=True, vmem_limit_bytes=60 * 1024 * 1024
        ),
    )(mine, wgu, wd, hidden, grad, gain, place)


def finish_kernel(
    back_hbm,
    hidden_hbm,
    grad_hbm,
    place_ref,
    gain_ref,
    ggu_hbm,
    gd_hbm,
    handed_hbm,
    ggu_out,
    gd_out,
    back,
    hidden,
    grad,
    handed,
    ggu,
    gd,
    scaled,
    in_sem,
    out_sem,
):
    width = hidden.shape[1]
    count = hidden.shape[0]
    ins = [
        pltpu.make_async_copy(src, dst, in_sem.at[i])
        for i, (src, dst) in enumerate(
            (
                (hidden_hbm, hidden),
                (back_hbm, back),
                (grad_hbm, grad),
                (ggu_hbm, ggu),
                (gd_hbm, gd),
            )
        )
    ]
    for copy in ins:
        copy.start()
    ins[0].wait()
    tile = 512
    square = jnp.zeros((count, 128), F32)
    for n in range(width // 128):
        h = hidden[:, n * 128 : (n + 1) * 128].astype(F32)
        square = square + h * h
    rms = jnp.sqrt(jnp.sum(square, axis=1, keepdims=True) / width + 1e-06)
    ins[1].wait()
    place = place_ref[...]
    along = jnp.zeros((count, 1), F32)
    for n in range(width // tile):
        cols = slice(n * tile, (n + 1) * tile)
        rows = back[:, :, 128 + n * tile : 128 + (n + 1) * tile].reshape(-1, tile)
        part = tn(place, rows) * gain_ref[:, cols]
        scaled[:, cols] = part
        along = along + jnp.sum(part * (hidden[:, cols].astype(F32) / rms), axis=1, keepdims=True)
    inner = along / width
    for i in (3, 4):
        ins[i].wait()
    outs = [
        pltpu.make_async_copy(ggu, ggu_out, out_sem.at[0]),
        pltpu.make_async_copy(gd, gd_out, out_sem.at[1]),
        pltpu.make_async_copy(handed, handed_hbm, out_sem.at[2]),
    ]
    outs[0].start()
    outs[1].start()
    ins[2].wait()
    for n in range(width // tile):
        cols = slice(n * tile, (n + 1) * tile)
        normed = hidden[:, cols].astype(F32) / rms
        handed[:, cols] = (
            grad[:, cols].astype(F32) + (scaled[:, cols] - normed * inner) / rms
        ).astype(BF16)
    outs[2].start()
    for copy in outs:
        copy.wait()


def finish(back, hidden, grad, place, gain, ggu, gd):
    like = lambda array: jax.ShapeDtypeStruct(array.shape, array.dtype)
    hbm = pl.BlockSpec(memory_space=pl.ANY)
    vmem = pl.BlockSpec(memory_space=pltpu.VMEM)
    room = lambda array: pltpu.VMEM(array.shape, array.dtype)
    return pl.pallas_call(
        finish_kernel,
        out_shape=(like(hidden), like(ggu), like(gd)),
        in_specs=[hbm, hbm, hbm, vmem, vmem, hbm, hbm],
        out_specs=[hbm, hbm, hbm],
        scratch_shapes=[
            room(back),
            room(hidden),
            room(grad),
            room(hidden),
            room(ggu),
            room(gd),
            pltpu.VMEM(hidden.shape, F32),
            pltpu.SemaphoreType.DMA((5,)),
            pltpu.SemaphoreType.DMA((3,)),
        ],
        compiler_params=pltpu.CompilerParams(vmem_limit_bytes=48 * 1024 * 1024),
    )(back, hidden, grad, place, gain, ggu, gd)


def on_device(hidden_in, out_grad, expert_ids, route_weight, norm_gain, w_gate_up, w_down):
    tokens_in = hidden_in[0]
    grad_out = out_grad[0]
    chosen = expert_ids[0]
    weights_in = route_weight[0]
    gain_row = norm_gain[0]
    devices = lax.axis_size("expert")
    span = devices // SPLIT
    width = tokens_in.shape[1]
    core = lax.rem(lax.axis_index("expert"), 2)
    pairs = [(i, i ^ 1) for i in range(devices)]

    tokens_f = tokens_in.astype(F32)
    rms_value = jnp.sqrt(jnp.mean(tokens_f * tokens_f, axis=-1, keepdims=True) + 1e-06)
    normed = tokens_f / rms_value
    normed_in = (normed * gain_row).astype(BF16)
    expert_range = jnp.arange(span, dtype=jnp.int32)
    picked = chosen[:, :, None] == expert_range[None, None, :]
    member = jnp.any(picked, axis=1).astype(jnp.int32)
    weight_te = jnp.sum(jnp.where(picked, weights_in.astype(F32)[:, :, None], 0.0), axis=1)
    position = jnp.cumsum(member, axis=0) - member
    slot_range = jnp.arange(CAP, dtype=jnp.int32)
    placing = (position.T[:, None, :] == slot_range[None, :, None]) & (member.T[:, None, :] == 1)
    place_f = placing.astype(F32)
    place_bf = placing.astype(BF16)
    place_w = (place_f * weight_te.T[:, None, :]).astype(BF16)
    sent_in = jnp.einsum("wst,td->wsd", place_bf, normed_in, preferred_element_type=F32).astype(BF16)
    sent_grad = jnp.einsum("wst,td->wsd", place_w, grad_out, preferred_element_type=F32).astype(BF16)
    keep = jnp.where(core == 0, sent_in, sent_grad)
    give = jnp.where(core == 0, sent_grad, sent_in)
    got = lax.ppermute(give, "expert", pairs)
    first = jnp.where(core == 0, keep, got)
    second = jnp.where(core == 0, got, keep)
    mine = jnp.concatenate([first, second], axis=1)

    back, dc_back, ggu, gd, hidden_next, grad_next, gain_next, place_next = experts(
        mine,
        w_gate_up[0, 0],
        w_down[0, 0],
        tokens_in,
        grad_out,
        gain_row.reshape(-1, 128),
        place_bf.reshape(span * CAP, -1),
    )

    handed, grad_gate_up, grad_down = finish(
        back, hidden_next, grad_next, place_next, gain_next.reshape(1, width), ggu, gd
    )

    comb_rows = dc_back[:, :, 0].astype(F32)
    comb_te = jnp.sum(place_f * comb_rows[:, :, None], axis=1)
    comb_te = comb_te / jnp.where(member.T == 1, weight_te.T, 1.0)
    grad_combine = jnp.sum(jnp.where(picked, comb_te.T[:, None, :], 0.0), axis=-1)
    return (
        handed[None],
        grad_gate_up[None, None],
        grad_down[None, None],
        grad_combine[None],
    )


def solution(mesh):
    return jax.shard_map(
        on_device,
        mesh=mesh,
        in_specs=(
            P("pipe", "expert", None),
            P("pipe", "expert", None),
            P("pipe", "expert", None),
            P("pipe", "expert", None),
            P("pipe", None),
            P("pipe", "expert", None, None, None),
            P("pipe", "expert", None, None),
        ),
        out_specs=(
            P("pipe", "expert", None),
            P("pipe", "expert", None, None, None),
            P("pipe", "expert", None, None),
            P("pipe", "expert", None),
        ),
        check_vma=False,
    )
```

```python
import jax
import jax.numpy as jnp
from jax import lax
from jax.experimental import pallas as pl
from jax.experimental.pallas import tpu as pltpu
from jax.sharding import PartitionSpec as P

SPLIT = 8
CAP = 8
NY = 4
NZ = 8
LINE = 4
MESH = pl.DeviceIdType.MESH
F32 = jnp.float32
BF16 = jnp.bfloat16


def nt(left, right):
    return lax.dot_general(left, right, (((1,), (1,)), ((), ())), preferred_element_type=F32)


def nn(left, right):
    return lax.dot_general(left, right, (((1,), (0,)), ((), ())), preferred_element_type=F32)


def tn(left, right):
    return lax.dot_general(left, right, (((0,), (0,)), ((), ())), preferred_element_type=F32)


def expert_kernel(
    mine_ref,
    wgu_hbm,
    wd_hbm,
    hidden_ref,
    grad_ref,
    gain_ref,
    place_ref,
    back_ref,
    dc_ref,
    ggu_hbm,
    gd_hbm,
    hidden_next,
    grad_next,
    gain_next,
    place_next,
    rows,
    wgu,
    wd,
    part,
    swap,
    chain,
    summed,
    final,
    acc,
    da,
    db,
    hd,
    ggu,
    gd,
    row_sem,
    pair_sem,
    right_sem,
    left_sem,
    share_sem,
    entry_sem,
    swap_send,
    swap_recv,
    chain_send,
    chain_recv,
    final_send,
    back_recv,
    dc_send,
    dc_recv,
    w_sem,
    out_sem,
    early_send,
    early_recv,
):
    me = lax.axis_index("expert")
    stage = lax.axis_index("pipe")
    stages = lax.axis_size("pipe")
    before = lax.rem(stage + stages - 1, stages)
    after = lax.rem(stage + 1, stages)
    core = lax.rem(me, 2)
    z = lax.rem(me // 2, NZ)
    y = me // (2 * NZ)
    half = z // LINE
    pos = lax.rem(z, LINE)
    expert = y * 2 + half
    width = mine_ref.shape[2]
    halfw = width // 2
    outw = halfw + 128
    slots = NY * NZ
    last = LINE - 1
    at_end = (pos == 0) | (pos == last)

    def at(yy, zz, cc):
        return (yy * NZ + zz) * 2 + cc

    partner = at(y, z, 1 - core)
    right = at(y, lax.rem(z + 1, NZ), core)
    left = at(y, lax.rem(z + NZ - 1, NZ), core)
    entry_z = jnp.where(pos >= 2, lax.rem(LINE * (half + 1), NZ), lax.rem(LINE * half + NZ - 1, NZ))

    barrier = pltpu.get_barrier_semaphore()

    def greet(pipe, other):
        pl.semaphore_signal(
            barrier, inc=1, device_id={"pipe": pipe, "expert": other}, device_id_type=MESH
        )

    greet(stage, partner)
    for step in range(1, NY):
        greet(stage, at(lax.rem(y + step, NY), z, core))

    @pl.when(pos > 0)
    def _():
        greet(stage, left)

    @pl.when(pos < last)
    def _():
        greet(stage, right)

    @pl.when(at_end)
    def _():
        way = jnp.where(pos == 0, NZ - 1, 1)
        for hop in (1, 2):
            for yy in range(NY):
                greet(stage, at(yy, lax.rem(z + hop * way, NZ), core))

    for cc in range(2):
        for yy in range(NY):
            greet(after, at(yy, z, cc))
            greet(after, at(yy, entry_z, cc))
    for yy in range(NY):
        greet(stage, at(yy, entry_z, 0))

        @pl.when((yy != y) | (core != 0))
        def _():
            greet(stage, at(yy, z, 0))

    w_copies = [
        pltpu.make_async_copy(wgu_hbm, wgu, w_sem.at[0]),
        pltpu.make_async_copy(wd_hbm, wd, w_sem.at[1]),
    ]
    for copy in w_copies:
        copy.start()
    common = 1 + (NY - 1) + NY + 2 * NY + jnp.where(core == 0, 2 * NY - 1, 0)
    ends = 1 + 4 * NY + jnp.where(core == 0, 4 * NY, 0)
    pl.semaphore_wait(barrier, common + jnp.where(at_end, ends, 2))

    def remote(src, dst, send, recv, other, pipe=None):
        return pltpu.make_async_remote_copy(
            src_ref=src,
            dst_ref=dst,
            send_sem=send,
            recv_sem=recv,
            device_id={"pipe": stage if pipe is None else pipe, "expert": other},
            device_id_type=MESH,
        )

    slot = z * NY + y

    def entry(src_idx, sem_idx, other):
        return remote(
            mine_ref.at[src_idx], rows.at[core, slot], entry_sem.at[sem_idx], row_sem.at[slot], other
        )

    own_copy = pltpu.make_async_copy(mine_ref.at[expert], rows.at[core, slot], row_sem.at[slot])
    own_copy.start()
    for step in range(NY):
        yy = lax.rem(y + step, NY)
        if step > 0:
            entry(yy * 2 + half, step, at(yy, z, core)).start()

    def entry_far(step):
        yy = lax.rem(y + step, NY)
        return entry(yy * 2 + 1 - half, NY + step, at(yy, entry_z, core))

    @pl.when(jnp.logical_not(at_end))
    def _():
        for step in range(NY):
            entry_far(step).start()

    early = [
        remote(src, dst, early_send.at[i], early_recv.at[i], me, before)
        for i, (src, dst) in enumerate(
            (
                (hidden_ref, hidden_next),
                (grad_ref, grad_next),
                (gain_ref, gain_next),
                (place_ref, place_next),
            )
        )
    ]
    for copy in early:
        copy.start()

    def piece(idx):
        return rows.at[core, idx]

    def forward(idx, sems, other):
        return remote(piece(idx), piece(idx), sems.at[idx], row_sem.at[idx], other)

    def share(idx):
        return remote(piece(idx), piece(idx), share_sem.at[idx], pair_sem.at[idx], partner)

    def arrived(idx):
        pltpu.make_async_copy(mine_ref.at[0], piece(idx), row_sem.at[idx]).wait()

    def z_of(offset):
        return lax.rem(z + offset + NZ, NZ)

    my_half = pl.multiple_of(core * outw, 128)
    their_half = pl.multiple_of((1 - core) * outw, 128)
    block = NY * 16

    def swap_copy(src_z):
        span = pl.ds(src_z * NY, NY)
        return remote(
            part.at[span, :, pl.ds(their_half, outw)],
            swap.at[span],
            swap_send.at[src_z],
            swap_recv.at[src_z],
            partner,
        )

    def compute(src_z):
        @pl.loop(0, NY)
        def _(j):
            idx = src_z * NY + j
            pltpu.make_async_copy(
                mine_ref.at[0], rows.at[1 - core, idx], pair_sem.at[idx]
            ).wait()

        span = pl.ds(src_z * NY, NY)
        u = rows[0, span].reshape(block, width)
        dy = rows[1, span].reshape(block, width)
        a = nt(u, wgu[0])
        b = nt(u, wgu[1])
        g = nt(dy, wd[...])
        sig = jax.nn.sigmoid(a)
        act = a * sig
        hdn = act * b
        dga = (g * b * sig * (1.0 + a * (1.0 - sig))).astype(BF16)
        dgb = (g * act).astype(BF16)
        where = pl.ds(pl.multiple_of(src_z * block, block), block)
        da[where] = dga
        db[where] = dgb
        hd[where] = hdn.astype(BF16)
        dc = jnp.sum(hdn * g, axis=1, keepdims=True)
        dc = jnp.broadcast_to(dc.astype(BF16), (block, 128)).reshape(NY, 16, 128)
        part[span, :, :128] = dc
        part[span, :, width + 128 :] = dc
        tile = 512
        for turn in range(2):
            low = (1 - core if turn == 0 else core) * halfw
            for n in range(halfw // tile):
                cols = pl.ds(pl.multiple_of(low + n * tile, tile), tile)
                du = nn(dga, wgu[0, :, cols]) + nn(dgb, wgu[1, :, cols])
                part[span, :, pl.ds(pl.multiple_of(128 + low + n * tile, 128), tile)] = (
                    du.astype(BF16).reshape(NY, 16, tile)
                )
            if turn == 0:
                swap_copy(src_z).start()

    def chain_in(idx):
        pltpu.make_async_copy(summed.at[0], chain.at[idx], chain_recv.at[idx]).wait()
        acc[...] += chain[idx].astype(F32)

    def chain_out(idx, dst, other):
        return remote(summed.at[idx], chain.at[dst], chain_send.at[idx], chain_recv.at[dst], other)

    def final_out(number, cc, src_y, src_z):
        return remote(
            final.at[number, pl.ds(cc * CAP, CAP)],
            back_ref.at[expert, :, pl.ds(my_half, outw)],
            final_send.at[2 * number + cc],
            back_recv.at[2 * expert + core],
            at(src_y, src_z, cc),
            before,
        )

    def dc_out(number, cc, src_y, src_z):
        return remote(
            final.at[number, pl.ds(cc * CAP, CAP), pl.ds(0, 128)],
            dc_ref.at[expert],
            dc_send.at[2 * number + cc],
            dc_recv.at[expert],
            at(src_y, src_z, cc),
        )

    def dc_own(number):
        return pltpu.make_async_copy(
            final.at[number, pl.ds(0, CAP), pl.ds(0, 128)], dc_ref.at[expert], dc_recv.at[expert]
        )

    def finish(number, src_y, src_z):
        final[number] = acc[...].astype(BF16)
        for cc in range(2):
            final_out(number, cc, src_y, src_z).start()

        @pl.when(core == 0)
        def _():
            dc_out(number, 1, src_y, src_z).start()

            @pl.when((src_y == y) & (src_z == z))
            def _():
                dc_own(number).start()

            @pl.when((src_y != y) | (src_z != z))
            def _():
                dc_out(number, 0, src_y, src_z).start()

    def combine(src_z, hop, kind):
        swap_copy(src_z).wait_recv()

        @pl.loop(0, NY)
        def _(j):
            idx = src_z * NY + j
            acc[...] = part[idx, :, pl.ds(my_half, outw)].astype(F32) + swap[idx].astype(F32)
            if kind == 0:

                @pl.when(pos < last)
                def _():
                    chain_in(idx)

                @pl.when(pos > 0)
                def _():
                    chain_in(slots + j)

                finish(j, j, src_z)
            elif kind < 0:

                @pl.when(pos < last)
                def _():
                    chain_in(idx)

                @pl.when(pos > 0)
                def _():
                    summed[idx] = acc[...].astype(BF16)
                    chain_out(idx, idx, left).start()

                @pl.when(pos == 0)
                def _():
                    finish(hop * NY + j, j, src_z)
            else:

                @pl.when(pos > 0)
                def _():
                    chain_in(idx)

                @pl.when(pos < last)
                def _():
                    summed[idx] = acc[...].astype(BF16)
                    chain_out(idx, jnp.where(hop == 1, slots + j, idx), right).start()

                @pl.when(pos == last)
                def _():
                    finish(hop * NY + j, j, src_z)

    def pick(values, index, default=0):
        out = default
        for i, value in enumerate(values):
            out = jnp.where(index == i, value, out)
        return out

    def list_at(place, slot):
        code = pick((0o12, 0o231, 0o3421, 0o145320), place)
        return lax.rem(code // pick((1, 8, 64, 512, 4096, 32768), slot, 8**6), 8)

    def origin(slot):
        return pick((9, 1, 0, -2, -1, 2), slot)

    flip = last - pos

    def own_idx(j):
        return z * NY + lax.rem(y + NY - j, NY)

    @pl.loop(0, 15)
    def _(it):
        slot_now = it // 2
        part_now = lax.rem(it, 2)
        from_l = list_at(pos, slot_now)
        from_r = list_at(flip, slot_now)

        for jj in range(2):
            j = 2 * part_now + jj
            src_y = lax.rem(y + NY - j, NY)

            @pl.when(slot_now == 0)
            def _():
                idx = own_idx(j)
                arrived(idx)

                @pl.when(pos <= 1)
                def _():
                    forward(idx, right_sem, right).start()

                @pl.when(pos >= 2)
                def _():
                    forward(idx, left_sem, left).start()

                share(idx).start()

            @pl.when(from_l > 0)
            def _():
                idx = z_of(-from_l) * NY + src_y
                arrived(idx)

                @pl.when(pos < last)
                def _():
                    forward(idx, right_sem, right).start()

                share(idx).start()

            @pl.when(from_r > 0)
            def _():
                idx = z_of(from_r) * NY + src_y
                arrived(idx)

                @pl.when(pos > 0)
                def _():
                    forward(idx, left_sem, left).start()

                share(idx).start()

        @pl.when((it == 1) & at_end)
        def _():
            for step in range(NY):
                entry_far(step).start()

        first = jnp.where(it == 1, 0, 3)
        until = jnp.where(it == 1, 3, NY)

        @pl.when(((it == 1) | (it == 7)) & (pos == 2))
        def _():
            @pl.loop(first, until)
            def _(j):
                forward(own_idx(j), right_sem, right).start()

        @pl.when(((it == 1) | (it == 7)) & (pos == 1))
        def _():
            @pl.loop(first, until)
            def _(j):
                forward(own_idx(j), left_sem, left).start()

        @pl.when(it == 1)
        def _():
            for copy in w_copies:
                copy.wait()

        gone_l = list_at(pos, slot_now - 1)
        gone_r = list_at(flip, slot_now - 1)
        late = slot_now >= 4
        away = jnp.where(
            part_now == 0,
            jnp.where(late & (gone_r > 0), gone_r, -gone_l),
            jnp.where(late, 0, gone_r),
        )

        @pl.when((it == 1) | ((it >= 2) & (away != 0)))
        def _():
            compute(z_of(jnp.where(it == 1, 0, away)))

        since_l = it - 3 - flip
        slot_l = since_l // 2
        away_l = pos - origin(slot_l)

        @pl.when((since_l >= 2) & (lax.rem(since_l + 2, 2) == 0) & (slot_l <= 5) & (away_l >= 1))
        def _():
            combine(z_of(-away_l), away_l, -1)

        since_r = it - 3 - pos
        slot_r = (since_r + 16) // 2 - 8
        away_r = flip - origin(slot_r)
        odd_r = lax.rem(since_r + 16, 2)

        @pl.when(
            (slot_r >= jnp.where(odd_r == 1, 1, 3))
            & (slot_r <= jnp.where(odd_r == 1, 2, 5))
            & (away_r >= 1)
        )
        def _():
            combine(z_of(away_r), away_r, 1)

        @pl.when(it == pick((10, 14, 14, 11), pos))
        def _():
            combine(z, 0, 0)

        @pl.loop(0, 4)
        def _(s):
            n = 4 * (it - 13) + s
            tile = 512

            @pl.when((n >= 0) & (n < width // tile))
            def _():
                cols = pl.ds(pl.multiple_of(n * tile, tile), tile)
                u = rows[0, :, :, cols].reshape(-1, tile)
                dy = rows[1, :, :, cols].reshape(-1, tile)
                ggu[0, :, cols] = tn(da[...], u).astype(BF16)
                ggu[1, :, cols] = tn(db[...], u).astype(BF16)
                gd[:, cols] = tn(hd[...], dy).astype(BF16)

    out_copies = [
        pltpu.make_async_copy(ggu, ggu_hbm, out_sem.at[0]),
        pltpu.make_async_copy(gd, gd_hbm, out_sem.at[1]),
    ]
    for copy in out_copies:
        copy.start()

    for step in range(NY):
        if step > 0:
            entry(expert, step, partner).wait_send()
        entry(expert, NY + step, partner).wait_send()
    for copy in early:
        copy.wait()

    @pl.loop(0, 6)
    def _(hop):
        from_left = z_of(-hop)
        from_right = z_of(hop)

        @pl.loop(0, NY)
        def _(j):
            @pl.when((hop <= pos + 2) & (pos < last))
            def _():
                forward(from_left * NY + j, right_sem, right).wait_send()

            @pl.when((hop <= 5 - pos) & (pos > 0))
            def _():
                forward(from_right * NY + j, left_sem, left).wait_send()

            @pl.when((hop >= 1) & (hop <= pos + 2) & (pos > 0))
            def _():
                idx = from_left * NY + j
                chain_out(idx, idx, left).wait_send()

            @pl.when((hop >= 1) & (hop <= 5 - pos) & (pos < last))
            def _():
                idx = from_right * NY + j
                chain_out(idx, idx, right).wait_send()

            @pl.when((hop == 0) | ((hop <= 2) & at_end))
            def _():
                for cc in range(2):
                    final_out(hop * NY + j, cc, j, z).wait_send()

                @pl.when(core == 0)
                def _():
                    dc_out(hop * NY + j, 1, j, z).wait_send()

                    @pl.when((hop > 0) | (j != y))
                    def _():
                        dc_out(hop * NY + j, 0, j, z).wait_send()

    @pl.loop(0, slots)
    def _(idx):
        share(idx).wait_send()

    @pl.loop(0, NZ)
    def _(src_z):
        swap_copy(src_z).wait_send()

    for e in range(NY * 2):
        for cc in range(2):
            pltpu.make_async_copy(
                final.at[0, pl.ds(0, CAP)],
                back_ref.at[e, :, pl.ds(cc * outw, outw)],
                back_recv.at[2 * e + cc],
            ).wait()
        pltpu.make_async_copy(
            final.at[0, pl.ds(0, CAP), pl.ds(0, 128)], dc_ref.at[e], dc_recv.at[e]
        ).wait()
    for copy in out_copies:
        copy.wait()


def experts(mine, wgu, wd, hidden, grad, gain, place):
    width = mine.shape[2]
    units = wd.shape[0]
    outw = width // 2 + 128
    slots = NY * NZ
    dma = pltpu.SemaphoreType.DMA
    hbm = pl.BlockSpec(memory_space=pl.ANY)
    vmem = pl.BlockSpec(memory_space=pltpu.VMEM)
    like = lambda array: jax.ShapeDtypeStruct(array.shape, array.dtype)
    return pl.pallas_call(
        expert_kernel,
        out_shape=(
            jax.ShapeDtypeStruct((NY * 2, CAP, 2 * outw), BF16),
            jax.ShapeDtypeStruct((NY * 2, CAP, 128), BF16),
            like(wgu),
            like(wd),
            like(hidden),
            like(grad),
            like(gain),
            like(place),
        ),
        in_specs=[vmem] + [hbm] * 6,
        out_specs=[vmem, vmem] + [hbm] * 6,
        scratch_shapes=[
            pltpu.VMEM((2, slots, 16, width), BF16),
            pltpu.VMEM(wgu.shape, BF16),
            pltpu.VMEM(wd.shape, BF16),
            pltpu.VMEM((slots, 16, 2 * outw), BF16),
            pltpu.VMEM((slots, 16, outw), BF16),
            pltpu.VMEM((slots + NY, 16, outw), BF16),
            pltpu.VMEM((slots, 16, outw), BF16),
            pltpu.VMEM((3 * NY, 16, outw), BF16),
            pltpu.VMEM((16, outw), F32),
            pltpu.VMEM((slots * 16, units), BF16),
            pltpu.VMEM((slots * 16, units), BF16),
            pltpu.VMEM((slots * 16, units), BF16),
            pltpu.VMEM(wgu.shape, BF16),
            pltpu.VMEM(wd.shape, BF16),
            dma((slots,)),
            dma((slots,)),
            dma((slots,)),
            dma((slots,)),
            dma((slots,)),
            dma((2 * NY,)),
            dma((NZ,)),
            dma((NZ,)),
            dma((slots,)),
            dma((slots + NY,)),
            dma((6 * NY,)),
            dma((4 * NY,)),
            dma((6 * NY,)),
            dma((2 * NY,)),
            dma((2,)),
            dma((2,)),
            dma((4,)),
            dma((4,)),
        ],
        compiler_params=pltpu.CompilerParams(
            collective_id=0, has_side_effects=True, vmem_limit_bytes=60 * 1024 * 1024
        ),
    )(mine, wgu, wd, hidden, grad, gain, place)


def finish_kernel(
    back_hbm,
    hidden_hbm,
    grad_hbm,
    place_ref,
    gain_ref,
    ggu_hbm,
    gd_hbm,
    handed_hbm,
    ggu_out,
    gd_out,
    back,
    hidden,
    grad,
    handed,
    ggu,
    gd,
    scaled,
    in_sem,
    out_sem,
):
    width = hidden.shape[1]
    count = hidden.shape[0]
    ins = [
        pltpu.make_async_copy(src, dst, in_sem.at[i])
        for i, (src, dst) in enumerate(
            (
                (hidden_hbm, hidden),
                (back_hbm, back),
                (grad_hbm, grad),
                (ggu_hbm, ggu),
                (gd_hbm, gd),
            )
        )
    ]
    for copy in ins:
        copy.start()
    ins[0].wait()
    tile = 512
    square = jnp.zeros((count, 128), F32)
    for n in range(width // 128):
        h = hidden[:, n * 128 : (n + 1) * 128].astype(F32)
        square = square + h * h
    rms = jnp.sqrt(jnp.sum(square, axis=1, keepdims=True) / width + 1e-06)
    ins[1].wait()
    place = place_ref[...]
    along = jnp.zeros((count, 1), F32)
    for n in range(width // tile):
        cols = slice(n * tile, (n + 1) * tile)
        rows = back[:, :, 128 + n * tile : 128 + (n + 1) * tile].reshape(-1, tile)
        part = tn(place, rows) * gain_ref[:, cols]
        scaled[:, cols] = part
        along = along + jnp.sum(part * (hidden[:, cols].astype(F32) / rms), axis=1, keepdims=True)
    inner = along / width
    for i in (3, 4):
        ins[i].wait()
    outs = [
        pltpu.make_async_copy(ggu, ggu_out, out_sem.at[0]),
        pltpu.make_async_copy(gd, gd_out, out_sem.at[1]),
        pltpu.make_async_copy(handed, handed_hbm, out_sem.at[2]),
    ]
    outs[0].start()
    outs[1].start()
    ins[2].wait()
    for n in range(width // tile):
        cols = slice(n * tile, (n + 1) * tile)
        normed = hidden[:, cols].astype(F32) / rms
        handed[:, cols] = (
            grad[:, cols].astype(F32) + (scaled[:, cols] - normed * inner) / rms
        ).astype(BF16)
    outs[2].start()
    for copy in outs:
        copy.wait()


def finish(back, hidden, grad, place, gain, ggu, gd):
    like = lambda array: jax.ShapeDtypeStruct(array.shape, array.dtype)
    hbm = pl.BlockSpec(memory_space=pl.ANY)
    vmem = pl.BlockSpec(memory_space=pltpu.VMEM)
    room = lambda array: pltpu.VMEM(array.shape, array.dtype)
    return pl.pallas_call(
        finish_kernel,
        out_shape=(like(hidden), like(ggu), like(gd)),
        in_specs=[hbm, hbm, hbm, vmem, vmem, hbm, hbm],
        out_specs=[hbm, hbm, hbm],
        scratch_shapes=[
            room(back),
            room(hidden),
            room(grad),
            room(hidden),
            room(ggu),
            room(gd),
            pltpu.VMEM(hidden.shape, F32),
            pltpu.SemaphoreType.DMA((5,)),
            pltpu.SemaphoreType.DMA((3,)),
        ],
        compiler_params=pltpu.CompilerParams(vmem_limit_bytes=63 * 1024 * 1024),
    )(back, hidden, grad, place, gain, ggu, gd)


def on_device(hidden_in, out_grad, expert_ids, route_weight, norm_gain, w_gate_up, w_down):
    tokens_in = hidden_in[0]
    grad_out = out_grad[0]
    chosen = expert_ids[0]
    weights_in = route_weight[0]
    gain_row = norm_gain[0]
    devices = lax.axis_size("expert")
    span = devices // SPLIT
    width = tokens_in.shape[1]
    core = lax.rem(lax.axis_index("expert"), 2)
    pairs = [(i, i ^ 1) for i in range(devices)]

    tokens_f = tokens_in.astype(F32)
    rms_value = jnp.sqrt(jnp.mean(tokens_f * tokens_f, axis=-1, keepdims=True) + 1e-06)
    normed = tokens_f / rms_value
    normed_in = (normed * gain_row).astype(BF16)
    expert_range = jnp.arange(span, dtype=jnp.int32)
    picked = chosen[:, :, None] == expert_range[None, None, :]
    member = jnp.any(picked, axis=1).astype(jnp.int32)
    weight_te = jnp.sum(jnp.where(picked, weights_in.astype(F32)[:, :, None], 0.0), axis=1)
    position = jnp.cumsum(member, axis=0) - member
    slot_range = jnp.arange(CAP, dtype=jnp.int32)
    placing = (position.T[:, None, :] == slot_range[None, :, None]) & (member.T[:, None, :] == 1)
    place_f = placing.astype(F32)
    place_bf = placing.astype(BF16)
    place_w = (place_f * weight_te.T[:, None, :]).astype(BF16)
    sent_in = jnp.einsum("wst,td->wsd", place_bf, normed_in, preferred_element_type=F32).astype(BF16)
    sent_grad = jnp.einsum("wst,td->wsd", place_w, grad_out, preferred_element_type=F32).astype(BF16)
    keep = jnp.where(core == 0, sent_in, sent_grad)
    give = jnp.where(core == 0, sent_grad, sent_in)
    got = lax.ppermute(give, "expert", pairs)
    first = jnp.where(core == 0, keep, got)
    second = jnp.where(core == 0, got, keep)
    mine = jnp.concatenate([first, second], axis=1)

    back, dc_back, ggu, gd, hidden_next, grad_next, gain_next, place_next = experts(
        mine,
        w_gate_up[0, 0],
        w_down[0, 0],
        tokens_in,
        grad_out,
        gain_row.reshape(-1, 128),
        place_bf.reshape(span * CAP, -1),
    )

    handed, grad_gate_up, grad_down = finish(
        back, hidden_next, grad_next, place_next, gain_next.reshape(1, width), ggu, gd
    )

    comb_rows = dc_back[:, :, 0].astype(F32)
    comb_te = jnp.sum(place_f * comb_rows[:, :, None], axis=1)
    comb_te = comb_te / jnp.where(member.T == 1, weight_te.T, 1.0)
    grad_combine = jnp.sum(jnp.where(picked, comb_te.T[:, None, :], 0.0), axis=-1)
    return (
        handed[None],
        grad_gate_up[None, None],
        grad_down[None, None],
        grad_combine[None],
    )


def solution(mesh):
    return jax.shard_map(
        on_device,
        mesh=mesh,
        in_specs=(
            P("pipe", "expert", None),
            P("pipe", "expert", None),
            P("pipe", "expert", None),
            P("pipe", "expert", None),
            P("pipe", None),
            P("pipe", "expert", None, None, None),
            P("pipe", "expert", None, None),
        ),
        out_specs=(
            P("pipe", "expert", None),
            P("pipe", "expert", None, None, None),
            P("pipe", "expert", None, None),
            P("pipe", "expert", None),
        ),
        check_vma=False,
    )
```

```python
import jax
import jax.numpy as jnp
from jax import lax
from jax.experimental import pallas as pl
from jax.experimental.pallas import tpu as pltpu
from jax.sharding import PartitionSpec as P

CAP = 8
NY = 4
NZ = 8
LINE = 4
MESH = pl.DeviceIdType.MESH
F32 = jnp.float32
BF16 = jnp.bfloat16


def nt(left, right):
    return lax.dot_general(left, right, (((1,), (1,)), ((), ())), preferred_element_type=F32)


def nn(left, right):
    return lax.dot_general(left, right, (((1,), (0,)), ((), ())), preferred_element_type=F32)


def tn(left, right):
    return lax.dot_general(left, right, (((0,), (0,)), ((), ())), preferred_element_type=F32)


def placing(ids, weights):
    count = ids.shape[1]
    span = NY * 2
    hits = [ids == e for e in range(span)]
    member = jnp.concatenate(
        [jnp.max(jnp.where(hit, 1.0, 0.0), axis=0, keepdims=True) for hit in hits], axis=0
    )
    above = lax.broadcasted_iota(jnp.int32, (count, count), 0) < lax.broadcasted_iota(
        jnp.int32, (count, count), 1
    )
    position = nn(member.astype(BF16), jnp.where(above, 1.0, 0.0).astype(BF16))
    row = lax.broadcasted_iota(jnp.int32, (CAP, count), 0).astype(F32)
    plain = []
    weighted = []
    for e in range(span):
        here = (row == position[e : e + 1]) & (member[e : e + 1] > 0.5)
        place = jnp.where(here, 1.0, 0.0)
        share = jnp.sum(jnp.where(hits[e], weights, 0.0), axis=0, keepdims=True)
        plain.append(place)
        weighted.append(place * share)
    return plain, weighted


def expert_kernel(
    ids_ref,
    weight_ref,
    gain_row,
    wgu_hbm,
    wd_hbm,
    hidden_ref,
    grad_ref,
    gain_ref,
    back_ref,
    dc_ref,
    ggu_hbm,
    gd_hbm,
    hidden_next,
    grad_next,
    gain_next,
    place_next,
    mine_ref,
    give,
    place_ref,
    tokens,
    token_grad,
    rows,
    wgu,
    wd,
    part,
    swap,
    chain,
    summed,
    final,
    acc,
    da,
    db,
    hd,
    ggu,
    gd,
    row_sem,
    pair_sem,
    right_sem,
    left_sem,
    share_sem,
    entry_sem,
    swap_send,
    swap_recv,
    chain_send,
    chain_recv,
    final_send,
    back_recv,
    dc_send,
    dc_recv,
    w_sem,
    out_sem,
    early_send,
    early_recv,
    pack_sem,
    give_send,
    give_recv,
):
    me = lax.axis_index("expert")
    stage = lax.axis_index("pipe")
    stages = lax.axis_size("pipe")
    before = lax.rem(stage + stages - 1, stages)
    after = lax.rem(stage + 1, stages)
    core = lax.rem(me, 2)
    z = lax.rem(me // 2, NZ)
    y = me // (2 * NZ)
    half = z // LINE
    pos = lax.rem(z, LINE)
    expert = y * 2 + half
    width = mine_ref.shape[2]
    halfw = width // 2
    outw = halfw + 128
    slots = NY * NZ
    last = LINE - 1
    at_end = (pos == 0) | (pos == last)

    def at(yy, zz, cc):
        return (yy * NZ + zz) * 2 + cc

    partner = at(y, z, 1 - core)
    right = at(y, lax.rem(z + 1, NZ), core)
    left = at(y, lax.rem(z + NZ - 1, NZ), core)
    entry_z = jnp.where(pos >= 2, lax.rem(LINE * (half + 1), NZ), lax.rem(LINE * half + NZ - 1, NZ))

    loads = [
        pltpu.make_async_copy(hidden_ref, tokens, pack_sem.at[0]),
        pltpu.make_async_copy(grad_ref, token_grad, pack_sem.at[1]),
    ]
    for copy in loads:
        copy.start()

    barrier = pltpu.get_barrier_semaphore()

    def greet(pipe, other):
        pl.semaphore_signal(
            barrier, inc=1, device_id={"pipe": pipe, "expert": other}, device_id_type=MESH
        )

    greet(stage, partner)
    for step in range(1, NY):
        greet(stage, at(lax.rem(y + step, NY), z, core))

    @pl.when(pos > 0)
    def _():
        greet(stage, left)

    @pl.when(pos < last)
    def _():
        greet(stage, right)

    @pl.when(at_end)
    def _():
        way = jnp.where(pos == 0, NZ - 1, 1)
        for hop in (1, 2):
            for yy in range(NY):
                greet(stage, at(yy, lax.rem(z + hop * way, NZ), core))

    for cc in range(2):
        for yy in range(NY):
            greet(after, at(yy, z, cc))
            greet(after, at(yy, entry_z, cc))
    for yy in range(NY):
        greet(stage, at(yy, entry_z, 0))

        @pl.when((yy != y) | (core != 0))
        def _():
            greet(stage, at(yy, z, 0))

    w_copies = [
        pltpu.make_async_copy(wgu_hbm, wgu, w_sem.at[0]),
        pltpu.make_async_copy(wd_hbm, wd, w_sem.at[1]),
    ]
    for copy in w_copies:
        copy.start()

    plain, weighted = placing(ids_ref[...], weight_ref[...].astype(F32))
    place = jnp.concatenate(plain, axis=0).astype(BF16)
    place_w = jnp.concatenate(weighted, axis=0).astype(BF16)
    place_ref[...] = place
    for copy in loads:
        copy.wait()
    count = tokens.shape[0]
    square = jnp.zeros((count, 128), F32)
    for n in range(width // 128):
        h = tokens[:, n * 128 : (n + 1) * 128].astype(F32)
        square = square + h * h
    rms = jnp.sqrt(jnp.sum(square, axis=1, keepdims=True) / width + 1e-06)
    for n in range(width // 512):
        cols = slice(n * 512, (n + 1) * 512)
        u = ((tokens[:, cols].astype(F32) / rms) * gain_row[:, cols]).astype(BF16)
        sent_in = nn(place, u).astype(BF16).reshape(NY * 2, CAP, 512)
        sent_grad = nn(place_w, token_grad[:, cols]).astype(BF16).reshape(NY * 2, CAP, 512)

        @pl.when(core == 0)
        def _():
            mine_ref[:, :CAP, cols] = sent_in
            give[:, :, cols] = sent_grad

        @pl.when(core == 1)
        def _():
            mine_ref[:, CAP:, cols] = sent_grad
            give[:, :, cols] = sent_in

    common = 1 + (NY - 1) + NY + 2 * NY + jnp.where(core == 0, 2 * NY - 1, 0)
    ends = 1 + 4 * NY + jnp.where(core == 0, 4 * NY, 0)
    pl.semaphore_wait(barrier, common + jnp.where(at_end, ends, 2))

    def remote(src, dst, send, recv, other, pipe=None):
        return pltpu.make_async_remote_copy(
            src_ref=src,
            dst_ref=dst,
            send_sem=send,
            recv_sem=recv,
            device_id={"pipe": stage if pipe is None else pipe, "expert": other},
            device_id_type=MESH,
        )

    def give_copy(place_of):
        return remote(
            give, mine_ref.at[:, pl.ds(place_of * CAP, CAP)], give_send.at[0], give_recv.at[0], partner
        )

    @pl.when(core == 0)
    def _():
        give_copy(0).start()

    @pl.when(core == 1)
    def _():
        give_copy(1).start()

    give_copy(0).wait()

    slot = z * NY + y

    def entry(src_idx, sem_idx, other):
        return remote(
            mine_ref.at[src_idx], rows.at[core, slot], entry_sem.at[sem_idx], row_sem.at[slot], other
        )

    own_copy = pltpu.make_async_copy(mine_ref.at[expert], rows.at[core, slot], row_sem.at[slot])
    own_copy.start()
    for step in range(NY):
        yy = lax.rem(y + step, NY)
        if step > 0:
            entry(yy * 2 + half, step, at(yy, z, core)).start()

    def entry_far(step):
        yy = lax.rem(y + step, NY)
        return entry(yy * 2 + 1 - half, NY + step, at(yy, entry_z, core))

    @pl.when(jnp.logical_not(at_end))
    def _():
        for step in range(NY):
            entry_far(step).start()

    early = [
        remote(src, dst, early_send.at[i], early_recv.at[i], me, before)
        for i, (src, dst) in enumerate(
            (
                (hidden_ref, hidden_next),
                (grad_ref, grad_next),
                (gain_ref, gain_next),
                (place_ref, place_next),
            )
        )
    ]
    for copy in early:
        copy.start()

    def piece(idx):
        return rows.at[core, idx]

    def forward(idx, sems, other):
        return remote(piece(idx), piece(idx), sems.at[idx], row_sem.at[idx], other)

    def share(idx):
        return remote(piece(idx), piece(idx), share_sem.at[idx], pair_sem.at[idx], partner)

    def arrived(idx):
        pltpu.make_async_copy(mine_ref.at[0], piece(idx), row_sem.at[idx]).wait()

    def z_of(offset):
        return lax.rem(z + offset + NZ, NZ)

    my_half = pl.multiple_of(core * outw, 128)
    their_half = pl.multiple_of((1 - core) * outw, 128)
    block = NY * 16

    def swap_copy(src_z):
        span = pl.ds(src_z * NY, NY)
        return remote(
            part.at[span, :, pl.ds(their_half, outw)],
            swap.at[span],
            swap_send.at[src_z],
            swap_recv.at[src_z],
            partner,
        )

    def compute(src_z):
        @pl.loop(0, NY)
        def _(j):
            idx = src_z * NY + j
            pltpu.make_async_copy(
                mine_ref.at[0], rows.at[1 - core, idx], pair_sem.at[idx]
            ).wait()

        span = pl.ds(src_z * NY, NY)
        u = rows[0, span].reshape(block, width)
        dy = rows[1, span].reshape(block, width)
        a = nt(u, wgu[0])
        b = nt(u, wgu[1])
        g = nt(dy, wd[...])
        sig = jax.nn.sigmoid(a)
        act = a * sig
        hdn = act * b
        dga = (g * b * sig * (1.0 + a * (1.0 - sig))).astype(BF16)
        dgb = (g * act).astype(BF16)
        where = pl.ds(pl.multiple_of(src_z * block, block), block)
        da[where] = dga
        db[where] = dgb
        hd[where] = hdn.astype(BF16)
        dc = jnp.sum(hdn * g, axis=1, keepdims=True)
        dc = jnp.broadcast_to(dc.astype(BF16), (block, 128)).reshape(NY, 16, 128)
        part[span, :, :128] = dc
        part[span, :, width + 128 :] = dc
        tile = 512
        for turn in range(2):
            low = (1 - core if turn == 0 else core) * halfw
            for n in range(halfw // tile):
                cols = pl.ds(pl.multiple_of(low + n * tile, tile), tile)
                du = nn(dga, wgu[0, :, cols]) + nn(dgb, wgu[1, :, cols])
                part[span, :, pl.ds(pl.multiple_of(128 + low + n * tile, 128), tile)] = (
                    du.astype(BF16).reshape(NY, 16, tile)
                )
            if turn == 0:
                swap_copy(src_z).start()

    def chain_in(idx):
        pltpu.make_async_copy(summed.at[0], chain.at[idx], chain_recv.at[idx]).wait()
        acc[...] += chain[idx].astype(F32)

    def chain_out(idx, dst, other):
        return remote(summed.at[idx], chain.at[dst], chain_send.at[idx], chain_recv.at[dst], other)

    def final_out(number, cc, src_y, src_z):
        return remote(
            final.at[number, pl.ds(cc * CAP, CAP)],
            back_ref.at[expert, :, pl.ds(my_half, outw)],
            final_send.at[2 * number + cc],
            back_recv.at[2 * expert + core],
            at(src_y, src_z, cc),
            before,
        )

    def dc_out(number, cc, src_y, src_z):
        return remote(
            final.at[number, pl.ds(cc * CAP, CAP), pl.ds(0, 128)],
            dc_ref.at[expert],
            dc_send.at[2 * number + cc],
            dc_recv.at[expert],
            at(src_y, src_z, cc),
        )

    def dc_own(number):
        return pltpu.make_async_copy(
            final.at[number, pl.ds(0, CAP), pl.ds(0, 128)], dc_ref.at[expert], dc_recv.at[expert]
        )

    def finish(number, src_y, src_z):
        final[number] = acc[...].astype(BF16)
        for cc in range(2):
            final_out(number, cc, src_y, src_z).start()

        @pl.when(core == 0)
        def _():
            dc_out(number, 1, src_y, src_z).start()

            @pl.when((src_y == y) & (src_z == z))
            def _():
                dc_own(number).start()

            @pl.when((src_y != y) | (src_z != z))
            def _():
                dc_out(number, 0, src_y, src_z).start()

    def combine(src_z, hop, kind):
        swap_copy(src_z).wait_recv()

        @pl.loop(0, NY)
        def _(j):
            idx = src_z * NY + j
            acc[...] = part[idx, :, pl.ds(my_half, outw)].astype(F32) + swap[idx].astype(F32)
            if kind == 0:

                @pl.when(pos < last)
                def _():
                    chain_in(idx)

                @pl.when(pos > 0)
                def _():
                    chain_in(slots + j)

                finish(j, j, src_z)
            elif kind < 0:

                @pl.when(pos < last)
                def _():
                    chain_in(idx)

                @pl.when(pos > 0)
                def _():
                    summed[idx] = acc[...].astype(BF16)
                    chain_out(idx, idx, left).start()

                @pl.when(pos == 0)
                def _():
                    finish(hop * NY + j, j, src_z)
            else:

                @pl.when(pos > 0)
                def _():
                    chain_in(idx)

                @pl.when(pos < last)
                def _():
                    summed[idx] = acc[...].astype(BF16)
                    chain_out(idx, jnp.where(hop == 1, slots + j, idx), right).start()

                @pl.when(pos == last)
                def _():
                    finish(hop * NY + j, j, src_z)

    def pick(values, index, default=0):
        out = default
        for i, value in enumerate(values):
            out = jnp.where(index == i, value, out)
        return out

    def list_at(place, slot):
        code = pick((0o12, 0o231, 0o3421, 0o145320), place)
        return lax.rem(code // pick((1, 8, 64, 512, 4096, 32768), slot, 8**6), 8)

    def origin(slot):
        return pick((9, 1, 0, -2, -1, 2), slot)

    flip = last - pos

    def own_idx(j):
        return z * NY + lax.rem(y + NY - j, NY)

    @pl.loop(0, 15)
    def _(it):
        slot_now = it // 2
        part_now = lax.rem(it, 2)
        from_l = list_at(pos, slot_now)
        from_r = list_at(flip, slot_now)

        for jj in range(2):
            j = 2 * part_now + jj
            src_y = lax.rem(y + NY - j, NY)

            @pl.when(slot_now == 0)
            def _():
                idx = own_idx(j)
                arrived(idx)

                @pl.when(pos <= 1)
                def _():
                    forward(idx, right_sem, right).start()

                @pl.when(pos >= 2)
                def _():
                    forward(idx, left_sem, left).start()

                share(idx).start()

            @pl.when(from_l > 0)
            def _():
                idx = z_of(-from_l) * NY + src_y
                arrived(idx)

                @pl.when(pos < last)
                def _():
                    forward(idx, right_sem, right).start()

                share(idx).start()

            @pl.when(from_r > 0)
            def _():
                idx = z_of(from_r) * NY + src_y
                arrived(idx)

                @pl.when(pos > 0)
                def _():
                    forward(idx, left_sem, left).start()

                share(idx).start()

        @pl.when((it == 1) & at_end)
        def _():
            for step in range(NY):
                entry_far(step).start()

        first = jnp.where(it == 1, 0, 3)
        until = jnp.where(it == 1, 3, NY)

        @pl.when(((it == 1) | (it == 7)) & (pos == 2))
        def _():
            @pl.loop(first, until)
            def _(j):
                forward(own_idx(j), right_sem, right).start()

        @pl.when(((it == 1) | (it == 7)) & (pos == 1))
        def _():
            @pl.loop(first, until)
            def _(j):
                forward(own_idx(j), left_sem, left).start()

        @pl.when(it == 1)
        def _():
            for copy in w_copies:
                copy.wait()

        gone_l = list_at(pos, slot_now - 1)
        gone_r = list_at(flip, slot_now - 1)
        late = slot_now >= 4
        away = jnp.where(
            part_now == 0,
            jnp.where(late & (gone_r > 0), gone_r, -gone_l),
            jnp.where(late, 0, gone_r),
        )

        @pl.when((it == 1) | ((it >= 2) & (away != 0)))
        def _():
            compute(z_of(jnp.where(it == 1, 0, away)))

        since_l = it - 3 - flip
        slot_l = since_l // 2
        away_l = pos - origin(slot_l)

        @pl.when((since_l >= 2) & (lax.rem(since_l + 2, 2) == 0) & (slot_l <= 5) & (away_l >= 1))
        def _():
            combine(z_of(-away_l), away_l, -1)

        since_r = it - 3 - pos
        slot_r = (since_r + 16) // 2 - 8
        away_r = flip - origin(slot_r)
        odd_r = lax.rem(since_r + 16, 2)

        @pl.when(
            (slot_r >= jnp.where(odd_r == 1, 1, 3))
            & (slot_r <= jnp.where(odd_r == 1, 2, 5))
            & (away_r >= 1)
        )
        def _():
            combine(z_of(away_r), away_r, 1)

        @pl.when(it == pick((10, 14, 14, 11), pos))
        def _():
            combine(z, 0, 0)

        @pl.loop(0, 4)
        def _(s):
            n = 4 * (it - 13) + s
            tile = 512

            @pl.when((n >= 0) & (n < width // tile))
            def _():
                cols = pl.ds(pl.multiple_of(n * tile, tile), tile)
                u = rows[0, :, :, cols].reshape(-1, tile)
                dy = rows[1, :, :, cols].reshape(-1, tile)
                ggu[0, :, cols] = tn(da[...], u).astype(BF16)
                ggu[1, :, cols] = tn(db[...], u).astype(BF16)
                gd[:, cols] = tn(hd[...], dy).astype(BF16)

    out_copies = [
        pltpu.make_async_copy(ggu, ggu_hbm, out_sem.at[0]),
        pltpu.make_async_copy(gd, gd_hbm, out_sem.at[1]),
    ]
    for copy in out_copies:
        copy.start()

    for step in range(NY):
        if step > 0:
            entry(expert, step, partner).wait_send()
        entry(expert, NY + step, partner).wait_send()
    for copy in early:
        copy.wait()

    @pl.loop(0, 6)
    def _(hop):
        from_left = z_of(-hop)
        from_right = z_of(hop)

        @pl.loop(0, NY)
        def _(j):
            @pl.when((hop <= pos + 2) & (pos < last))
            def _():
                forward(from_left * NY + j, right_sem, right).wait_send()

            @pl.when((hop <= 5 - pos) & (pos > 0))
            def _():
                forward(from_right * NY + j, left_sem, left).wait_send()

            @pl.when((hop >= 1) & (hop <= pos + 2) & (pos > 0))
            def _():
                idx = from_left * NY + j
                chain_out(idx, idx, left).wait_send()

            @pl.when((hop >= 1) & (hop <= 5 - pos) & (pos < last))
            def _():
                idx = from_right * NY + j
                chain_out(idx, idx, right).wait_send()

            @pl.when((hop == 0) | ((hop <= 2) & at_end))
            def _():
                for cc in range(2):
                    final_out(hop * NY + j, cc, j, z).wait_send()

                @pl.when(core == 0)
                def _():
                    dc_out(hop * NY + j, 1, j, z).wait_send()

                    @pl.when((hop > 0) | (j != y))
                    def _():
                        dc_out(hop * NY + j, 0, j, z).wait_send()

    @pl.loop(0, slots)
    def _(idx):
        share(idx).wait_send()

    @pl.loop(0, NZ)
    def _(src_z):
        swap_copy(src_z).wait_send()

    for e in range(NY * 2):
        for cc in range(2):
            pltpu.make_async_copy(
                final.at[0, pl.ds(0, CAP)],
                back_ref.at[e, :, pl.ds(cc * outw, outw)],
                back_recv.at[2 * e + cc],
            ).wait()
        pltpu.make_async_copy(
            final.at[0, pl.ds(0, CAP), pl.ds(0, 128)], dc_ref.at[e], dc_recv.at[e]
        ).wait()
    for copy in out_copies:
        copy.wait()


def experts(ids, weights, gain_row, wgu, wd, hidden, grad, gain):
    width = hidden.shape[1]
    count = hidden.shape[0]
    units = wd.shape[0]
    outw = width // 2 + 128
    slots = NY * NZ
    dma = pltpu.SemaphoreType.DMA
    hbm = pl.BlockSpec(memory_space=pl.ANY)
    vmem = pl.BlockSpec(memory_space=pltpu.VMEM)
    like = lambda array: jax.ShapeDtypeStruct(array.shape, array.dtype)
    return pl.pallas_call(
        expert_kernel,
        out_shape=(
            jax.ShapeDtypeStruct((NY * 2, CAP, 2 * outw), BF16),
            jax.ShapeDtypeStruct((NY * 2, CAP, 128), BF16),
            like(wgu),
            like(wd),
            like(hidden),
            like(grad),
            like(gain),
            jax.ShapeDtypeStruct((NY * 2 * CAP, count), BF16),
        ),
        in_specs=[vmem] * 3 + [hbm] * 5,
        out_specs=[vmem, vmem] + [hbm] * 6,
        scratch_shapes=[
            pltpu.VMEM((NY * 2, 16, width), BF16),
            pltpu.VMEM((NY * 2, CAP, width), BF16),
            pltpu.VMEM((NY * 2 * CAP, count), BF16),
            pltpu.VMEM(hidden.shape, BF16),
            pltpu.VMEM(grad.shape, BF16),
            pltpu.VMEM((2, slots, 16, width), BF16),
            pltpu.VMEM(wgu.shape, BF16),
            pltpu.VMEM(wd.shape, BF16),
            pltpu.VMEM((slots, 16, 2 * outw), BF16),
            pltpu.VMEM((slots, 16, outw), BF16),
            pltpu.VMEM((slots + NY, 16, outw), BF16),
            pltpu.VMEM((slots, 16, outw), BF16),
            pltpu.VMEM((3 * NY, 16, outw), BF16),
            pltpu.VMEM((16, outw), F32),
            pltpu.VMEM((slots * 16, units), BF16),
            pltpu.VMEM((slots * 16, units), BF16),
            pltpu.VMEM((slots * 16, units), BF16),
            pltpu.VMEM(wgu.shape, BF16),
            pltpu.VMEM(wd.shape, BF16),
            dma((slots,)),
            dma((slots,)),
            dma((slots,)),
            dma((slots,)),
            dma((slots,)),
            dma((2 * NY,)),
            dma((NZ,)),
            dma((NZ,)),
            dma((slots,)),
            dma((slots + NY,)),
            dma((6 * NY,)),
            dma((4 * NY,)),
            dma((6 * NY,)),
            dma((2 * NY,)),
            dma((2,)),
            dma((2,)),
            dma((4,)),
            dma((4,)),
            dma((2,)),
            dma((1,)),
            dma((1,)),
        ],
        compiler_params=pltpu.CompilerParams(
            collective_id=0, has_side_effects=True, vmem_limit_bytes=60 * 1024 * 1024
        ),
    )(ids, weights, gain_row, wgu, wd, hidden, grad, gain)


def finish_kernel(
    back_hbm,
    hidden_hbm,
    grad_hbm,
    place_ref,
    gain_ref,
    ids_ref,
    weight_ref,
    dc_ref,
    ggu_hbm,
    gd_hbm,
    handed_hbm,
    ggu_out,
    gd_out,
    combine_ref,
    back,
    hidden,
    grad,
    handed,
    ggu,
    gd,
    scaled,
    in_sem,
    out_sem,
):
    width = hidden.shape[1]
    count = hidden.shape[0]
    ins = [
        pltpu.make_async_copy(src, dst, in_sem.at[i])
        for i, (src, dst) in enumerate(
            (
                (hidden_hbm, hidden),
                (back_hbm, back),
                (grad_hbm, grad),
                (ggu_hbm, ggu),
                (gd_hbm, gd),
            )
        )
    ]
    for copy in ins:
        copy.start()
    ids = ids_ref[...]
    weights = weight_ref[...].astype(F32)
    plain, _ = placing(ids, weights)
    total = jnp.zeros(ids.shape, F32)
    for e in range(NY * 2):
        dc = jnp.sum(plain[e] * dc_ref[e].astype(F32), axis=0, keepdims=True)
        total = total + jnp.where(ids == e, dc, 0.0)
    combine_ref[...] = total / weights
    ins[0].wait()
    tile = 512
    square = jnp.zeros((count, 128), F32)
    for n in range(width // 128):
        h = hidden[:, n * 128 : (n + 1) * 128].astype(F32)
        square = square + h * h
    rms = jnp.sqrt(jnp.sum(square, axis=1, keepdims=True) / width + 1e-06)
    ins[1].wait()
    place = place_ref[...]
    along = jnp.zeros((count, 1), F32)
    for n in range(width // tile):
        cols = slice(n * tile, (n + 1) * tile)
        rows = back[:, :, 128 + n * tile : 128 + (n + 1) * tile].reshape(-1, tile)
        part = tn(place, rows) * gain_ref[:, cols]
        scaled[:, cols] = part
        along = along + jnp.sum(part * (hidden[:, cols].astype(F32) / rms), axis=1, keepdims=True)
    inner = along / width
    for i in (3, 4):
        ins[i].wait()
    outs = [
        pltpu.make_async_copy(ggu, ggu_out, out_sem.at[0]),
        pltpu.make_async_copy(gd, gd_out, out_sem.at[1]),
        pltpu.make_async_copy(handed, handed_hbm, out_sem.at[2]),
    ]
    outs[0].start()
    outs[1].start()
    ins[2].wait()
    for n in range(width // tile):
        cols = slice(n * tile, (n + 1) * tile)
        normed = hidden[:, cols].astype(F32) / rms
        handed[:, cols] = (
            grad[:, cols].astype(F32) + (scaled[:, cols] - normed * inner) / rms
        ).astype(BF16)
    outs[2].start()
    for copy in outs:
        copy.wait()


def finish(back, hidden, grad, place, gain, ids, weights, dc, ggu, gd):
    like = lambda array: jax.ShapeDtypeStruct(array.shape, array.dtype)
    hbm = pl.BlockSpec(memory_space=pl.ANY)
    vmem = pl.BlockSpec(memory_space=pltpu.VMEM)
    room = lambda array: pltpu.VMEM(array.shape, array.dtype)
    return pl.pallas_call(
        finish_kernel,
        out_shape=(like(hidden), like(ggu), like(gd), jax.ShapeDtypeStruct(ids.shape, F32)),
        in_specs=[hbm, hbm, hbm, vmem, vmem, vmem, vmem, vmem, hbm, hbm],
        out_specs=[hbm, hbm, hbm, vmem],
        scratch_shapes=[
            room(back),
            room(hidden),
            room(grad),
            room(hidden),
            room(ggu),
            room(gd),
            pltpu.VMEM(hidden.shape, F32),
            pltpu.SemaphoreType.DMA((5,)),
            pltpu.SemaphoreType.DMA((3,)),
        ],
        compiler_params=pltpu.CompilerParams(vmem_limit_bytes=63 * 1024 * 1024),
    )(back, hidden, grad, place, gain, ids, weights, dc, ggu, gd)


def on_device(hidden_in, out_grad, expert_ids, route_weight, norm_gain, w_gate_up, w_down):
    width = hidden_in.shape[2]
    ids = expert_ids[0].T
    weights = route_weight[0].T
    back, dc_back, ggu, gd, hidden_next, grad_next, gain_next, place_next = experts(
        ids,
        weights,
        norm_gain,
        w_gate_up[0, 0],
        w_down[0, 0],
        hidden_in[0],
        out_grad[0],
        norm_gain.reshape(-1, 128),
    )
    handed, grad_gate_up, grad_down, combine = finish(
        back,
        hidden_next,
        grad_next,
        place_next,
        gain_next.reshape(1, width),
        ids,
        weights,
        dc_back,
        ggu,
        gd,
    )
    return (
        handed[None],
        grad_gate_up[None, None],
        grad_down[None, None],
        combine.T[None],
    )


def solution(mesh):
    return jax.shard_map(
        on_device,
        mesh=mesh,
        in_specs=(
            P("pipe", "expert", None),
            P("pipe", "expert", None),
            P("pipe", "expert", None),
            P("pipe", "expert", None),
            P("pipe", None),
            P("pipe", "expert", None, None, None),
            P("pipe", "expert", None, None),
        ),
        out_specs=(
            P("pipe", "expert", None),
            P("pipe", "expert", None, None, None),
            P("pipe", "expert", None, None),
            P("pipe", "expert", None),
        ),
        check_vma=False,
    )
```

```python
import jax
import jax.numpy as jnp
from jax import lax
from jax.experimental import pallas as pl
from jax.experimental.pallas import tpu as pltpu
from jax.sharding import PartitionSpec as P

CAP = 8
NY = 4
NZ = 8
LINE = 4
MESH = pl.DeviceIdType.MESH
F32 = jnp.float32
BF16 = jnp.bfloat16


def nt(left, right):
    return lax.dot_general(left, right, (((1,), (1,)), ((), ())), preferred_element_type=F32)


def nn(left, right):
    return lax.dot_general(left, right, (((1,), (0,)), ((), ())), preferred_element_type=F32)


def tn(left, right):
    return lax.dot_general(left, right, (((0,), (0,)), ((), ())), preferred_element_type=F32)


def placing(ids, weights):
    count = ids.shape[1]
    span = NY * 2
    hits = [ids == e for e in range(span)]
    member = jnp.concatenate(
        [jnp.max(jnp.where(hit, 1.0, 0.0), axis=0, keepdims=True) for hit in hits], axis=0
    )
    above = lax.broadcasted_iota(jnp.int32, (count, count), 0) < lax.broadcasted_iota(
        jnp.int32, (count, count), 1
    )
    position = nn(member.astype(BF16), jnp.where(above, 1.0, 0.0).astype(BF16))
    row = lax.broadcasted_iota(jnp.int32, (CAP, count), 0).astype(F32)
    plain = []
    weighted = []
    for e in range(span):
        here = (row == position[e : e + 1]) & (member[e : e + 1] > 0.5)
        place = jnp.where(here, 1.0, 0.0)
        share = jnp.sum(jnp.where(hits[e], weights, 0.0), axis=0, keepdims=True)
        plain.append(place)
        weighted.append(place * share)
    return plain, weighted


def expert_kernel(
    ids_ref,
    weight_ref,
    gain_row,
    wgu_hbm,
    wd_hbm,
    hidden_ref,
    grad_ref,
    gain_ref,
    back_ref,
    dc_ref,
    ggu_hbm,
    gd_hbm,
    hidden_next,
    grad_next,
    gain_next,
    place_next,
    mine_ref,
    give,
    place_ref,
    tokens,
    token_grad,
    rows,
    wgu,
    wd,
    part,
    swap,
    chain,
    summed,
    final,
    acc,
    da,
    db,
    hd,
    ggu,
    gd,
    row_sem,
    pair_sem,
    right_sem,
    left_sem,
    share_sem,
    entry_sem,
    swap_send,
    swap_recv,
    chain_send,
    chain_recv,
    final_send,
    back_recv,
    dc_send,
    dc_recv,
    w_sem,
    out_sem,
    early_send,
    early_recv,
    pack_sem,
    give_send,
    give_recv,
):
    me = lax.axis_index("expert")
    stage = lax.axis_index("pipe")
    stages = lax.axis_size("pipe")
    before = lax.rem(stage + stages - 1, stages)
    after = lax.rem(stage + 1, stages)
    core = lax.rem(me, 2)
    z = lax.rem(me // 2, NZ)
    y = me // (2 * NZ)
    half = z // LINE
    pos = lax.rem(z, LINE)
    expert = y * 2 + half
    width = mine_ref.shape[2]
    halfw = width // 2
    outw = halfw + 128
    slots = NY * NZ
    last = LINE - 1
    at_end = (pos == 0) | (pos == last)

    def at(yy, zz, cc):
        return (yy * NZ + zz) * 2 + cc

    partner = at(y, z, 1 - core)
    right = at(y, lax.rem(z + 1, NZ), core)
    left = at(y, lax.rem(z + NZ - 1, NZ), core)
    entry_z = jnp.where(pos >= 2, lax.rem(LINE * (half + 1), NZ), lax.rem(LINE * half + NZ - 1, NZ))

    loads = [
        pltpu.make_async_copy(hidden_ref, tokens, pack_sem.at[0]),
        pltpu.make_async_copy(grad_ref, token_grad, pack_sem.at[1]),
    ]
    for copy in loads:
        copy.start()

    barrier = pltpu.get_barrier_semaphore()

    def greet(pipe, other):
        pl.semaphore_signal(
            barrier, inc=1, device_id={"pipe": pipe, "expert": other}, device_id_type=MESH
        )

    greet(stage, partner)
    for step in range(1, NY):
        greet(stage, at(lax.rem(y + step, NY), z, core))

    @pl.when(pos > 0)
    def _():
        greet(stage, left)

    @pl.when(pos < last)
    def _():
        greet(stage, right)

    @pl.when(at_end)
    def _():
        way = jnp.where(pos == 0, NZ - 1, 1)
        for hop in (1, 2):
            for yy in range(NY):
                greet(stage, at(yy, lax.rem(z + hop * way, NZ), core))

    for cc in range(2):
        for yy in range(NY):
            greet(after, at(yy, z, cc))
            greet(after, at(yy, entry_z, cc))
    for yy in range(NY):
        greet(stage, at(yy, entry_z, 0))

        @pl.when((yy != y) | (core != 0))
        def _():
            greet(stage, at(yy, z, 0))

    w_copies = [
        pltpu.make_async_copy(wgu_hbm, wgu, w_sem.at[0]),
        pltpu.make_async_copy(wd_hbm, wd, w_sem.at[1]),
    ]
    for copy in w_copies:
        copy.start()

    plain, weighted = placing(ids_ref[...], weight_ref[...].astype(F32))
    place = jnp.concatenate(plain, axis=0).astype(BF16)
    place_w = jnp.concatenate(weighted, axis=0).astype(BF16)
    place_ref[...] = place
    for copy in loads:
        copy.wait()
    count = tokens.shape[0]
    square = jnp.zeros((count, 128), F32)
    for n in range(width // 128):
        h = tokens[:, n * 128 : (n + 1) * 128].astype(F32)
        square = square + h * h
    scale = 1.0 / jnp.sqrt(jnp.sum(square, axis=1, keepdims=True) / width + 1e-06)
    for n in range(width // 512):
        cols = slice(n * 512, (n + 1) * 512)
        u = ((tokens[:, cols].astype(F32) * scale) * gain_row[:, cols]).astype(BF16)
        sent_in = nn(place, u).astype(BF16).reshape(NY * 2, CAP, 512)
        sent_grad = nn(place_w, token_grad[:, cols]).astype(BF16).reshape(NY * 2, CAP, 512)

        @pl.when(core == 0)
        def _():
            mine_ref[:, :CAP, cols] = sent_in
            give[:, :, cols] = sent_grad

        @pl.when(core == 1)
        def _():
            mine_ref[:, CAP:, cols] = sent_grad
            give[:, :, cols] = sent_in

    common = 1 + (NY - 1) + NY + 2 * NY + jnp.where(core == 0, 2 * NY - 1, 0)
    ends = 1 + 4 * NY + jnp.where(core == 0, 4 * NY, 0)
    pl.semaphore_wait(barrier, common + jnp.where(at_end, ends, 2))

    def remote(src, dst, send, recv, other, pipe=None):
        return pltpu.make_async_remote_copy(
            src_ref=src,
            dst_ref=dst,
            send_sem=send,
            recv_sem=recv,
            device_id={"pipe": stage if pipe is None else pipe, "expert": other},
            device_id_type=MESH,
        )

    def give_copy(e, place_of):
        return remote(
            give.at[e],
            mine_ref.at[e, pl.ds(place_of * CAP, CAP)],
            give_send.at[e],
            give_recv.at[e],
            partner,
        )

    for step in range(NY):
        yy = lax.rem(y + step, NY)
        for e in (yy * 2 + half, yy * 2 + 1 - half):

            @pl.when(core == 0)
            def _():
                give_copy(e, 0).start()

            @pl.when(core == 1)
            def _():
                give_copy(e, 1).start()

    slot = z * NY + y

    def entry(src_idx, sem_idx, other):
        return remote(
            mine_ref.at[src_idx], rows.at[core, slot], entry_sem.at[sem_idx], row_sem.at[slot], other
        )

    own_copy = pltpu.make_async_copy(mine_ref.at[expert], rows.at[core, slot], row_sem.at[slot])

    def entry_far(step):
        yy = lax.rem(y + step, NY)
        return entry(yy * 2 + 1 - half, NY + step, at(yy, entry_z, core))

    for step in range(NY):
        yy = lax.rem(y + step, NY)
        give_copy(yy * 2 + half, 0).wait()
        if step > 0:
            entry(yy * 2 + half, step, at(yy, z, core)).start()
        else:
            own_copy.start()
        give_copy(yy * 2 + 1 - half, 0).wait()

        @pl.when(jnp.logical_not(at_end))
        def _():
            entry_far(step).start()

    early = [
        remote(src, dst, early_send.at[i], early_recv.at[i], me, before)
        for i, (src, dst) in enumerate(
            (
                (hidden_ref, hidden_next),
                (grad_ref, grad_next),
                (gain_ref, gain_next),
                (place_ref, place_next),
            )
        )
    ]
    for copy in early:
        copy.start()

    def piece(idx):
        return rows.at[core, idx]

    def forward(idx, sems, other):
        return remote(piece(idx), piece(idx), sems.at[idx], row_sem.at[idx], other)

    def share(idx):
        return remote(piece(idx), piece(idx), share_sem.at[idx], pair_sem.at[idx], partner)

    def arrived(idx):
        pltpu.make_async_copy(mine_ref.at[0], piece(idx), row_sem.at[idx]).wait()

    def z_of(offset):
        return lax.rem(z + offset + NZ, NZ)

    my_half = pl.multiple_of(core * outw, 128)
    their_half = pl.multiple_of((1 - core) * outw, 128)
    block = NY * 16

    def swap_copy(src_z):
        span = pl.ds(src_z * NY, NY)
        return remote(
            part.at[span, :, pl.ds(their_half, outw)],
            swap.at[span],
            swap_send.at[src_z],
            swap_recv.at[src_z],
            partner,
        )

    def compute(src_z):
        @pl.loop(0, NY)
        def _(j):
            idx = src_z * NY + j
            pltpu.make_async_copy(
                mine_ref.at[0], rows.at[1 - core, idx], pair_sem.at[idx]
            ).wait()

        span = pl.ds(src_z * NY, NY)
        u = rows[0, span].reshape(block, width)
        dy = rows[1, span].reshape(block, width)
        a = nt(u, wgu[0])
        b = nt(u, wgu[1])
        g = nt(dy, wd[...])
        sig = jax.nn.sigmoid(a)
        act = a * sig
        hdn = act * b
        dga = (g * b * sig * (1.0 + a * (1.0 - sig))).astype(BF16)
        dgb = (g * act).astype(BF16)
        where = pl.ds(pl.multiple_of(src_z * block, block), block)
        da[where] = dga
        db[where] = dgb
        hd[where] = hdn.astype(BF16)
        dc = jnp.sum(hdn * g, axis=1, keepdims=True)
        dc = jnp.broadcast_to(dc.astype(BF16), (block, 128)).reshape(NY, 16, 128)
        part[span, :, :128] = dc
        part[span, :, width + 128 :] = dc
        tile = 512
        for turn in range(2):
            low = (1 - core if turn == 0 else core) * halfw
            for n in range(halfw // tile):
                cols = pl.ds(pl.multiple_of(low + n * tile, tile), tile)
                du = nn(dga, wgu[0, :, cols]) + nn(dgb, wgu[1, :, cols])
                part[span, :, pl.ds(pl.multiple_of(128 + low + n * tile, 128), tile)] = (
                    du.astype(BF16).reshape(NY, 16, tile)
                )
            if turn == 0:
                swap_copy(src_z).start()

    def chain_in(idx):
        pltpu.make_async_copy(summed.at[0], chain.at[idx], chain_recv.at[idx]).wait()
        acc[...] += chain[idx].astype(F32)

    def chain_out(idx, dst, other):
        return remote(summed.at[idx], chain.at[dst], chain_send.at[idx], chain_recv.at[dst], other)

    def final_out(number, cc, src_y, src_z):
        return remote(
            final.at[number, pl.ds(cc * CAP, CAP)],
            back_ref.at[expert, :, pl.ds(my_half, outw)],
            final_send.at[2 * number + cc],
            back_recv.at[2 * expert + core],
            at(src_y, src_z, cc),
            before,
        )

    def dc_out(number, cc, src_y, src_z):
        return remote(
            final.at[number, pl.ds(cc * CAP, CAP), pl.ds(0, 128)],
            dc_ref.at[expert],
            dc_send.at[2 * number + cc],
            dc_recv.at[expert],
            at(src_y, src_z, cc),
        )

    def dc_own(number):
        return pltpu.make_async_copy(
            final.at[number, pl.ds(0, CAP), pl.ds(0, 128)], dc_ref.at[expert], dc_recv.at[expert]
        )

    def finish(number, src_y, src_z):
        final[number] = acc[...].astype(BF16)
        for cc in range(2):
            final_out(number, cc, src_y, src_z).start()

        @pl.when(core == 0)
        def _():
            dc_out(number, 1, src_y, src_z).start()

            @pl.when((src_y == y) & (src_z == z))
            def _():
                dc_own(number).start()

            @pl.when((src_y != y) | (src_z != z))
            def _():
                dc_out(number, 0, src_y, src_z).start()

    def combine(src_z, hop, kind):
        swap_copy(src_z).wait_recv()

        @pl.loop(0, NY)
        def _(j):
            idx = src_z * NY + j
            acc[...] = part[idx, :, pl.ds(my_half, outw)].astype(F32) + swap[idx].astype(F32)
            if kind == 0:

                @pl.when(pos < last)
                def _():
                    chain_in(idx)

                @pl.when(pos > 0)
                def _():
                    chain_in(slots + j)

                finish(j, j, src_z)
            elif kind < 0:

                @pl.when(pos < last)
                def _():
                    chain_in(idx)

                @pl.when(pos > 0)
                def _():
                    summed[idx] = acc[...].astype(BF16)
                    chain_out(idx, idx, left).start()

                @pl.when(pos == 0)
                def _():
                    finish(hop * NY + j, j, src_z)
            else:

                @pl.when(pos > 0)
                def _():
                    chain_in(idx)

                @pl.when(pos < last)
                def _():
                    summed[idx] = acc[...].astype(BF16)
                    chain_out(idx, jnp.where(hop == 1, slots + j, idx), right).start()

                @pl.when(pos == last)
                def _():
                    finish(hop * NY + j, j, src_z)

    def pick(values, index, default=0):
        out = default
        for i, value in enumerate(values):
            out = jnp.where(index == i, value, out)
        return out

    def list_at(place, slot):
        code = pick((0o12, 0o231, 0o3421, 0o145320), place)
        return lax.rem(code // pick((1, 8, 64, 512, 4096, 32768), slot, 8**6), 8)

    def origin(slot):
        return pick((9, 1, 0, -2, -1, 2), slot)

    flip = last - pos

    def own_idx(j):
        return z * NY + lax.rem(y + NY - j, NY)

    @pl.loop(0, 15)
    def _(it):
        slot_now = it // 2
        part_now = lax.rem(it, 2)
        from_l = list_at(pos, slot_now)
        from_r = list_at(flip, slot_now)

        for jj in range(2):
            j = 2 * part_now + jj
            src_y = lax.rem(y + NY - j, NY)

            @pl.when(slot_now == 0)
            def _():
                idx = own_idx(j)
                arrived(idx)

                @pl.when(pos <= 1)
                def _():
                    forward(idx, right_sem, right).start()

                @pl.when(pos >= 2)
                def _():
                    forward(idx, left_sem, left).start()

                share(idx).start()

            @pl.when(from_l > 0)
            def _():
                idx = z_of(-from_l) * NY + src_y
                arrived(idx)

                @pl.when(pos < last)
                def _():
                    forward(idx, right_sem, right).start()

                share(idx).start()

            @pl.when(from_r > 0)
            def _():
                idx = z_of(from_r) * NY + src_y
                arrived(idx)

                @pl.when(pos > 0)
                def _():
                    forward(idx, left_sem, left).start()

                share(idx).start()

        @pl.when((it == 1) & at_end)
        def _():
            for step in range(NY):
                entry_far(step).start()

        first = jnp.where(it == 1, 0, 3)
        until = jnp.where(it == 1, 3, NY)

        @pl.when(((it == 1) | (it == 7)) & (pos == 2))
        def _():
            @pl.loop(first, until)
            def _(j):
                forward(own_idx(j), right_sem, right).start()

        @pl.when(((it == 1) | (it == 7)) & (pos == 1))
        def _():
            @pl.loop(first, until)
            def _(j):
                forward(own_idx(j), left_sem, left).start()

        @pl.when(it == 1)
        def _():
            for copy in w_copies:
                copy.wait()

        gone_l = list_at(pos, slot_now - 1)
        gone_r = list_at(flip, slot_now - 1)
        late = slot_now >= 4
        away = jnp.where(
            part_now == 0,
            jnp.where(late & (gone_r > 0), gone_r, -gone_l),
            jnp.where(late, 0, gone_r),
        )

        @pl.when((it == 1) | ((it >= 2) & (away != 0)))
        def _():
            compute(z_of(jnp.where(it == 1, 0, away)))

        since_l = it - 3 - flip
        slot_l = since_l // 2
        away_l = pos - origin(slot_l)

        @pl.when((since_l >= 2) & (lax.rem(since_l + 2, 2) == 0) & (slot_l <= 5) & (away_l >= 1))
        def _():
            combine(z_of(-away_l), away_l, -1)

        since_r = it - 3 - pos
        slot_r = (since_r + 16) // 2 - 8
        away_r = flip - origin(slot_r)
        odd_r = lax.rem(since_r + 16, 2)

        @pl.when(
            (slot_r >= jnp.where(odd_r == 1, 1, 3))
            & (slot_r <= jnp.where(odd_r == 1, 2, 5))
            & (away_r >= 1)
        )
        def _():
            combine(z_of(away_r), away_r, 1)

        @pl.when(it == pick((10, 14, 14, 11), pos))
        def _():
            combine(z, 0, 0)

        @pl.loop(0, 4)
        def _(s):
            n = jnp.where(at_end, 4 * (it - 13) + s, jnp.where(s < 2, 2 * (it - 9) + s, -1))
            tile = 512

            @pl.when((n >= 0) & (n < width // tile))
            def _():
                cols = pl.ds(pl.multiple_of(n * tile, tile), tile)
                u = rows[0, :, :, cols].reshape(-1, tile)
                dy = rows[1, :, :, cols].reshape(-1, tile)
                ggu[0, :, cols] = tn(da[...], u).astype(BF16)
                ggu[1, :, cols] = tn(db[...], u).astype(BF16)
                gd[:, cols] = tn(hd[...], dy).astype(BF16)

    out_copies = [
        pltpu.make_async_copy(ggu, ggu_hbm, out_sem.at[0]),
        pltpu.make_async_copy(gd, gd_hbm, out_sem.at[1]),
    ]
    for copy in out_copies:
        copy.start()

    for step in range(NY):
        if step > 0:
            entry(expert, step, partner).wait_send()
        entry(expert, NY + step, partner).wait_send()
    for copy in early:
        copy.wait()

    @pl.loop(0, 6)
    def _(hop):
        from_left = z_of(-hop)
        from_right = z_of(hop)

        @pl.loop(0, NY)
        def _(j):
            @pl.when((hop <= pos + 2) & (pos < last))
            def _():
                forward(from_left * NY + j, right_sem, right).wait_send()

            @pl.when((hop <= 5 - pos) & (pos > 0))
            def _():
                forward(from_right * NY + j, left_sem, left).wait_send()

            @pl.when((hop >= 1) & (hop <= pos + 2) & (pos > 0))
            def _():
                idx = from_left * NY + j
                chain_out(idx, idx, left).wait_send()

            @pl.when((hop >= 1) & (hop <= 5 - pos) & (pos < last))
            def _():
                idx = from_right * NY + j
                chain_out(idx, idx, right).wait_send()

            @pl.when((hop == 0) | ((hop <= 2) & at_end))
            def _():
                for cc in range(2):
                    final_out(hop * NY + j, cc, j, z).wait_send()

                @pl.when(core == 0)
                def _():
                    dc_out(hop * NY + j, 1, j, z).wait_send()

                    @pl.when((hop > 0) | (j != y))
                    def _():
                        dc_out(hop * NY + j, 0, j, z).wait_send()

    @pl.loop(0, slots)
    def _(idx):
        share(idx).wait_send()

    @pl.loop(0, NZ)
    def _(src_z):
        swap_copy(src_z).wait_send()

    for e in range(NY * 2):
        for cc in range(2):
            pltpu.make_async_copy(
                final.at[0, pl.ds(0, CAP)],
                back_ref.at[e, :, pl.ds(cc * outw, outw)],
                back_recv.at[2 * e + cc],
            ).wait()
        pltpu.make_async_copy(
            final.at[0, pl.ds(0, CAP), pl.ds(0, 128)], dc_ref.at[e], dc_recv.at[e]
        ).wait()
    for copy in out_copies:
        copy.wait()


def experts(ids, weights, gain_row, wgu, wd, hidden, grad, gain):
    width = hidden.shape[1]
    count = hidden.shape[0]
    units = wd.shape[0]
    outw = width // 2 + 128
    slots = NY * NZ
    dma = pltpu.SemaphoreType.DMA
    hbm = pl.BlockSpec(memory_space=pl.ANY)
    vmem = pl.BlockSpec(memory_space=pltpu.VMEM)
    like = lambda array: jax.ShapeDtypeStruct(array.shape, array.dtype)
    return pl.pallas_call(
        expert_kernel,
        out_shape=(
            jax.ShapeDtypeStruct((NY * 2, CAP, 2 * outw), BF16),
            jax.ShapeDtypeStruct((NY * 2, CAP, 128), BF16),
            like(wgu),
            like(wd),
            like(hidden),
            like(grad),
            like(gain),
            jax.ShapeDtypeStruct((NY * 2 * CAP, count), BF16),
        ),
        in_specs=[vmem] * 3 + [hbm] * 5,
        out_specs=[vmem, vmem] + [hbm] * 6,
        scratch_shapes=[
            pltpu.VMEM((NY * 2, 16, width), BF16),
            pltpu.VMEM((NY * 2, CAP, width), BF16),
            pltpu.VMEM((NY * 2 * CAP, count), BF16),
            pltpu.VMEM(hidden.shape, BF16),
            pltpu.VMEM(grad.shape, BF16),
            pltpu.VMEM((2, slots, 16, width), BF16),
            pltpu.VMEM(wgu.shape, BF16),
            pltpu.VMEM(wd.shape, BF16),
            pltpu.VMEM((slots, 16, 2 * outw), BF16),
            pltpu.VMEM((slots, 16, outw), BF16),
            pltpu.VMEM((slots + NY, 16, outw), BF16),
            pltpu.VMEM((slots, 16, outw), BF16),
            pltpu.VMEM((3 * NY, 16, outw), BF16),
            pltpu.VMEM((16, outw), F32),
            pltpu.VMEM((slots * 16, units), BF16),
            pltpu.VMEM((slots * 16, units), BF16),
            pltpu.VMEM((slots * 16, units), BF16),
            pltpu.VMEM(wgu.shape, BF16),
            pltpu.VMEM(wd.shape, BF16),
            dma((slots,)),
            dma((slots,)),
            dma((slots,)),
            dma((slots,)),
            dma((slots,)),
            dma((2 * NY,)),
            dma((NZ,)),
            dma((NZ,)),
            dma((slots,)),
            dma((slots + NY,)),
            dma((6 * NY,)),
            dma((4 * NY,)),
            dma((6 * NY,)),
            dma((2 * NY,)),
            dma((2,)),
            dma((2,)),
            dma((4,)),
            dma((4,)),
            dma((2,)),
            dma((2 * NY,)),
            dma((2 * NY,)),
        ],
        compiler_params=pltpu.CompilerParams(
            collective_id=0, has_side_effects=True, vmem_limit_bytes=60 * 1024 * 1024
        ),
    )(ids, weights, gain_row, wgu, wd, hidden, grad, gain)


def finish_kernel(
    back_hbm,
    hidden_hbm,
    grad_hbm,
    place_ref,
    gain_ref,
    ids_ref,
    weight_ref,
    dc_ref,
    ggu_hbm,
    gd_hbm,
    handed_hbm,
    ggu_out,
    gd_out,
    combine_ref,
    back,
    hidden,
    grad,
    handed,
    ggu,
    gd,
    scaled,
    in_sem,
    out_sem,
):
    width = hidden.shape[1]
    count = hidden.shape[0]
    ins = [
        pltpu.make_async_copy(src, dst, in_sem.at[i])
        for i, (src, dst) in enumerate(
            (
                (hidden_hbm, hidden),
                (back_hbm, back),
                (grad_hbm, grad),
                (ggu_hbm, ggu),
                (gd_hbm, gd),
            )
        )
    ]
    for copy in ins:
        copy.start()
    ids = ids_ref[...]
    weights = weight_ref[...].astype(F32)
    plain, _ = placing(ids, weights)
    total = jnp.zeros(ids.shape, F32)
    for e in range(NY * 2):
        dc = jnp.sum(plain[e] * dc_ref[e].astype(F32), axis=0, keepdims=True)
        total = total + jnp.where(ids == e, dc, 0.0)
    combine_ref[...] = total / weights
    ins[0].wait()
    tile = 512
    square = jnp.zeros((count, 128), F32)
    for n in range(width // 128):
        h = hidden[:, n * 128 : (n + 1) * 128].astype(F32)
        square = square + h * h
    scale = 1.0 / jnp.sqrt(jnp.sum(square, axis=1, keepdims=True) / width + 1e-06)
    for i in (3, 4):
        ins[i].wait()
    grads = [
        pltpu.make_async_copy(ggu, ggu_out, out_sem.at[0]),
        pltpu.make_async_copy(gd, gd_out, out_sem.at[1]),
    ]
    for copy in grads:
        copy.start()
    ins[1].wait()
    place = place_ref[...]
    along = jnp.zeros((count, 1), F32)
    for n in range(width // tile):
        cols = slice(n * tile, (n + 1) * tile)
        rows = back[:, :, 128 + n * tile : 128 + (n + 1) * tile].reshape(-1, tile)
        part = tn(place, rows) * gain_ref[:, cols]
        scaled[:, cols] = part
        along = along + jnp.sum(part * hidden[:, cols].astype(F32), axis=1, keepdims=True)
    inner = along * scale / width
    ins[2].wait()
    halves = []
    for n in range(width // tile):
        cols = slice(n * tile, (n + 1) * tile)
        normed = hidden[:, cols].astype(F32) * scale
        handed[:, cols] = (
            grad[:, cols].astype(F32) + (scaled[:, cols] - normed * inner) * scale
        ).astype(BF16)
        if n in (width // tile // 2 - 1, width // tile - 1):
            span = pl.ds(len(halves) * (width // 2), width // 2)
            halves.append(
                pltpu.make_async_copy(
                    handed.at[:, span], handed_hbm.at[:, span], out_sem.at[2 + len(halves)]
                )
            )
            halves[-1].start()
    for copy in grads + halves:
        copy.wait()


def finish(back, hidden, grad, place, gain, ids, weights, dc, ggu, gd):
    like = lambda array: jax.ShapeDtypeStruct(array.shape, array.dtype)
    hbm = pl.BlockSpec(memory_space=pl.ANY)
    vmem = pl.BlockSpec(memory_space=pltpu.VMEM)
    room = lambda array: pltpu.VMEM(array.shape, array.dtype)
    return pl.pallas_call(
        finish_kernel,
        out_shape=(like(hidden), like(ggu), like(gd), jax.ShapeDtypeStruct(ids.shape, F32)),
        in_specs=[hbm, hbm, hbm, vmem, vmem, vmem, vmem, vmem, hbm, hbm],
        out_specs=[hbm, hbm, hbm, vmem],
        scratch_shapes=[
            room(back),
            room(hidden),
            room(grad),
            room(hidden),
            room(ggu),
            room(gd),
            pltpu.VMEM(hidden.shape, F32),
            pltpu.SemaphoreType.DMA((5,)),
            pltpu.SemaphoreType.DMA((4,)),
        ],
        compiler_params=pltpu.CompilerParams(vmem_limit_bytes=63 * 1024 * 1024),
    )(back, hidden, grad, place, gain, ids, weights, dc, ggu, gd)


def on_device(hidden_in, out_grad, expert_ids, route_weight, norm_gain, w_gate_up, w_down):
    width = hidden_in.shape[2]
    ids = expert_ids[0].T
    weights = route_weight[0].T
    back, dc_back, ggu, gd, hidden_next, grad_next, gain_next, place_next = experts(
        ids,
        weights,
        norm_gain,
        w_gate_up[0, 0],
        w_down[0, 0],
        hidden_in[0],
        out_grad[0],
        norm_gain.reshape(-1, 128),
    )
    handed, grad_gate_up, grad_down, combine = finish(
        back,
        hidden_next,
        grad_next,
        place_next,
        gain_next.reshape(1, width),
        ids,
        weights,
        dc_back,
        ggu,
        gd,
    )
    return (
        handed[None],
        grad_gate_up[None, None],
        grad_down[None, None],
        combine.T[None],
    )


def solution(mesh):
    return jax.shard_map(
        on_device,
        mesh=mesh,
        in_specs=(
            P("pipe", "expert", None),
            P("pipe", "expert", None),
            P("pipe", "expert", None),
            P("pipe", "expert", None),
            P("pipe", None),
            P("pipe", "expert", None, None, None),
            P("pipe", "expert", None, None),
        ),
        out_specs=(
            P("pipe", "expert", None),
            P("pipe", "expert", None, None, None),
            P("pipe", "expert", None, None),
            P("pipe", "expert", None),
        ),
        check_vma=False,
    )
```

```python
import jax
import jax.numpy as jnp
from jax import lax
from jax.experimental import pallas as pl
from jax.experimental.pallas import tpu as pltpu
from jax.sharding import PartitionSpec as P

CAP = 8
NY = 4
NZ = 8
LINE = 4
MESH = pl.DeviceIdType.MESH
F32 = jnp.float32
BF16 = jnp.bfloat16


def nt(left, right):
    return lax.dot_general(left, right, (((1,), (1,)), ((), ())), preferred_element_type=F32)


def nn(left, right):
    return lax.dot_general(left, right, (((1,), (0,)), ((), ())), preferred_element_type=F32)


def tn(left, right):
    return lax.dot_general(left, right, (((0,), (0,)), ((), ())), preferred_element_type=F32)


def placing(ids, weights):
    count = ids.shape[1]
    span = NY * 2
    hits = [ids == e for e in range(span)]
    member = jnp.concatenate(
        [jnp.max(jnp.where(hit, 1.0, 0.0), axis=0, keepdims=True) for hit in hits], axis=0
    )
    above = lax.broadcasted_iota(jnp.int32, (count, count), 0) < lax.broadcasted_iota(
        jnp.int32, (count, count), 1
    )
    position = nn(member.astype(BF16), jnp.where(above, 1.0, 0.0).astype(BF16))
    row = lax.broadcasted_iota(jnp.int32, (CAP, count), 0).astype(F32)
    plain = []
    weighted = []
    for e in range(span):
        here = (row == position[e : e + 1]) & (member[e : e + 1] > 0.5)
        place = jnp.where(here, 1.0, 0.0)
        share = jnp.sum(jnp.where(hits[e], weights, 0.0), axis=0, keepdims=True)
        plain.append(place)
        weighted.append(place * share)
    return plain, weighted


def expert_kernel(
    ids_ref,
    weight_ref,
    gain_row,
    wgu_hbm,
    wd_hbm,
    hidden_ref,
    grad_ref,
    gain_ref,
    back_ref,
    dc_ref,
    ggu_hbm,
    gd_hbm,
    hidden_next,
    grad_next,
    gain_next,
    place_next,
    mine_ref,
    give,
    place_ref,
    tokens,
    token_grad,
    rows,
    wgu,
    wd,
    part,
    swap,
    chain,
    summed,
    final,
    acc,
    da,
    db,
    hd,
    ggu,
    gd,
    row_sem,
    pair_sem,
    right_sem,
    left_sem,
    share_sem,
    entry_sem,
    swap_send,
    swap_recv,
    chain_send,
    chain_recv,
    final_send,
    back_recv,
    dc_send,
    dc_recv,
    w_sem,
    out_sem,
    early_send,
    early_recv,
    pack_sem,
    give_send,
    give_recv,
):
    me = lax.axis_index("expert")
    stage = lax.axis_index("pipe")
    stages = lax.axis_size("pipe")
    before = lax.rem(stage + stages - 1, stages)
    after = lax.rem(stage + 1, stages)
    core = lax.rem(me, 2)
    z = lax.rem(me // 2, NZ)
    y = me // (2 * NZ)
    half = z // LINE
    pos = lax.rem(z, LINE)
    expert = y * 2 + half
    width = mine_ref.shape[2]
    halfw = width // 2
    outw = halfw + 128
    slots = NY * NZ
    last = LINE - 1
    at_end = (pos == 0) | (pos == last)

    def at(yy, zz, cc):
        return (yy * NZ + zz) * 2 + cc

    partner = at(y, z, 1 - core)
    right = at(y, lax.rem(z + 1, NZ), core)
    left = at(y, lax.rem(z + NZ - 1, NZ), core)
    entry_z = jnp.where(pos >= 2, lax.rem(LINE * (half + 1), NZ), lax.rem(LINE * half + NZ - 1, NZ))

    loads = [
        pltpu.make_async_copy(hidden_ref, tokens, pack_sem.at[0]),
        pltpu.make_async_copy(grad_ref, token_grad, pack_sem.at[1]),
    ]
    for copy in loads:
        copy.start()

    barrier = pltpu.get_barrier_semaphore()

    def greet(pipe, other):
        pl.semaphore_signal(
            barrier, inc=1, device_id={"pipe": pipe, "expert": other}, device_id_type=MESH
        )

    greet(stage, partner)
    for step in range(1, NY):
        greet(stage, at(lax.rem(y + step, NY), z, core))

    @pl.when(pos > 0)
    def _():
        greet(stage, left)

    @pl.when(pos < last)
    def _():
        greet(stage, right)

    @pl.when(at_end)
    def _():
        way = jnp.where(pos == 0, NZ - 1, 1)
        for hop in (1, 2):
            for yy in range(NY):
                greet(stage, at(yy, lax.rem(z + hop * way, NZ), core))

    for cc in range(2):
        for yy in range(NY):
            greet(after, at(yy, z, cc))
            greet(after, at(yy, entry_z, cc))
    for yy in range(NY):
        greet(stage, at(yy, entry_z, 0))

        @pl.when((yy != y) | (core != 0))
        def _():
            greet(stage, at(yy, z, 0))

    w_copies = [
        pltpu.make_async_copy(wgu_hbm, wgu, w_sem.at[0]),
        pltpu.make_async_copy(wd_hbm, wd, w_sem.at[1]),
    ]
    for copy in w_copies:
        copy.start()

    plain, weighted = placing(ids_ref[...], weight_ref[...].astype(F32))
    place = jnp.concatenate(plain, axis=0).astype(BF16)
    place_w = jnp.concatenate(weighted, axis=0).astype(BF16)
    place_ref[...] = place
    for copy in loads:
        copy.wait()
    count = tokens.shape[0]
    square = jnp.zeros((count, 128), F32)
    for n in range(width // 128):
        h = tokens[:, n * 128 : (n + 1) * 128].astype(F32)
        square = square + h * h
    scale = 1.0 / jnp.sqrt(jnp.sum(square, axis=1, keepdims=True) / width + 1e-06)
    for n in range(width // 512):
        cols = slice(n * 512, (n + 1) * 512)
        u = ((tokens[:, cols].astype(F32) * scale) * gain_row[:, cols]).astype(BF16)
        sent_in = nn(place, u).astype(BF16).reshape(NY * 2, CAP, 512)
        sent_grad = nn(place_w, token_grad[:, cols]).astype(BF16).reshape(NY * 2, CAP, 512)

        @pl.when(core == 0)
        def _():
            mine_ref[:, :CAP, cols] = sent_in
            give[:, :, cols] = sent_grad

        @pl.when(core == 1)
        def _():
            mine_ref[:, CAP:, cols] = sent_grad
            give[:, :, cols] = sent_in

    common = 1 + (NY - 1) + NY + 2 * NY + jnp.where(core == 0, 2 * NY - 1, 0)
    ends = 1 + 4 * NY + jnp.where(core == 0, 4 * NY, 0)
    pl.semaphore_wait(barrier, common + jnp.where(at_end, ends, 2))

    def remote(src, dst, send, recv, other, pipe=None):
        return pltpu.make_async_remote_copy(
            src_ref=src,
            dst_ref=dst,
            send_sem=send,
            recv_sem=recv,
            device_id={"pipe": stage if pipe is None else pipe, "expert": other},
            device_id_type=MESH,
        )

    def give_copy(e, place_of):
        return remote(
            give.at[e],
            mine_ref.at[e, pl.ds(place_of * CAP, CAP)],
            give_send.at[e],
            give_recv.at[e],
            partner,
        )

    for step in range(NY):
        yy = lax.rem(y + step, NY)
        for e in (yy * 2 + half, yy * 2 + 1 - half):

            @pl.when(core == 0)
            def _():
                give_copy(e, 0).start()

            @pl.when(core == 1)
            def _():
                give_copy(e, 1).start()

    slot = z * NY + y

    def entry(src_idx, sem_idx, other):
        return remote(
            mine_ref.at[src_idx], rows.at[core, slot], entry_sem.at[sem_idx], row_sem.at[slot], other
        )

    own_copy = pltpu.make_async_copy(mine_ref.at[expert], rows.at[core, slot], row_sem.at[slot])

    def entry_far(step):
        yy = lax.rem(y + step, NY)
        return entry(yy * 2 + 1 - half, NY + step, at(yy, entry_z, core))

    for step in range(NY):
        yy = lax.rem(y + step, NY)
        give_copy(yy * 2 + half, 0).wait()
        if step > 0:
            entry(yy * 2 + half, step, at(yy, z, core)).start()
        else:
            own_copy.start()
        give_copy(yy * 2 + 1 - half, 0).wait()

        @pl.when(jnp.logical_not(at_end))
        def _():
            entry_far(step).start()

    early = [
        remote(src, dst, early_send.at[i], early_recv.at[i], me, before)
        for i, (src, dst) in enumerate(
            (
                (hidden_ref, hidden_next),
                (grad_ref, grad_next),
                (gain_ref, gain_next),
                (place_ref, place_next),
            )
        )
    ]
    for copy in early:
        copy.start()

    def piece(idx):
        return rows.at[core, idx]

    def forward(idx, sems, other):
        return remote(piece(idx), piece(idx), sems.at[idx], row_sem.at[idx], other)

    def share(idx):
        return remote(piece(idx), piece(idx), share_sem.at[idx], pair_sem.at[idx], partner)

    def arrived(idx):
        pltpu.make_async_copy(mine_ref.at[0], piece(idx), row_sem.at[idx]).wait()

    def z_of(offset):
        return lax.rem(z + offset + NZ, NZ)

    my_half = pl.multiple_of(core * outw, 128)
    their_half = pl.multiple_of((1 - core) * outw, 128)
    block = NY * 16

    def swap_copy(src_z):
        span = pl.ds(src_z * NY, NY)
        return remote(
            part.at[span, :, pl.ds(their_half, outw)],
            swap.at[span],
            swap_send.at[src_z],
            swap_recv.at[src_z],
            partner,
        )

    def compute(src_z):
        @pl.loop(0, NY)
        def _(j):
            idx = src_z * NY + j
            pltpu.make_async_copy(
                mine_ref.at[0], rows.at[1 - core, idx], pair_sem.at[idx]
            ).wait()

        span = pl.ds(src_z * NY, NY)
        u = rows[0, span].reshape(block, width)
        dy = rows[1, span].reshape(block, width)
        a = nt(u, wgu[0])
        b = nt(u, wgu[1])
        g = nt(dy, wd[...])
        sig = jax.nn.sigmoid(a)
        act = a * sig
        hdn = act * b
        dga = (g * b * sig * (1.0 + a * (1.0 - sig))).astype(BF16)
        dgb = (g * act).astype(BF16)
        where = pl.ds(pl.multiple_of(src_z * block, block), block)
        da[where] = dga
        db[where] = dgb
        hd[where] = hdn.astype(BF16)
        dc = jnp.sum(hdn * g, axis=1, keepdims=True)
        dc = jnp.broadcast_to(dc.astype(BF16), (block, 128)).reshape(NY, 16, 128)
        part[span, :, :128] = dc
        part[span, :, width + 128 :] = dc
        tile = 512
        for turn in range(2):
            low = (1 - core if turn == 0 else core) * halfw
            for n in range(halfw // tile):
                cols = pl.ds(pl.multiple_of(low + n * tile, tile), tile)
                du = nn(dga, wgu[0, :, cols]) + nn(dgb, wgu[1, :, cols])
                part[span, :, pl.ds(pl.multiple_of(128 + low + n * tile, 128), tile)] = (
                    du.astype(BF16).reshape(NY, 16, tile)
                )
            if turn == 0:
                swap_copy(src_z).start()

    def chain_in(idx):
        pltpu.make_async_copy(summed.at[0], chain.at[idx], chain_recv.at[idx]).wait()
        acc[...] += chain[idx].astype(F32)

    def chain_out(idx, dst, other):
        return remote(summed.at[idx], chain.at[dst], chain_send.at[idx], chain_recv.at[dst], other)

    def final_out(number, cc, src_y, src_z):
        return remote(
            final.at[number, pl.ds(cc * CAP, CAP)],
            back_ref.at[expert, :, pl.ds(my_half, outw)],
            final_send.at[2 * number + cc],
            back_recv.at[2 * expert + core],
            at(src_y, src_z, cc),
            before,
        )

    def dc_out(number, cc, src_y, src_z):
        return remote(
            final.at[number, pl.ds(cc * CAP, CAP), pl.ds(0, 128)],
            dc_ref.at[expert],
            dc_send.at[2 * number + cc],
            dc_recv.at[expert],
            at(src_y, src_z, cc),
        )

    def dc_own(number):
        return pltpu.make_async_copy(
            final.at[number, pl.ds(0, CAP), pl.ds(0, 128)], dc_ref.at[expert], dc_recv.at[expert]
        )

    def finish(number, src_y, src_z):
        final[number] = acc[...].astype(BF16)
        for cc in range(2):
            final_out(number, cc, src_y, src_z).start()

        @pl.when(core == 0)
        def _():
            dc_out(number, 1, src_y, src_z).start()

            @pl.when((src_y == y) & (src_z == z))
            def _():
                dc_own(number).start()

            @pl.when((src_y != y) | (src_z != z))
            def _():
                dc_out(number, 0, src_y, src_z).start()

    def combine(src_z, hop, kind):
        swap_copy(src_z).wait_recv()

        @pl.loop(0, NY)
        def _(j):
            idx = src_z * NY + j
            acc[...] = part[idx, :, pl.ds(my_half, outw)].astype(F32) + swap[idx].astype(F32)
            if kind == 0:

                @pl.when(pos < last)
                def _():
                    chain_in(idx)

                @pl.when(pos > 0)
                def _():
                    chain_in(slots + j)

                finish(j, j, src_z)
            elif kind < 0:

                @pl.when(pos < last)
                def _():
                    chain_in(idx)

                @pl.when(pos > 0)
                def _():
                    summed[idx] = acc[...].astype(BF16)
                    chain_out(idx, idx, left).start()

                @pl.when(pos == 0)
                def _():
                    finish(hop * NY + j, j, src_z)
            else:

                @pl.when(pos > 0)
                def _():
                    chain_in(idx)

                @pl.when(pos < last)
                def _():
                    summed[idx] = acc[...].astype(BF16)
                    chain_out(idx, jnp.where(hop == 1, slots + j, idx), right).start()

                @pl.when(pos == last)
                def _():
                    finish(hop * NY + j, j, src_z)

    def pick(values, index, default=0):
        out = default
        for i, value in enumerate(values):
            out = jnp.where(index == i, value, out)
        return out

    def list_at(place, slot):
        code = pick((0o12, 0o231, 0o3421, 0o145320), place)
        return lax.rem(code // pick((1, 8, 64, 512, 4096, 32768), slot, 8**6), 8)

    def origin(slot):
        return pick((9, 1, 0, -2, -1, 2), slot)

    flip = last - pos

    def own_idx(j):
        return z * NY + lax.rem(y + NY - j, NY)

    @pl.loop(0, 15)
    def _(it):
        slot_now = it // 2
        part_now = lax.rem(it, 2)
        from_l = list_at(pos, slot_now)
        from_r = list_at(flip, slot_now)

        for jj in range(2):
            j = 2 * part_now + jj
            src_y = lax.rem(y + NY - j, NY)

            @pl.when(slot_now == 0)
            def _():
                idx = own_idx(j)
                arrived(idx)

                @pl.when(pos <= 1)
                def _():
                    forward(idx, right_sem, right).start()

                @pl.when(pos >= 2)
                def _():
                    forward(idx, left_sem, left).start()

                share(idx).start()

            @pl.when(from_l > 0)
            def _():
                idx = z_of(-from_l) * NY + src_y
                arrived(idx)

                @pl.when(pos < last)
                def _():
                    forward(idx, right_sem, right).start()

                share(idx).start()

            @pl.when(from_r > 0)
            def _():
                idx = z_of(from_r) * NY + src_y
                arrived(idx)

                @pl.when(pos > 0)
                def _():
                    forward(idx, left_sem, left).start()

                share(idx).start()

        @pl.when((it == 1) & at_end)
        def _():
            for step in range(NY):
                entry_far(step).start()

        first = jnp.where(it == 1, 0, 3)
        until = jnp.where(it == 1, 3, NY)

        @pl.when(((it == 1) | (it == 7)) & (pos == 2))
        def _():
            @pl.loop(first, until)
            def _(j):
                forward(own_idx(j), right_sem, right).start()

        @pl.when(((it == 1) | (it == 7)) & (pos == 1))
        def _():
            @pl.loop(first, until)
            def _(j):
                forward(own_idx(j), left_sem, left).start()

        @pl.when(it == 1)
        def _():
            for copy in w_copies:
                copy.wait()

        gone_l = list_at(pos, slot_now - 1)
        gone_r = list_at(flip, slot_now - 1)
        late = slot_now >= 4
        away = jnp.where(
            part_now == 0,
            jnp.where(late & (gone_r > 0), gone_r, -gone_l),
            jnp.where(late, 0, gone_r),
        )

        @pl.when((it == 1) | ((it >= 2) & (away != 0)))
        def _():
            compute(z_of(jnp.where(it == 1, 0, away)))

        since_l = it - 3 - flip
        slot_l = since_l // 2
        away_l = pos - origin(slot_l)

        @pl.when((since_l >= 2) & (lax.rem(since_l + 2, 2) == 0) & (slot_l <= 5) & (away_l >= 1))
        def _():
            combine(z_of(-away_l), away_l, -1)

        since_r = it - 3 - pos
        slot_r = (since_r + 16) // 2 - 8
        away_r = flip - origin(slot_r)
        odd_r = lax.rem(since_r + 16, 2)

        @pl.when(
            (slot_r >= jnp.where(odd_r == 1, 1, 3))
            & (slot_r <= jnp.where(odd_r == 1, 2, 5))
            & (away_r >= 1)
        )
        def _():
            combine(z_of(away_r), away_r, 1)

        @pl.when(it == pick((10, 14, 14, 11), pos))
        def _():
            combine(z, 0, 0)

        @pl.loop(0, 6)
        def _(s):
            few = jnp.where(s < 2, jnp.where(at_end, s - 100 * (13 - it), 2 * (it - 9) + s), -1)
            n = jnp.where(at_end & (it == 14), 2 + s, few)
            tile = 512

            @pl.when((n >= 0) & (n < width // tile))
            def _():
                cols = pl.ds(pl.multiple_of(n * tile, tile), tile)
                u = rows[0, :, :, cols].reshape(-1, tile)
                dy = rows[1, :, :, cols].reshape(-1, tile)
                ggu[0, :, cols] = tn(da[...], u).astype(BF16)
                ggu[1, :, cols] = tn(db[...], u).astype(BF16)
                gd[:, cols] = tn(hd[...], dy).astype(BF16)

    out_copies = [
        pltpu.make_async_copy(ggu, ggu_hbm, out_sem.at[0]),
        pltpu.make_async_copy(gd, gd_hbm, out_sem.at[1]),
    ]
    for copy in out_copies:
        copy.start()

    for step in range(NY):
        if step > 0:
            entry(expert, step, partner).wait_send()
        entry(expert, NY + step, partner).wait_send()
    for copy in early:
        copy.wait()

    @pl.loop(0, 6)
    def _(hop):
        from_left = z_of(-hop)
        from_right = z_of(hop)

        @pl.loop(0, NY)
        def _(j):
            @pl.when((hop <= pos + 2) & (pos < last))
            def _():
                forward(from_left * NY + j, right_sem, right).wait_send()

            @pl.when((hop <= 5 - pos) & (pos > 0))
            def _():
                forward(from_right * NY + j, left_sem, left).wait_send()

            @pl.when((hop >= 1) & (hop <= pos + 2) & (pos > 0))
            def _():
                idx = from_left * NY + j
                chain_out(idx, idx, left).wait_send()

            @pl.when((hop >= 1) & (hop <= 5 - pos) & (pos < last))
            def _():
                idx = from_right * NY + j
                chain_out(idx, idx, right).wait_send()

            @pl.when((hop == 0) | ((hop <= 2) & at_end))
            def _():
                for cc in range(2):
                    final_out(hop * NY + j, cc, j, z).wait_send()

                @pl.when(core == 0)
                def _():
                    dc_out(hop * NY + j, 1, j, z).wait_send()

                    @pl.when((hop > 0) | (j != y))
                    def _():
                        dc_out(hop * NY + j, 0, j, z).wait_send()

    @pl.loop(0, slots)
    def _(idx):
        share(idx).wait_send()

    @pl.loop(0, NZ)
    def _(src_z):
        swap_copy(src_z).wait_send()

    for e in range(NY * 2):
        for cc in range(2):
            pltpu.make_async_copy(
                final.at[0, pl.ds(0, CAP)],
                back_ref.at[e, :, pl.ds(cc * outw, outw)],
                back_recv.at[2 * e + cc],
            ).wait()
        pltpu.make_async_copy(
            final.at[0, pl.ds(0, CAP), pl.ds(0, 128)], dc_ref.at[e], dc_recv.at[e]
        ).wait()
    for copy in out_copies:
        copy.wait()


def experts(ids, weights, gain_row, wgu, wd, hidden, grad, gain):
    width = hidden.shape[1]
    count = hidden.shape[0]
    units = wd.shape[0]
    outw = width // 2 + 128
    slots = NY * NZ
    dma = pltpu.SemaphoreType.DMA
    hbm = pl.BlockSpec(memory_space=pl.ANY)
    vmem = pl.BlockSpec(memory_space=pltpu.VMEM)
    like = lambda array: jax.ShapeDtypeStruct(array.shape, array.dtype)
    return pl.pallas_call(
        expert_kernel,
        out_shape=(
            jax.ShapeDtypeStruct((NY * 2, CAP, 2 * outw), BF16),
            jax.ShapeDtypeStruct((NY * 2, CAP, 128), BF16),
            like(wgu),
            like(wd),
            like(hidden),
            like(grad),
            like(gain),
            jax.ShapeDtypeStruct((NY * 2 * CAP, count), BF16),
        ),
        in_specs=[vmem] * 3 + [hbm] * 5,
        out_specs=[vmem, vmem] + [hbm] * 6,
        scratch_shapes=[
            pltpu.VMEM((NY * 2, 16, width), BF16),
            pltpu.VMEM((NY * 2, CAP, width), BF16),
            pltpu.VMEM((NY * 2 * CAP, count), BF16),
            pltpu.VMEM(hidden.shape, BF16),
            pltpu.VMEM(grad.shape, BF16),
            pltpu.VMEM((2, slots, 16, width), BF16),
            pltpu.VMEM(wgu.shape, BF16),
            pltpu.VMEM(wd.shape, BF16),
            pltpu.VMEM((slots, 16, 2 * outw), BF16),
            pltpu.VMEM((slots, 16, outw), BF16),
            pltpu.VMEM((slots + NY, 16, outw), BF16),
            pltpu.VMEM((slots, 16, outw), BF16),
            pltpu.VMEM((3 * NY, 16, outw), BF16),
            pltpu.VMEM((16, outw), F32),
            pltpu.VMEM((slots * 16, units), BF16),
            pltpu.VMEM((slots * 16, units), BF16),
            pltpu.VMEM((slots * 16, units), BF16),
            pltpu.VMEM(wgu.shape, BF16),
            pltpu.VMEM(wd.shape, BF16),
            dma((slots,)),
            dma((slots,)),
            dma((slots,)),
            dma((slots,)),
            dma((slots,)),
            dma((2 * NY,)),
            dma((NZ,)),
            dma((NZ,)),
            dma((slots,)),
            dma((slots + NY,)),
            dma((6 * NY,)),
            dma((4 * NY,)),
            dma((6 * NY,)),
            dma((2 * NY,)),
            dma((2,)),
            dma((2,)),
            dma((4,)),
            dma((4,)),
            dma((2,)),
            dma((2 * NY,)),
            dma((2 * NY,)),
        ],
        compiler_params=pltpu.CompilerParams(
            collective_id=0, has_side_effects=True, vmem_limit_bytes=60 * 1024 * 1024
        ),
    )(ids, weights, gain_row, wgu, wd, hidden, grad, gain)


def finish_kernel(
    back_hbm,
    hidden_hbm,
    grad_hbm,
    place_ref,
    gain_ref,
    ids_ref,
    weight_ref,
    dc_ref,
    ggu_hbm,
    gd_hbm,
    handed_hbm,
    ggu_out,
    gd_out,
    combine_ref,
    back,
    hidden,
    grad,
    handed,
    ggu,
    gd,
    scaled,
    in_sem,
    out_sem,
):
    width = hidden.shape[1]
    count = hidden.shape[0]
    ins = [
        pltpu.make_async_copy(src, dst, in_sem.at[i])
        for i, (src, dst) in enumerate(
            (
                (hidden_hbm, hidden),
                (back_hbm, back),
                (grad_hbm, grad),
                (ggu_hbm, ggu),
                (gd_hbm, gd),
            )
        )
    ]
    for copy in ins:
        copy.start()
    ids = ids_ref[...]
    weights = weight_ref[...].astype(F32)
    plain, _ = placing(ids, weights)
    total = jnp.zeros(ids.shape, F32)
    for e in range(NY * 2):
        dc = jnp.sum(plain[e] * dc_ref[e].astype(F32), axis=0, keepdims=True)
        total = total + jnp.where(ids == e, dc, 0.0)
    combine_ref[...] = total / weights
    ins[0].wait()
    tile = 512
    square = jnp.zeros((count, 128), F32)
    for n in range(width // 128):
        h = hidden[:, n * 128 : (n + 1) * 128].astype(F32)
        square = square + h * h
    scale = 1.0 / jnp.sqrt(jnp.sum(square, axis=1, keepdims=True) / width + 1e-06)
    for i in (3, 4):
        ins[i].wait()
    grads = [
        pltpu.make_async_copy(ggu, ggu_out, out_sem.at[0]),
        pltpu.make_async_copy(gd, gd_out, out_sem.at[1]),
    ]
    for copy in grads:
        copy.start()
    ins[1].wait()
    place = place_ref[...]
    along = jnp.zeros((count, 1), F32)
    for n in range(width // tile):
        cols = slice(n * tile, (n + 1) * tile)
        rows = back[:, :, 128 + n * tile : 128 + (n + 1) * tile].reshape(-1, tile)
        part = tn(place, rows) * gain_ref[:, cols]
        scaled[:, cols] = part
        along = along + jnp.sum(part * hidden[:, cols].astype(F32), axis=1, keepdims=True)
    inner = along * scale / width
    ins[2].wait()
    halves = []
    for n in range(width // tile):
        cols = slice(n * tile, (n + 1) * tile)
        normed = hidden[:, cols].astype(F32) * scale
        handed[:, cols] = (
            grad[:, cols].astype(F32) + (scaled[:, cols] - normed * inner) * scale
        ).astype(BF16)
        if n in (width // tile // 2 - 1, width // tile - 1):
            span = pl.ds(len(halves) * (width // 2), width // 2)
            halves.append(
                pltpu.make_async_copy(
                    handed.at[:, span], handed_hbm.at[:, span], out_sem.at[2 + len(halves)]
                )
            )
            halves[-1].start()
    for copy in grads + halves:
        copy.wait()


def finish(back, hidden, grad, place, gain, ids, weights, dc, ggu, gd):
    like = lambda array: jax.ShapeDtypeStruct(array.shape, array.dtype)
    hbm = pl.BlockSpec(memory_space=pl.ANY)
    vmem = pl.BlockSpec(memory_space=pltpu.VMEM)
    room = lambda array: pltpu.VMEM(array.shape, array.dtype)
    return pl.pallas_call(
        finish_kernel,
        out_shape=(like(hidden), like(ggu), like(gd), jax.ShapeDtypeStruct(ids.shape, F32)),
        in_specs=[hbm, hbm, hbm, vmem, vmem, vmem, vmem, vmem, hbm, hbm],
        out_specs=[hbm, hbm, hbm, vmem],
        scratch_shapes=[
            room(back),
            room(hidden),
            room(grad),
            room(hidden),
            room(ggu),
            room(gd),
            pltpu.VMEM(hidden.shape, F32),
            pltpu.SemaphoreType.DMA((5,)),
            pltpu.SemaphoreType.DMA((4,)),
        ],
        compiler_params=pltpu.CompilerParams(vmem_limit_bytes=63 * 1024 * 1024),
    )(back, hidden, grad, place, gain, ids, weights, dc, ggu, gd)


def on_device(hidden_in, out_grad, expert_ids, route_weight, norm_gain, w_gate_up, w_down):
    width = hidden_in.shape[2]
    ids = expert_ids[0].T
    weights = route_weight[0].T
    back, dc_back, ggu, gd, hidden_next, grad_next, gain_next, place_next = experts(
        ids,
        weights,
        norm_gain,
        w_gate_up[0, 0],
        w_down[0, 0],
        hidden_in[0],
        out_grad[0],
        norm_gain.reshape(-1, 128),
    )
    handed, grad_gate_up, grad_down, combine = finish(
        back,
        hidden_next,
        grad_next,
        place_next,
        gain_next.reshape(1, width),
        ids,
        weights,
        dc_back,
        ggu,
        gd,
    )
    return (
        handed[None],
        grad_gate_up[None, None],
        grad_down[None, None],
        combine.T[None],
    )


def solution(mesh):
    return jax.shard_map(
        on_device,
        mesh=mesh,
        in_specs=(
            P("pipe", "expert", None),
            P("pipe", "expert", None),
            P("pipe", "expert", None),
            P("pipe", "expert", None),
            P("pipe", None),
            P("pipe", "expert", None, None, None),
            P("pipe", "expert", None, None),
        ),
        out_specs=(
            P("pipe", "expert", None),
            P("pipe", "expert", None, None, None),
            P("pipe", "expert", None, None),
            P("pipe", "expert", None),
        ),
        check_vma=False,
    )
```
